32 devices in a mesh: gx: 2 (over core), gy: 4 (over z), gz: 4 (over y, x).
Axes of the slice: x: 2, y: 2, z: 4, core: 2. Of those that a mesh axis runs over, the one named last changes fastest.
Arguments:
- particles: float32 [28, 65536], P(None, ('gx', 'gy', 'gz')), may hold values from -3 to 3, as said below
- stencil_base: int32 [3, 65536], P(None, ('gx', 'gy', 'gz')), may hold values from 0 to 32, as said below
- weights: float32 [8, 65536], P(None, ('gx', 'gy', 'gz')), may hold values from 0.02 to 0.25
- gradients: float32 [3, 8, 65536], P(None, None, ('gx', 'gy', 'gz')), may hold values from -4 to 4
- counts: int32 [32], P(('gx', 'gy', 'gz')), may hold values from 0 to 8, as said below
Outputs:
- migrated: float32 [28, 98304], P(None, ('gx', 'gy', 'gz'))
- damage: float32 [16, 64, 128], P('gx', 'gy', 'gz')
The draws below stay inside these ranges and needn't reach their ends.
Inputs may be any that keep to these rules, and one draw needn't show every extreme that they name: `particles`: mass and volume in 0.5 to 2, deformation gradient entries within 0.1 of the identity's, damage in 0 to 0.5, history in 0.05 to 1. `stencil_base`: row 0 lies in 0 to 8, row 1 in 0 to 16, row 2 in 0 to 32. `counts`: some device hands exactly 8 bins.
All inputs are finite; a program needn't handle non-finite values.
Results may differ from the reference program's by a relative error of at most 0.0003.
Values sent between devices are 32-bit elements; how exact they have to be, the bound alone decides.
A program may use at most 64 MiB of HBM per device.

```python
import math
import jax
import jax.numpy as jnp
from jax import lax

CX = 8
CY = 16
CZ = 32
NBIN = 16
BIN = 128
SUBSTEPS = 4
FIELDS = 28
MOST = 8
RANKS = 32
PARTICLES = 65536
NX = 16
NY = 64
NZ = 128
N_GX = 2
N_GY = 4
N_GZ = 4


def draw_particles(key, part):
    keys = jax.random.split(key, 7)
    count = PARTICLES
    scales = jnp.exp(jax.random.uniform(keys[0], (2, count), jnp.float32, math.log(0.5), math.log(2.0)))
    velocity = jnp.clip(0.5 * jax.random.normal(keys[1], (3, count), jnp.float32), -2.0, 2.0)
    stress = jnp.clip(0.5 * jax.random.normal(keys[3], (9, count), jnp.float32), -3.0, 3.0)
    deform = jnp.eye(3, dtype=jnp.float32).reshape(9, 1) + jax.random.uniform(keys[2], (9, count), jnp.float32, -0.1, 0.1)
    damage = jax.random.uniform(keys[4], (1, count), jnp.float32, 0.0, 0.5)
    history = jnp.exp(jax.random.uniform(keys[5], (1, count), jnp.float32, math.log(0.05), 0.0))
    position = jax.random.uniform(keys[6], (3, count), jnp.float32, 0.0, 1.0)
    return jnp.concatenate([scales, velocity, deform, stress, damage, history, position], axis=0)


def draw_stencil_base(key, part):
    keys = jax.random.split(key, 3)
    row_x = jax.random.randint(keys[0], (PARTICLES,), 0, CX + 1)
    row_y = jax.random.randint(keys[1], (PARTICLES,), 0, CY + 1)
    row_z = jax.random.randint(keys[2], (PARTICLES,), 0, CZ + 1)
    return jnp.stack([row_x, row_y, row_z]).astype(jnp.int32)


def draw_counts(key, part):
    values = jax.random.randint(key, (RANKS,), 0, MOST + 1)
    chosen = jax.random.randint(jax.random.fold_in(key, 7), (), 0, RANKS)
    return values.at[chosen].set(MOST).astype(jnp.int32)


def level_of(key, shape, cuts, low, top_value):
    def one(axis_at, shards_of):
        draws = jax.random.uniform(jax.random.fold_in(jax.random.fold_in(key, 6), axis_at), (shards_of,), jnp.float32, low / len(cuts), top_value / len(cuts))
        return jnp.repeat(jnp.exp(draws), shape[axis_at] // shards_of).reshape((-1,) + (1,) * (len(shape) - axis_at - 1))

    level = one(*cuts[0])
    for cut in cuts[1:]:
        level = level * one(*cut)
    return level


def noise(key, dims, scale, most, shards=(), kind=jnp.bfloat16):
    result = scale * jax.random.normal(key, dims, jnp.float32)
    if shards:
        result = result * level_of(key, dims, shards, -0.22, 0.18)
    return jnp.clip(result, -most, most).astype(kind)


def setup_inputs(seed: int = 0) -> dict:
    splits = jax.random.split(jax.random.key(seed), 6)
    particles = draw_particles(jax.random.fold_in(splits[5], 71), 0)
    stencil_base = draw_stencil_base(jax.random.fold_in(splits[5], 71), 0)
    weights = jnp.clip(0.02 + 0.23 * jax.random.uniform(splits[2], (8, PARTICLES), jnp.float32) ** level_of(splits[2], (8, PARTICLES), ((1, 32),), -0.2, 0.2), 0.02, 0.25)
    gradients = noise(splits[3], (3, 8, PARTICLES), 1.0, 4.0, ((2, 32),), jnp.float32)
    counts = draw_counts(jax.random.fold_in(splits[5], 71), 0)
    return {"particles": particles, "stencil_base": stencil_base, "weights": weights, "gradients": gradients, "counts": counts}


time_step = 0.1
relax_rate = 0.2
length_sq = 0.6
shear_mod = 1.0
bulk_coef = 1.5
mass_floor = 0.5


def corner_offsets(corner):
    return (corner >> 2) & 1, (corner >> 1) & 1, corner & 1


def node_terms(particles, weights, gradients, corner):
    volume = particles[1]
    velocity = particles[2:5]
    stress = particles[14:23].reshape(3, 3, -1)
    share = particles[0] * weights[corner]
    slope = gradients[:, corner]
    force = -volume[None] * jnp.sum(stress * slope[None], axis=1)
    return jnp.concatenate([share[None], share[None] * velocity, force, (share * particles[23])[None], (share * particles[24])[None]], axis=0)


def relax(padded, drive):
    centre = padded[1:-1, 1:-1, 1:-1]
    laplace = (padded[2:, 1:-1, 1:-1] + padded[:-2, 1:-1, 1:-1] + padded[1:-1, 2:, 1:-1] + padded[1:-1, :-2, 1:-1] + padded[1:-1, 1:-1, 2:] + padded[1:-1, 1:-1, :-2]) - 6.0 * centre
    return centre + relax_rate * (length_sq * laplace - centre + 2.0 * (1.0 - centre) * drive)


def advance(particles, near_velocity, near_damage, weights, gradients):
    moved = [jnp.sum(weights * near_velocity[i], axis=0) for i in range(3)]
    velgrad = [[jnp.sum(near_velocity[i] * gradients[j], axis=0) for j in range(3)] for i in range(3)]
    damage_node = jnp.sum(weights * near_damage, axis=0)
    deform = [[particles[5 + 3 * i + j] for j in range(3)] for i in range(3)]
    stretch = [[(1.0 if i == j else 0.0) + time_step * velgrad[i][j] for j in range(3)] for i in range(3)]
    mapped = [[stretch[i][0] * deform[0][j] + stretch[i][1] * deform[1][j] + stretch[i][2] * deform[2][j] for j in range(3)] for i in range(3)]
    jacobian = (mapped[0][0] * (mapped[1][1] * mapped[2][2] - mapped[1][2] * mapped[2][1])
                - mapped[0][1] * (mapped[1][0] * mapped[2][2] - mapped[1][2] * mapped[2][0])
                + mapped[0][2] * (mapped[1][0] * mapped[2][1] - mapped[1][1] * mapped[2][0]))
    left = [[mapped[i][0] * mapped[j][0] + mapped[i][1] * mapped[j][1] + mapped[i][2] * mapped[j][2] for j in range(3)] for i in range(3)]
    damaged = jnp.maximum(particles[23], damage_node)
    degrade = (1.0 - damaged) ** 2
    rows_out = []
    for i in range(3):
        for j in range(3):
            term = shear_mod * (left[i][j] - (1.0 if i == j else 0.0))
            if i == j:
                term = term + bulk_coef * (jacobian - 1.0)
            rows_out.append(degrade * term)
    energy = 0.5 * shear_mod * (left[0][0] + left[1][1] + left[2][2] - 3.0) + 0.5 * bulk_coef * (jacobian - 1.0) ** 2
    history = jnp.maximum(particles[24], energy)
    position = particles[25:28] + time_step * jnp.stack(moved)
    flat_mapped = jnp.stack([mapped[i][j] for i in range(3) for j in range(3)])
    return jnp.concatenate([particles[0:2], jnp.stack(moved), flat_mapped, jnp.stack(rows_out), damaged[None], history[None], position], axis=0)


def assemble(own, tail, own_count, prior):
    buffer_all = jnp.concatenate([tail, own, jnp.zeros((own.shape[0], MOST * BIN), own.dtype)], axis=1)
    start = ((MOST - prior) * BIN).astype(jnp.int32)
    window = lax.dynamic_slice_in_dim(buffer_all, start, (NBIN + MOST) * BIN, 1)
    live = (NBIN - own_count + prior) * BIN
    slot = jnp.arange((NBIN + MOST) * BIN, dtype=jnp.int32)
    return jnp.where(slot[None, :] < live, window, jnp.zeros_like(window))


def reference(particles, stencil_base, weights, gradients, counts):
    per_device = NBIN * BIN
    span_y = NY + 2
    span_z = NZ + 2
    base = stencil_base.reshape(3, N_GX, N_GY, N_GZ, per_device)
    row_x = base[0] + (jnp.arange(N_GX, dtype=jnp.int32) * CX)[:, None, None, None]
    row_y = base[1] + (jnp.arange(N_GY, dtype=jnp.int32) * CY)[None, :, None, None]
    row_z = base[2] + (jnp.arange(N_GZ, dtype=jnp.int32) * CZ)[None, None, :, None]
    flats = []
    terms = []
    for corner in range(8):
        offset_x, offset_y, offset_z = corner_offsets(corner)
        flat_index = (((row_x + offset_x) * span_y + row_y + offset_y) * span_z + row_z + offset_z).reshape(-1).astype(jnp.int32)
        flats.append(flat_index)
        terms.append(node_terms(particles, weights, gradients, corner))
    all_index = jnp.concatenate(flats)
    grid_sum = jnp.zeros((9, (NX + 2) * span_y * span_z), jnp.float32).at[:, all_index].add(jnp.concatenate(terms, axis=1))
    owned = grid_sum.reshape(9, NX + 2, span_y, span_z)[:, 1:-1, 1:-1, 1:-1]
    masses = jnp.maximum(owned[0], mass_floor)
    velocity = (owned[1:4] + time_step * owned[4:7]) / masses[None]
    damage = owned[7] / masses
    drive = owned[8] / masses
    for step in range(SUBSTEPS):
        damage = relax(jnp.pad(damage, 1), drive)
    fields = jnp.pad(jnp.concatenate([velocity, damage[None]], axis=0), ((0, 0), (1, 1), (1, 1), (1, 1))).reshape(4, -1)
    near = fields[:, all_index].reshape(4, 8, PARTICLES)
    updated = advance(particles, near[0:3], near[3], weights, gradients)
    lines = N_GX * N_GY
    grouped = updated.reshape(FIELDS, lines, N_GZ, per_device)
    earlier = jnp.roll(grouped, 1, axis=2)
    tails = earlier[..., (NBIN - MOST) * BIN:]
    count_grid = counts.reshape(lines, N_GZ)
    prior = jnp.roll(count_grid, 1, axis=1)
    owns = jnp.transpose(grouped, (1, 2, 0, 3)).reshape(lines * N_GZ, FIELDS, per_device)
    tail_rows = jnp.transpose(tails, (1, 2, 0, 3)).reshape(lines * N_GZ, FIELDS, MOST * BIN)
    placed = jax.vmap(assemble)(owns, tail_rows, count_grid.reshape(-1), prior.reshape(-1))
    migrated = jnp.transpose(placed, (1, 0, 2)).reshape(FIELDS, -1)
    return migrated, damage
```

```python
import functools
import jax
import jax.numpy as jnp
from jax import lax
from jax.experimental import pallas as pl
from jax.experimental.pallas import tpu as pltpu
from jax.sharding import PartitionSpec as P

CX = 8
CY = 16
CZ = 32
NBIN = 16
BIN = 128
SUBSTEPS = 4
MOST = 8

time_step = 0.1
relax_rate = 0.2
length_sq = 0.6
shear_mod = 1.0
bulk_coef = 1.5
mass_floor = 0.5

MESH = pl.DeviceIdType.MESH


def up_to(value, unit):
    return (value + unit - 1) // unit * unit


H = SUBSTEPS + 1
SX, SY, SZ = CX + 2 * H, CY + 2 * H, CZ + 2 * H
LW = up_to(SY * SZ, 128)
NB = up_to(CY * SZ + CZ + 1, 128)
OFF = (H - 1) * SZ + H - 1
RD = up_to(SX, 8)
DS, VS = SX, CX + 2
DR, VR = up_to(3 * DS, 8), up_to(3 * VS, 16)
XA, XB = (H - 1) * SZ // 128 * 128, up_to((H + 1 + CY) * SZ, 128)
KEEP = H + 1
XROWS = 3 * KEEP + 6
YW = up_to(KEEP * SZ, 128)
YROWS = DR + VR // 2
DT, VT = DR // 8, VR // 8
SLOTS = SZ // KEEP
ZB = (DT + SLOTS - 1) // SLOTS
FOLDS = 3
FW = (CY + 2) // FOLDS * SZ
ZV = up_to(FW, 128)
ZW = ZB * LW + ZV
TAIL = MOST * BIN


def split(value):
    high = value.astype(jnp.bfloat16)
    low = (value - high.astype(jnp.float32)).astype(jnp.bfloat16)
    return high, low


def take(ref, lane0, width):
    a = lane0 // 128 * 128
    span = up_to(lane0 - a + width, 128)
    value = ref[:, a : a + span]
    shift = (span - (lane0 - a)) % span
    if shift:
        value = pltpu.roll(value, shift, 1)
    value = value[:, : up_to(width, 128)]
    lane = lax.broadcasted_iota(jnp.int32, value.shape, 1)
    return jnp.where(lane < width, value, 0.0)


def put_add(ref, lane0, width, value):
    a = lane0 // 128 * 128
    span = max(up_to(lane0 - a + width, 128), value.shape[1])
    extra = span - value.shape[1]
    if extra:
        value = jnp.concatenate([value, jnp.zeros((value.shape[0], extra), jnp.float32)], axis=1)
    if lane0 - a:
        value = pltpu.roll(value, lane0 - a, 1)
    ref[:, a : a + span] += value


def make_onehot(base_ref, hot):
    flat = base_ref[1:2, :] * SZ + base_ref[2:3, :]
    for r in range(0, NB, 128):
        row = lax.broadcasted_iota(jnp.int32, (128, flat.shape[1]), 0) + r
        hot[r : r + 128, :] = (row == flat).astype(jnp.float32).astype(jnp.bfloat16)


def scatter(part, base_ref, weight, slope, hot, coef, left, nodes, dref, vref, xs_low, xs_high):
    count = part.shape[1]
    mass = part[0:1, :]
    scale = -time_step * part[1:2, :]
    coef[...] = jnp.zeros_like(coef)
    coef[0:1, :] = mass
    coef[1:2, :] = mass * part[23:24, :]
    coef[2:3, :] = mass * part[24:25, :]
    coef[3:6, :] = mass * part[2:5, :]
    for j in range(3):
        for i in range(3):
            coef[8 + 8 * j + 3 + i : 8 + 8 * j + 4 + i, :] = scale * part[14 + 3 * i + j : 15 + 3 * i + j, :]
    bx = jnp.broadcast_to(base_ref[0:1, :], (8, count))
    for bc in range(4):
        pair = []
        for a in range(2):
            k = 4 * a + bc
            term = weight[k : k + 1, :] * coef[0:8, :]
            for j in range(3):
                term = term + slope[8 * j + k : 8 * j + k + 1, :] * coef[8 + 8 * j : 16 + 8 * j, :]
            high = term.astype(jnp.bfloat16).astype(jnp.float32)
            pair.append((high, term - high))
        for x in range(CX + 2):
            for s in range(2):
                row = x * 64 + s * 32 + bc * 8
                value = jnp.where(bx == x, pair[0][s], jnp.where(bx == x - 1, pair[1][s], 0.0))
                left[row : row + 8, :] = value.astype(jnp.bfloat16)
    sums = lax.dot_general(left[...], hot[...], (((1,), (1,)), ((), ())), preferred_element_type=jnp.float32)
    sums = sums.reshape(CX + 2, 2, 4, 8, NB)
    sums = sums[:, 0] + sums[:, 1]
    total = None
    for bc in range(4):
        piece = sums[:, bc].reshape((CX + 2) * 8, NB)
        piece = jnp.concatenate([piece, jnp.zeros((piece.shape[0], LW - NB), jnp.float32)], axis=1)
        piece = pltpu.roll(piece, OFF + (bc >> 1) * SZ + (bc & 1), 1)
        total = piece if total is None else total + piece
    for x in range(CX + 2):
        nodes[x] = total[8 * x : 8 * x + 8, :]
    dref[...] = jnp.zeros_like(dref)
    vref[...] = jnp.zeros_like(vref)
    for x in range(CX + 2):
        for c in range(3):
            dref[c * DS + H - 1 + x : c * DS + H + x, :] = nodes[x, c : c + 1, :]
            vref[c * VS + x : c * VS + x + 1, :] = nodes[x, 3 + c : 4 + c, :]
    for c in range(3):
        at = c * DS + H - 1
        xs_high[c * KEEP : (c + 1) * KEEP, :] = dref[at + CX + 2 - KEEP : at + CX + 2, XA:XB]
        xs_low[c * KEEP : (c + 1) * KEEP, :] = dref[at : at + KEEP, XA:XB]
        at = 3 * KEEP + 2 * c
        xs_high[at : at + 2, :] = vref[c * VS + CX : c * VS + CX + 2, XA:XB]
        xs_low[at : at + 2, :] = vref[c * VS : c * VS + 2, XA:XB]


def only(has, value):
    return jnp.where(has, value, jnp.zeros_like(value))


def add_x(dref, vref, from_low, from_high, has_low, has_high, ys_low, ys_high):
    low = only(has_low, from_low[...])
    high = only(has_high, from_high[...])
    for c in range(3):
        dref[c * DS : c * DS + KEEP, XA:XB] += low[c * KEEP : (c + 1) * KEEP]
        dref[c * DS + SX - KEEP : c * DS + SX, XA:XB] += high[c * KEEP : (c + 1) * KEEP]
        at = 3 * KEEP + 2 * c
        vref[c * VS : c * VS + 2, XA:XB] += low[at : at + 2]
        vref[c * VS + CX : c * VS + CX + 2, XA:XB] += high[at : at + 2]
    half = VR // 2
    for ys, d0, v0 in ((ys_high, CY * SZ, (H - 1 + CY) * SZ), (ys_low, (H - 1) * SZ, (H - 1) * SZ)):
        ys[:DR, :] = take(dref.at[:DR], d0, KEEP * SZ)
        near = take(vref, v0, 2 * SZ)
        ys[DR:, 0:128] = near[:half]
        ys[DR:, 128:256] = near[half:]


def lane_z():
    lane = lax.broadcasted_iota(jnp.int32, (8, LW), 1).astype(jnp.float32)
    y = jnp.floor((lane + 0.5) * (1.0 / SZ))
    return lane - SZ * y, y


def in_slot(z, at, width):
    return (z >= at) & (z < at + width)


def spin(value, shift):
    shift = shift % value.shape[1]
    return pltpu.roll(value, shift, 1) if shift else value


def add_y(dref, vref, from_low, from_high, has_low, has_high, zs_low, zs_high):
    for got, has, d0, v0 in (
        (from_low, has_low, 0, (H - 1) * SZ),
        (from_high, has_high, (SY - KEEP) * SZ, (H - 1 + CY) * SZ),
    ):
        put_add(dref.at[:DR], d0, KEEP * SZ, only(has, got[:DR, :]))
        near = jnp.concatenate([got[DR:, 0:128], got[DR:, 128:256]], axis=0)
        put_add(vref, v0, 2 * SZ, only(has, near))
    z, _ = lane_z()
    short = z[:, :ZV]
    for zs, d0, v0 in ((zs_high, CZ, H - 1 + CZ), (zs_low, H - 1, H - 1)):
        for block in range(ZB):
            out = jnp.zeros((8, LW), jnp.float32)
            for s in range(min(SLOTS, DT - block * SLOTS)):
                r = 8 * (block * SLOTS + s)
                value = spin(dref[r : r + 8, :], s * KEEP - d0)
                out = jnp.where(in_slot(z, s * KEEP, KEEP), value, out)
            zs[:, block * LW : (block + 1) * LW] = out
        out = jnp.zeros((8, ZV), jnp.float32)
        for t in range(VT):
            for q in range(FOLDS):
                at = 2 * (t * FOLDS + q)
                value = take(vref.at[8 * t : 8 * t + 8], (H - 1) * SZ + q * FW + v0, FW)
                value = spin(value, at)
                out = jnp.where(in_slot(short, at, 2), value, out)
        zs[:, ZB * LW :] = out


def add_z(dref, vref, from_low, from_high, has_low, has_high):
    z, _ = lane_z()
    short = z[:, :ZV]
    lane = lax.broadcasted_iota(jnp.int32, (8, ZV), 1)
    for got, has, d0, v0 in (
        (from_low, has_low, 0, H - 1),
        (from_high, has_high, SZ - KEEP, H - 1 + CZ),
    ):
        for block in range(ZB):
            whole = only(has, got[:, block * LW : (block + 1) * LW])
            for s in range(min(SLOTS, DT - block * SLOTS)):
                r = 8 * (block * SLOTS + s)
                value = jnp.where(in_slot(z, s * KEEP, KEEP), whole, 0.0)
                dref[r : r + 8, :] += spin(value, d0 - s * KEEP)
        whole = only(has, got[:, ZB * LW :])
        for t in range(VT):
            for q in range(FOLDS):
                at = 2 * (t * FOLDS + q)
                value = jnp.where(in_slot(short, at, 2) & (lane < FW), whole, 0.0)
                value = spin(value, -at)
                put_add(vref.at[8 * t : 8 * t + 8], (H - 1) * SZ + q * FW + v0, FW, value)


def relax_all(dref, vref, place, nodes_x, nodes_y, nodes_z, wet, fields, field_left, damage_out):
    ix, iy, iz = place
    z, y = lane_z()
    z, y = z[0:1], y[0:1]
    gz = z - H + (iz * CZ).astype(jnp.float32)
    gy = y - H + (iy * CY).astype(jnp.float32)
    flat_in = (gz >= 0) & (gz < nodes_z) & (gy >= 0) & (gy < nodes_y) & (y < SY)
    row = lax.broadcasted_iota(jnp.int32, (RD, 1), 0)
    gx = row - H + ix * CX
    row_in = (gx >= 0) & (gx < nodes_x) & (row < SX)
    inside = row_in.astype(jnp.float32) * flat_in.astype(jnp.float32)
    mass = jnp.maximum(dref[0:RD, :], mass_floor)
    damage = dref[DS : DS + RD, :] / mass * inside
    drive = dref[2 * DS : 2 * DS + RD, :] / mass
    wet[0:RD, :] = mass
    wet[RD : 2 * RD, :] = inside
    for _ in range(SUBSTEPS):
        ring = (
            pltpu.roll(damage, 1, 0)
            + pltpu.roll(damage, RD - 1, 0)
            + pltpu.roll(damage, SZ, 1)
            + pltpu.roll(damage, LW - SZ, 1)
            + pltpu.roll(damage, 1, 1)
            + pltpu.roll(damage, LW - 1, 1)
        )
        laplace = ring - 6.0 * damage
        damage = (damage + relax_rate * (length_sq * laplace - damage + 2.0 * (1.0 - damage) * drive)) * inside
    wet[2 * RD : 3 * RD, :] = damage
    own = wet[2 * RD + H : 2 * RD + H + CX, :]
    for y in range(CY):
        damage_out[:, y, :] = pltpu.roll(own, LW - (H + y) * SZ - H, 1)[:, :CZ]
    n = CX + 2
    factor = wet[RD + H - 1 : RD + H - 1 + n, :] / wet[H - 1 : H - 1 + n, :]
    fields[...] = jnp.zeros_like(fields)
    for c in range(3):
        fields[c * 16 : c * 16 + n, :] = vref[c * VS : c * VS + n, :] * factor
    fields[48 : 48 + n, :] = wet[2 * RD + H - 1 : 2 * RD + H - 1 + n, :]
    whole = fields[...]
    for bc in range(4):
        moved = pltpu.roll(whole, LW - OFF - (bc >> 1) * SZ - (bc & 1), 1)[:, :NB]
        for f in range(4):
            for x in range(n):
                r = x * 16 + f * 4 + bc
                field_left[r : r + 1, :] = moved[f * 16 + x : f * 16 + x + 1, :]


def advance(part, base_ref, weight, slope, hot, field_left, out, at, count):
    lanes = slice(at, at + count)
    there = slice(TAIL + at, TAIL + at + count)
    n = CX + 2
    high, low = split(field_left[...])
    got = jnp.dot(high, hot[:, lanes], preferred_element_type=jnp.float32)
    got = got + jnp.dot(low, hot[:, lanes], preferred_element_type=jnp.float32)
    bx = jnp.broadcast_to(base_ref[0:1, lanes], (16, count))
    near = [jnp.zeros((16, count), jnp.float32), jnp.zeros((16, count), jnp.float32)]
    for x in range(n):
        rows = got[16 * x : 16 * x + 16]
        near[0] = jnp.where(bx == x, rows, near[0])
        near[1] = jnp.where(bx == x - 1, rows, near[1])
    w = weight[:, lanes]
    g = [slope[8 * j : 8 * j + 8, lanes] for j in range(3)]
    corner = [jnp.concatenate([near[0][4 * f : 4 * f + 4], near[1][4 * f : 4 * f + 4]], axis=0) for f in range(4)]
    total = lambda v: jnp.sum(v, axis=0, keepdims=True)
    moved = [total(w * corner[i]) for i in range(3)]
    velgrad = [[total(corner[i] * g[j]) for j in range(3)] for i in range(3)]
    damage_node = total(w * corner[3])
    p = lambda r: part[r : r + 1, lanes]
    deform = [[p(5 + 3 * i + j) for j in range(3)] for i in range(3)]
    stretch = [[(1.0 if i == j else 0.0) + time_step * velgrad[i][j] for j in range(3)] for i in range(3)]
    mapped = [
        [stretch[i][0] * deform[0][j] + stretch[i][1] * deform[1][j] + stretch[i][2] * deform[2][j] for j in range(3)]
        for i in range(3)
    ]
    jacobian = (
        mapped[0][0] * (mapped[1][1] * mapped[2][2] - mapped[1][2] * mapped[2][1])
        - mapped[0][1] * (mapped[1][0] * mapped[2][2] - mapped[1][2] * mapped[2][0])
        + mapped[0][2] * (mapped[1][0] * mapped[2][1] - mapped[1][1] * mapped[2][0])
    )
    left = {}
    for i in range(3):
        for j in range(i, 3):
            left[i, j] = mapped[i][0] * mapped[j][0] + mapped[i][1] * mapped[j][1] + mapped[i][2] * mapped[j][2]
            left[j, i] = left[i, j]
    damaged = jnp.maximum(p(23), damage_node)
    degrade = (1.0 - damaged) ** 2
    swell = bulk_coef * (jacobian - 1.0)

    def put(r, value):
        out[r : r + 1, there] = value

    out[0:2, there] = part[0:2, lanes]
    for i in range(3):
        put(2 + i, moved[i])
        put(25 + i, p(25 + i) + time_step * moved[i])
        for j in range(3):
            put(5 + 3 * i + j, mapped[i][j])
            term = shear_mod * (left[i, j] - (1.0 if i == j else 0.0))
            if i == j:
                term = term + swell
            put(14 + 3 * i + j, degrade * term)
    put(23, damaged)
    energy = 0.5 * shear_mod * (left[0, 0] + left[1, 1] + left[2, 2] - 3.0) + 0.5 * bulk_coef * (jacobian - 1.0) ** 2
    put(24, jnp.maximum(p(24), energy))


def step_kernel(
    sizes, part, base_ref, weight, slope, counts, ext, prior_out, damage_out,
    hot, coef, left, nodes, dref, vref, wet, fields, field_left,
    sx, rx, sy, ry, sz, rz, tell, told, send_sem, recv_sem,
):
    names = ("gx", "gy", "gz")
    place = [lax.axis_index(a) for a in names]
    has_low = [i > 0 for i in place]
    has_high = [i < n - 1 for i, n in zip(place, sizes)]
    last = sizes[2]
    following, previous = lax.rem(place[2] + 1, last), lax.rem(place[2] + last - 1, last)
    barrier = pltpu.get_barrier_semaphore()
    waits = 2
    for k in range(2):
        for has, other in ((has_low[k], place[k] - 1), (has_high[k], place[k] + 1)):
            @pl.when(has)
            def _(k=k, other=other):
                pl.semaphore_signal(barrier, inc=1, device_id={names[k]: other}, device_id_type=MESH)
            waits = waits + has.astype(jnp.int32)
    for other in (following, previous):
        pl.semaphore_signal(barrier, inc=1, device_id={"gz": other}, device_id_type=MESH)

    make_onehot(base_ref, hot)
    scatter(part, base_ref, weight, slope, hot, coef, left, nodes, dref, vref, sx.at[0], sx.at[1])
    pl.semaphore_wait(barrier, waits)

    def copies(k, src, dst):
        made = []
        for d, other in ((0, place[k] - 1), (1, place[k] + 1)):
            made.append(pltpu.make_async_remote_copy(
                src_ref=src.at[d], dst_ref=dst.at[1 - d], send_sem=send_sem.at[k, d],
                recv_sem=recv_sem.at[k, 1 - d], device_id={names[k]: other}, device_id_type=MESH))
        return made

    def exchange(k, src, dst):
        made = copies(k, src, dst)
        ahead = ((has_low[k], made[0]), (has_high[k], made[1]))
        for has, copy in ahead:
            @pl.when(has)
            def _(copy=copy):
                copy.start()
        for has, copy in ((has_low[k], made[1]), (has_high[k], made[0])):
            @pl.when(has)
            def _(copy=copy):
                copy.wait_recv()
        for has, copy in ahead:
            @pl.when(has)
            def _(copy=copy):
                copy.wait_send()

    exchange(0, sx, rx)
    add_x(dref, vref, rx.at[0], rx.at[1], has_low[0], has_high[0], sy.at[0], sy.at[1])
    exchange(1, sy, ry)
    add_y(dref, vref, ry.at[0], ry.at[1], has_low[1], has_high[1], sz.at[0], sz.at[1])
    exchange(2, sz, rz)
    add_z(dref, vref, rz.at[0], rz.at[1], has_low[2], has_high[2])
    relax_all(dref, vref, place, sizes[0] * CX, sizes[1] * CY, sizes[2] * CZ, wet, fields, field_left, damage_out)
    count = part.shape[1]

    def to_next(src, dst, slot):
        copy = pltpu.make_async_remote_copy(
            src_ref=src, dst_ref=dst, send_sem=send_sem.at[3 + slot, 0], recv_sem=recv_sem.at[3 + slot, 0],
            device_id={"gz": following}, device_id_type=MESH)
        copy.start()
        return copy

    tell[...] = jnp.broadcast_to(counts[0], tell.shape)
    flying = [to_next(tell, told, 0)]
    chunk = TAIL // 2
    for k in (1, 0):
        at = count - TAIL + k * chunk
        advance(part, base_ref, weight, slope, hot, field_left, ext, at, chunk)
        flying.append(to_next(ext.at[:, TAIL + at : TAIL + at + chunk], ext.at[:, k * chunk : (k + 1) * chunk], 1 + k))
    for at in range(0, count - TAIL, chunk):
        advance(part, base_ref, weight, slope, hot, field_left, ext, at, min(chunk, count - TAIL - at))
    ext[:, TAIL + count :] = jnp.zeros((28, TAIL), jnp.float32)
    for copy in flying:
        copy.wait()
    prior_out[...] = told[...]
    for j in range(count // BIN - MOST, count // BIN):
        gone = jnp.broadcast_to(counts[0], (28, BIN)) >= count // BIN - j
        lanes = slice(TAIL + j * BIN, TAIL + (j + 1) * BIN)
        ext[:, lanes] = jnp.where(gone, 0.0, ext[:, lanes])


def place_kernel(ext, prior_ref, damage_in, migrated, damage_out, sem):
    width = migrated.shape[1]
    start = pl.multiple_of((MOST - prior_ref[0, 0]) * BIN, BIN)
    copies = [
        pltpu.make_async_copy(ext.at[:, pl.ds(start, width)], migrated, sem.at[0]),
        pltpu.make_async_copy(damage_in, damage_out, sem.at[1]),
    ]
    for copy in copies:
        copy.start()
    for copy in copies:
        copy.wait()


def per_device(particles, stencil_base, weights, gradients, counts):
    count = particles.shape[1]
    sizes = tuple(lax.axis_size(a) for a in ("gx", "gy", "gz"))
    vmem = pl.BlockSpec(memory_space=pltpu.VMEM)
    f32 = jnp.float32
    ext, prior, near_damage = pl.pallas_call(
        functools.partial(step_kernel, sizes),
        name="step",
        out_shape=(
            pltpu.VMEM((28, count + 2 * TAIL), f32),
            pltpu.VMEM((8, 128), jnp.int32),
            pltpu.VMEM((CX, CY, CZ), f32),
        ),
        in_specs=[vmem] * 4 + [pl.BlockSpec(memory_space=pltpu.SMEM)],
        out_specs=(vmem,) * 3,
        scratch_shapes=[
            pltpu.VMEM((NB, count), jnp.bfloat16),
            pltpu.VMEM((32, count), f32),
            pltpu.VMEM(((CX + 2) * 64, count), jnp.bfloat16),
            pltpu.VMEM((CX + 2, 8, LW), f32),
            pltpu.VMEM((up_to(2 * DS + RD, 8), LW), f32),
            pltpu.VMEM((VR, LW), f32),
            pltpu.VMEM((3 * RD, LW), f32),
            pltpu.VMEM((64, LW), f32),
            pltpu.VMEM(((CX + 2) * 16, NB), f32),
            pltpu.VMEM((2, XROWS, XB - XA), f32),
            pltpu.VMEM((2, XROWS, XB - XA), f32),
            pltpu.VMEM((2, YROWS, YW), f32),
            pltpu.VMEM((2, YROWS, YW), f32),
            pltpu.VMEM((2, 8, ZW), f32),
            pltpu.VMEM((2, 8, ZW), f32),
            pltpu.VMEM((8, 128), jnp.int32),
            pltpu.VMEM((8, 128), jnp.int32),
            pltpu.SemaphoreType.DMA((6, 2)),
            pltpu.SemaphoreType.DMA((6, 2)),
        ],
        compiler_params=pltpu.CompilerParams(
            collective_id=0, has_side_effects=True, vmem_limit_bytes=60 * 1024 * 1024
        ),
    )(particles, stencil_base, weights, gradients.reshape(24, count), counts)
    return pl.pallas_call(
        place_kernel,
        name="place",
        out_shape=(
            jax.ShapeDtypeStruct((28, count + TAIL), f32),
            jax.ShapeDtypeStruct((CX, CY, CZ), f32),
        ),
        in_specs=[pl.BlockSpec(memory_space=pl.ANY), pl.BlockSpec(memory_space=pltpu.VMEM), pl.BlockSpec(memory_space=pl.ANY)],
        out_specs=(pl.BlockSpec(memory_space=pl.ANY),) * 2,
        scratch_shapes=[pltpu.SemaphoreType.DMA((2,))],
        compiler_params=pltpu.CompilerParams(vmem_limit_bytes=4 * 1024 * 1024),
    )(ext, prior, near_damage)


def solution(mesh):
    return jax.shard_map(
        per_device,
        mesh=mesh,
        in_specs=(
            P(None, ("gx", "gy", "gz")),
            P(None, ("gx", "gy", "gz")),
            P(None, ("gx", "gy", "gz")),
            P(None, None, ("gx", "gy", "gz")),
            P(("gx", "gy", "gz")),
        ),
        out_specs=(P(None, ("gx", "gy", "gz")), P("gx", "gy", "gz")),
        check_vma=False,
    )
```

```python
import functools
import jax
import jax.numpy as jnp
from jax import lax
from jax.experimental import pallas as pl
from jax.experimental.pallas import tpu as pltpu
from jax.sharding import PartitionSpec as P

CX = 8
CY = 16
CZ = 32
NBIN = 16
BIN = 128
SUBSTEPS = 4
MOST = 8

time_step = 0.1
relax_rate = 0.2
length_sq = 0.6
shear_mod = 1.0
bulk_coef = 1.5
mass_floor = 0.5

MESH = pl.DeviceIdType.MESH


def up_to(value, unit):
    return (value + unit - 1) // unit * unit


H = SUBSTEPS + 1
EX, EY, EZ = CX + 2, CY + 2, CZ + 2
SX, SY, SZ = CX + 2 * H, CY + 2 * H, CZ + 2 * H
LANE = 128
LW = up_to(SY * SZ, LANE)
NB = up_to((CY + 1) * SZ + CZ + 2, LANE)
JB = NB // LANE
OFF = (H - 1) * SZ + H - 1
KEEP = H + 1
RD = 24
ROWS = 32
LEFT = EX * 24
PATTERNS = 3
WIDE = {0: KEEP, 1: 2}
FACE = {0: up_to(KEEP * SZ, LANE), 1: up_to(2 * SZ, LANE)}
ZA, ZB = (H - 1) * SZ // LANE * LANE, up_to((H + CY + 1) * SZ, LANE)
FL = EX * 16
TAIL = MOST * BIN
PARTS = 28
SLOT = 32
GROUPS = 8
LATE = 13
EARLY = 7
DIRS = [(dy, dz) for dy in (-1, 0, 1) for dz in (-1, 0, 1) if (dy, dz) != (0, 0)]


def iota(shape, axis):
    return lax.broadcasted_iota(jnp.int32, shape, axis)


def take(value, lane0, width):
    a = lane0 // LANE * LANE
    span = up_to(lane0 - a + width, LANE)
    value = value[:, a : a + span]
    shift = (span - (lane0 - a)) % span
    if shift:
        value = pltpu.roll(value, shift, 1)
    value = value[:, : up_to(width, LANE)]
    return jnp.where(iota(value.shape, 1) < width, value, 0.0)


def put_add(ref, lane0, width, value):
    a = lane0 // LANE * LANE
    span = max(up_to(lane0 - a + width, LANE), value.shape[1])
    extra = span - value.shape[1]
    if extra:
        value = jnp.concatenate([value, jnp.zeros((value.shape[0], extra), jnp.float32)], axis=1)
    if lane0 - a:
        value = pltpu.roll(value, lane0 - a, 1)
    ref[:, a : a + span] += value


def spin(value, shift):
    shift = shift % value.shape[1]
    return pltpu.roll(value, shift, 1) if shift else value


def only(has, value):
    return jnp.where(has, value, jnp.zeros_like(value))


def lane_z(rows):
    lane = lax.broadcasted_iota(jnp.int32, (rows, LW), 1).astype(jnp.float32)
    y = jnp.floor((lane + 0.5) * (1.0 / SZ))
    return lane - SZ * y, y


def make_onehot(base_ref, hot):
    flat = base_ref[1:2, :] * SZ + base_ref[2:3, :]
    flat = jnp.broadcast_to(flat, (16, flat.shape[1])).astype(jnp.int16)
    row = lax.broadcasted_iota(jnp.int32, flat.shape, 0).astype(jnp.int16)
    one, zero = jnp.bfloat16(1), jnp.bfloat16(0)
    for r in range(0, NB, 16):
        hot[r : r + 16, :] = jnp.where(row + jnp.int16(r) == flat, one, zero)


def make_left(terms, base_ref, left):
    count = terms[0].shape[1]
    low = iota((8, count), 0) < 4
    turned = [pltpu.roll(t, 4, 0) for t in terms]
    patterns = []
    for a in range(2):
        def join(p, q):
            return jnp.where(low, turned[p] if a else terms[p], terms[q] if a else turned[q])
        parts = [join(0, 1), join(2, 0), join(1, 2)]
        high = [v.astype(jnp.bfloat16).astype(jnp.float32) for v in parts[:2]]
        high_of_last = parts[2].astype(jnp.bfloat16).astype(jnp.float32)
        groups = [high[0], jnp.where(low, high[1], parts[1] - high[1]), parts[2] - high_of_last]
        patterns.append([
            jnp.concatenate([groups[i], groups[j]], axis=0).astype(jnp.bfloat16) for i, j in ((0, 1), (2, 0), (1, 2))
        ])
    bx = jnp.broadcast_to(base_ref[0:1, :], (16, count))
    step = bx - (iota((16, count), 0) >= 8).astype(jnp.int32)
    bx, step = (v.astype(jnp.float32).astype(jnp.bfloat16) for v in (bx, step))
    zero = jnp.bfloat16(0)
    for t in range(LEFT // 16):
        pair, k = divmod(t, 3)
        x = 2 * pair + (1 if k == 2 else 0)
        where = step if k == 1 else bx
        value = jnp.where(
            where == jnp.bfloat16(x), patterns[0][k],
            jnp.where(where == jnp.bfloat16(x - 1), patterns[1][k], zero))
        left[16 * t : 16 * t + 16, :] = value


def gather_sums(left, hot, sums, acc):
    total = lax.dot_general(left[...], hot[...], (((1,), (1,)), ((), ())), preferred_element_type=jnp.float32)
    for j in range(JB):
        sums[j * LEFT : (j + 1) * LEFT, :] = total[:, j * LANE : (j + 1) * LANE]
    sums[JB * LEFT :, :] = jnp.zeros((8, LANE), jnp.float32)
    row = iota((8, LANE), 0)
    pieces = []
    for bc in range(4):
        tiles = []
        for j in range(JB):
            base = j * LEFT + bc
            column = [
                sums[pl.ds(base + 4 * c, 8, stride=24), :] + sums[pl.ds(base + 12 + 4 * c, 8, stride=24), :]
                for c in range(3)
            ]
            first = sums[pl.ds(base + 192, 8, stride=4), :]
            second = sums[pl.ds(base + 216, 8, stride=4), :]
            first = first + pltpu.roll(first, 5, 0)
            second = pltpu.roll(second + pltpu.roll(second, 5, 0), 4, 0)
            last = jnp.where(row < 3, first, jnp.where((row >= 4) & (row < 7), second, 0.0))
            tiles.append(jnp.concatenate(column + [last], axis=0))
        pieces.append(jnp.concatenate(tiles, axis=1))
    near = [pieces[2 * b] + pltpu.roll(pieces[2 * b + 1], 1, 1) for b in range(2)]
    total = near[0] + pltpu.roll(near[1], SZ, 1)
    total = jnp.concatenate([total, jnp.zeros((ROWS, LW - NB), jnp.float32)], axis=1)
    acc[...] = pltpu.roll(total, OFF, 1)


def damage_terms(part, weight):
    w = weight[...]
    share = part[0:1, :] * w
    return [share, share * part[23:24, :], share * part[24:25, :]]


def velocity_terms(part, weight, slope):
    mass = part[0:1, :]
    scale = -time_step * part[1:2, :]
    terms = []
    for i in range(3):
        term = (mass * part[2 + i : 3 + i, :]) * weight[...]
        for j in range(3):
            term = term + (scale * part[14 + 3 * i + j : 15 + 3 * i + j, :]) * slope[8 * j : 8 * j + 8, :]
        terms.append(term)
    return terms


def send_spots(kind):
    if kind:
        return ((H - 1) * SZ, (H - 1 + CY) * SZ), (H - 1, H - 1 + CZ)
    return ((H - 1) * SZ, CY * SZ), (H - 1, CZ)


def land_spots(kind):
    if kind:
        return ((H - 1) * SZ, (H - 1 + CY) * SZ), (H - 1, H - 1 + CZ)
    return (0, (SY - KEEP) * SZ), (0, SZ - KEEP)


def pack_y(kind, acc, ysend):
    for d, lane0 in enumerate(send_spots(kind)[0]):
        ysend[d] = take(acc[...], lane0, WIDE[kind] * SZ)


def pack_z(kind, acc, zsend, esend):
    wide = WIDE[kind]
    y_at, z_at = send_spots(kind)
    z, _ = lane_z(8)
    for d, z0 in enumerate(z_at):
        out = jnp.zeros((8, LW), jnp.float32)
        for s in range(4):
            value = spin(acc[8 * s : 8 * s + 8, :], s * wide - z0)
            out = jnp.where((z >= s * wide) & (z < (s + 1) * wide), value, out)
        zsend[d] = out[:, ZA:ZB]
        for e, lane0 in enumerate(y_at):
            esend[2 * e + d] = take(out, lane0, wide * SZ)


def land_y(kind, acc, yrecv, has):
    for d, lane0 in enumerate(land_spots(kind)[0]):
        put_add(acc, lane0, WIDE[kind] * SZ, only(has(2 * d - 1, 0), yrecv[d]))


def land_z(kind, acc, zrecv, erecv, zin, has):
    wide = WIDE[kind]
    y_at, z_at = land_spots(kind)
    z, _ = lane_z(8)
    for d, z0 in enumerate(z_at):
        zin[:, :ZA] = jnp.zeros((8, ZA), jnp.float32)
        zin[:, ZB:] = jnp.zeros((8, LW - ZB), jnp.float32)
        zin[:, ZA:ZB] = only(has(0, 2 * d - 1), zrecv[d])
        for e, lane0 in enumerate(y_at):
            put_add(zin, lane0, wide * SZ, only(has(2 * e - 1, 2 * d - 1), erecv[2 * e + d]))
        whole = zin[...]
        for s in range(4):
            value = jnp.where((z >= s * wide) & (z < (s + 1) * wide), whole, 0.0)
            acc[8 * s : 8 * s + 8, :] += spin(value, z0 - s * wide)


def tail_rows(last, c):
    row = iota(last.shape, 0)
    first = spin0(last, -c)
    second = spin0(last, -c - 3)
    return jnp.where(row == 0, first, jnp.where(row == 1, second, 0.0))


def spin0(value, shift):
    shift = shift % value.shape[0]
    return pltpu.roll(value, shift, 0) if shift else value


def build_full(acc, low, high, has_low, has_high):
    row = iota((8, LW), 0)
    own_last, low_last = acc[24:32, :], low[24:32, :]
    out = []
    for c in range(3):
        at = slice(8 * c, 8 * c + 8)
        first = only(has_low, jnp.where(row >= 4, low[at, :], 0.0))
        middle = acc[at, :] + only(has_low, tail_rows(low_last, c))
        last = tail_rows(own_last, c) + only(has_high, jnp.where(row < 6, high[at, :], 0.0))
        out.append(jnp.concatenate([first, middle, last], axis=0))
    return out


def relax_all(place, nodes, full, damage_out):
    ix, iy, iz = place
    z, y = lane_z(1)
    gz = z - H + (iz * CZ).astype(jnp.float32)
    gy = y - H + (iy * CY).astype(jnp.float32)
    flat_in = (gz >= 0) & (gz < nodes[2]) & (gy >= 0) & (gy < nodes[1]) & (y < SY)
    row = lax.broadcasted_iota(jnp.int32, (RD, 1), 0)
    gx = row - 4 - H + ix * CX
    row_in = (gx >= 0) & (gx < nodes[0]) & (row >= 4) & (row < 4 + SX)
    inside = row_in.astype(jnp.float32) * flat_in.astype(jnp.float32)
    mass = jnp.maximum(full[0], mass_floor)
    factor = inside / mass
    damage = full[1] * factor
    drive = full[2] * factor
    keep = (1.0 - relax_rate * (6.0 * length_sq + 1.0)) * inside - (2.0 * relax_rate) * drive
    push = (2.0 * relax_rate) * drive
    spread = (relax_rate * length_sq) * inside
    for _ in range(SUBSTEPS):
        ring = (
            pltpu.roll(damage, 1, 0)
            + pltpu.roll(damage, RD - 1, 0)
            + pltpu.roll(damage, SZ, 1)
            + pltpu.roll(damage, LW - SZ, 1)
            + pltpu.roll(damage, 1, 1)
            + pltpu.roll(damage, LW - 1, 1)
        )
        damage = spread * ring + keep * damage + push
    own = pltpu.roll(damage, RD - 4 - H, 0)[0:CX]
    for y in range(CY):
        damage_out[:, y, :] = pltpu.roll(own, LW - (H + y) * SZ - H, 1)[:, :CZ]
    return damage, factor


def make_fields(damage, factor, acc, low, high, has_low, has_high, field_left, lhs):
    row = iota((8, LW), 0)
    last = acc[24:32, :]
    low_last = only(has_low, low[24:32, :])
    velocity = []
    for c in range(3):
        at = slice(8 * c, 8 * c + 8)
        first = acc[at, :] + tail_rows(low_last, c)
        velocity.append(first * factor[8:16])
        from_high = only(has_high, high[at, :])
        last = last + jnp.where(row == c, spin0(from_high, c), jnp.where(row == 4 + c, spin0(from_high, 3 + c), 0.0))
    pair = lambda v: jnp.where(row < 4, jnp.broadcast_to(v[16:17], row.shape), jnp.broadcast_to(v[17:18], row.shape))
    last = jnp.where((row == 3) | (row == 7), pair(damage), last * pair(factor))
    whole = jnp.concatenate(velocity + [damage[8:16], last], axis=0)
    whole = pltpu.roll(whole, LW - OFF, 1)[:, :NB]
    turned = [whole, pltpu.roll(whole, NB - 1, 1)]
    for bc in range(4):
        moved = turned[bc & 1]
        if bc >> 1:
            moved = pltpu.roll(moved, NB - SZ, 1)
        for j in range(JB):
            lanes = slice(j * LANE, (j + 1) * LANE)
            for f in range(4):
                field_left[pl.ds(j * FL + 4 * f + bc, 8, stride=16), :] = moved[8 * f : 8 * f + 8, lanes]
            field_left[pl.ds(j * FL + 128 + bc, 8, stride=4), :] = moved[32:40, lanes]
    for j in range(JB):
        value = field_left[j * FL : (j + 1) * FL, :]
        high_part = value.astype(jnp.bfloat16)
        lhs[:FL, j * LANE : (j + 1) * LANE] = high_part
        lhs[FL:, j * LANE : (j + 1) * LANE] = (value - high_part.astype(jnp.float32)).astype(jnp.bfloat16)


def turn(group, natural, turned, bins):
    for j in range(bins):
        turned[(group * bins + j) * 8 : (group * bins + j + 1) * 8, :] = natural(j)


def corners(half, hot, lhs, got_ref, bx_ref):
    lanes = slice(half * TAIL, (half + 1) * TAIL)
    got = jnp.dot(lhs[...], hot[:, lanes], preferred_element_type=jnp.float32)
    for j in range(MOST):
        got_ref[j * 2 * FL : (j + 1) * 2 * FL, :] = got[:, j * LANE : (j + 1) * LANE]
    bx = bx_ref[MOST * half : MOST * half + MOST, :]
    at = [bx == x for x in range(CX + 1)]
    out = [[None] * 8 for _ in range(4)]
    for f in range(4):
        for bc in range(4):
            near = [jnp.zeros((MOST, LANE), jnp.float32)] * 2
            for x in range(EX):
                r = 16 * x + 4 * f + bc
                value = got_ref[pl.ds(r, MOST, stride=2 * FL), :] + got_ref[pl.ds(FL + r, MOST, stride=2 * FL), :]
                if x < EX - 1:
                    near[0] = jnp.where(at[x], value, near[0])
                if x > 0:
                    near[1] = jnp.where(at[x - 1], value, near[1])
            out[f][bc], out[f][4 + bc] = near
    return out


def total(values):
    while len(values) > 1:
        values = [a + b for a, b in zip(values[::2], values[1::2])]
    return values[0]


def move(corner, w, g, p):
    moved = [total([w(k) * corner[i][k] for k in range(8)]) for i in range(3)]
    velgrad = [[total([corner[i][k] * g(j, k) for k in range(8)]) for j in range(3)] for i in range(3)]
    damaged = jnp.maximum(p(23), total([w(k) * corner[3][k] for k in range(8)]))
    deform = [[p(5 + 3 * i + j) for j in range(3)] for i in range(3)]
    stretch = [[(1.0 if i == j else 0.0) + time_step * velgrad[i][j] for j in range(3)] for i in range(3)]
    mapped = [
        stretch[i][0] * deform[0][j] + stretch[i][1] * deform[1][j] + stretch[i][2] * deform[2][j]
        for i in range(3) for j in range(3)
    ]
    return moved + mapped + [damaged]


def finish(late, early):
    moved, m, damaged = late[:3], late[3:12], late[12]
    mapped = [m[0:3], m[3:6], m[6:9]]
    jacobian = (
        mapped[0][0] * (mapped[1][1] * mapped[2][2] - mapped[1][2] * mapped[2][1])
        - mapped[0][1] * (mapped[1][0] * mapped[2][2] - mapped[1][2] * mapped[2][0])
        + mapped[0][2] * (mapped[1][0] * mapped[2][1] - mapped[1][1] * mapped[2][0])
    )
    left = {}
    for i in range(3):
        for j in range(i, 3):
            left[i, j] = mapped[i][0] * mapped[j][0] + mapped[i][1] * mapped[j][1] + mapped[i][2] * mapped[j][2]
            left[j, i] = left[i, j]
    degrade = (1.0 - damaged) ** 2
    swell = bulk_coef * (jacobian - 1.0)
    stress = []
    for i in range(3):
        for j in range(3):
            term = shear_mod * (left[i, j] - (1.0 if i == j else 0.0))
            if i == j:
                term = term + swell
            stress.append(degrade * term)
    energy = 0.5 * shear_mod * (left[0, 0] + left[1, 1] + left[2, 2] - 3.0) + 0.5 * bulk_coef * (jacobian - 1.0) ** 2
    history = jnp.maximum(early[2], energy)
    position = [early[3 + i] + time_step * moved[i] for i in range(3)]
    return early[:2] + moved + m + stress + [damaged, history] + position


def step_kernel(
    sizes, part, base_ref, weight, slope, counts, out, prior_out, damage_out,
    hot, left, sums, acc_d, acc_v, zin, field_left, lhs, got, turned, bx_ref,
    ysend_d, yrecv_d, zsend_d, zrecv_d, esend_d, erecv_d, ysend_v, yrecv_v, zsend_v, zrecv_v, esend_v, erecv_v,
    xrecv_d, xrecv_v, early_send, early_recv, late_send, late_recv, send_sem, recv_sem,
):
    names = ("gx", "gy", "gz")
    place = [lax.axis_index(a) for a in names]
    has_low = [i > 0 for i in place]
    has_high = [i < n - 1 for i, n in zip(place, sizes)]
    last = sizes[2]
    following, previous = lax.rem(place[2] + 1, last), lax.rem(place[2] + last - 1, last)
    count = part.shape[1]
    bins = count // BIN

    def has(dy, dz):
        found = None
        for k, d in ((1, dy), (2, dz)):
            if d:
                one = has_high[k] if d > 0 else has_low[k]
                found = one if found is None else found & one
        return found

    def device(dy, dz):
        return {names[k]: place[k] + d for k, d in ((1, dy), (2, dz)) if d}

    barrier = pltpu.get_barrier_semaphore()
    waits = 2
    ahead = [(has_low[0], {"gx": place[0] - 1}), (has_high[0], {"gx": place[0] + 1})]
    for exists, other in ahead + [(has(*d), device(*d)) for d in DIRS]:
        @pl.when(exists)
        def _(other=other):
            pl.semaphore_signal(barrier, inc=1, device_id=other, device_id_type=MESH)
        waits = waits + exists.astype(jnp.int32)
    for other in (following, previous):
        pl.semaphore_signal(barrier, inc=1, device_id={"gz": other}, device_id_type=MESH)

    pending = []

    def copy_to(slot, back, src, dst, other):
        return pltpu.make_async_remote_copy(
            src_ref=src, dst_ref=dst, send_sem=send_sem.at[slot], recv_sem=recv_sem.at[back],
            device_id=other, device_id_type=MESH)

    def bufs(kind):
        if kind:
            return (ysend_v, yrecv_v), (zsend_v, zrecv_v), (esend_v, erecv_v)
        return (ysend_d, yrecv_d), (zsend_d, zrecv_d), (esend_d, erecv_d)

    def message(kind, dy, dz):
        y, z = (dy + 1) // 2, (dz + 1) // 2
        if dz == 0:
            (src, dst), at, back = bufs(kind)[0], y, 1 - y
            base = 0
        elif dy == 0:
            (src, dst), at, back = bufs(kind)[1], z, 1 - z
            base = 2
        else:
            (src, dst), at, back = bufs(kind)[2], 2 * y + z, 2 * (1 - y) + 1 - z
            base = 4
        base += 8 * kind
        return copy_to(base + at, base + back, src.at[at], dst.at[back], device(dy, dz))

    def start(kind, chosen):
        for d in chosen:
            copy = message(kind, *d)
            pending.append((has(*d), copy))
            @pl.when(has(*d))
            def _(copy=copy):
                copy.start()

    def arrive(kind, chosen):
        for dy, dz in chosen:
            copy = message(kind, -dy, -dz)
            @pl.when(has(dy, dz))
            def _(copy=copy):
                copy.wait_recv()

    faces_y = [(-1, 0), (1, 0)]
    others = [d for d in DIRS if d[1] != 0]

    def x_messages(kind):
        acc, recv = (acc_v, xrecv_v) if kind else (acc_d, xrecv_d)
        base = 16 + 2 * kind
        return [copy_to(base + d, base + 1 - d, acc, recv.at[1 - d], {"gx": place[0] + 2 * d - 1}) for d in range(2)]

    def x_start(kind):
        for (exists, _), copy in zip(ahead, x_messages(kind)):
            pending.append((exists, copy))
            @pl.when(exists)
            def _(copy=copy):
                copy.start()

    def x_arrive(kind):
        made = x_messages(kind)
        for exists, copy in ((has_low[0], made[1]), (has_high[0], made[0])):
            @pl.when(exists)
            def _(copy=copy):
                copy.wait_recv()

    def ring(slot, src, dst):
        copy = copy_to(slot, slot, src, dst, {"gz": following})
        copy.start()
        return copy

    make_onehot(base_ref, hot)
    make_left(damage_terms(part, weight), base_ref, left)
    gather_sums(left, hot, sums, acc_d)
    pl.semaphore_wait(barrier, waits)
    pack_y(0, acc_d, ysend_d)
    start(0, faces_y)
    pack_z(0, acc_d, zsend_d, esend_d)
    start(0, others)

    make_left(velocity_terms(part, weight, slope), base_ref, left)
    gather_sums(left, hot, sums, acc_v)
    pack_y(1, acc_v, ysend_v)
    start(1, faces_y)
    pack_z(1, acc_v, zsend_v, esend_v)
    start(1, others)

    lanes = lambda j: slice(j * LANE, (j + 1) * LANE)
    for j in range(bins):
        for group in range(3):
            turned[(group * bins + j) * 8 : (group * bins + j + 1) * 8, :] = part[8 * group : 8 * group + 8, lanes(j)]
        turned[(3 * bins + j) * 8 : (3 * bins + j) * 8 + 4, :] = part[24:28, lanes(j)]
        turned[(4 * bins + j) * 8 : (4 * bins + j + 1) * 8, :] = weight[:, lanes(j)]
        for group in range(3):
            at = ((5 + group) * bins + j) * 8
            turned[at : at + 8, :] = slope[8 * group : 8 * group + 8, lanes(j)]
        bx_ref[j : j + 1, :] = base_ref[0:1, lanes(j)]

    def dense(half):
        def read(group, s):
            return turned[pl.ds((group * bins + half * MOST) * 8 + s, MOST, stride=8), :]
        return (
            lambda k: read(4, k), lambda j, k: read(5 + j, k), lambda r: read(r // 8, r % 8)
        )

    halves = bins // MOST
    flying = []
    _, _, p = dense(halves - 1)
    early = [p(0), p(1), p(24), p(25), p(26), p(27)]
    early.append(jnp.broadcast_to(counts[0], (8, LANE)).astype(jnp.float32))
    for q, value in enumerate(early):
        early_send[8 * q : 8 * q + 8, :] = value
    flying.append(ring(20, early_send, early_recv))
    for j in range(MOST + bins, 2 * MOST + bins):
        out[j * SLOT : (j + 1) * SLOT, :] = jnp.zeros((SLOT, LANE), jnp.float32)

    arrive(0, faces_y)
    land_y(0, acc_d, yrecv_d, has)
    arrive(0, others)
    land_z(0, acc_d, zrecv_d, erecv_d, zin, has)
    x_start(0)
    arrive(1, faces_y)
    land_y(1, acc_v, yrecv_v, has)
    arrive(1, others)
    land_z(1, acc_v, zrecv_v, erecv_v, zin, has)
    x_start(1)
    x_arrive(0)
    full = build_full(acc_d, xrecv_d.at[0], xrecv_d.at[1], has_low[0], has_high[0])
    nodes = [n * c for n, c in zip(sizes, (CX, CY, CZ))]
    damage, factor = relax_all(place, nodes, full, damage_out)
    x_arrive(1)
    make_fields(damage, factor, acc_v, xrecv_v.at[0], xrecv_v.at[1], has_low[0], has_high[0], field_left, lhs)

    def store(first, values, gone=None):
        for r, value in enumerate(values):
            if gone is not None:
                value = jnp.where(gone, 0.0, value)
            out[pl.ds(first * SLOT + r, MOST, stride=SLOT), :] = value

    for half in reversed(range(halves)):
        w, g, p = dense(half)
        late = move(corners(half, hot, lhs, got, bx_ref), w, g, p)
        gone = None
        if half == halves - 1:
            for q, value in enumerate(late):
                late_send[8 * q : 8 * q + 8, :] = value
            flying.append(ring(21, late_send, late_recv))
            gone = iota((MOST, LANE), 0) + jnp.broadcast_to(counts[0], (MOST, LANE)) >= MOST
        store((half + 1) * MOST, finish(late, [p(0), p(1), p(24), p(25), p(26), p(27)]), gone)

    for copy in flying:
        copy.wait_recv()
    rows = lambda ref, q: ref[8 * q : 8 * q + 8, :]
    store(0, finish([rows(late_recv, q) for q in range(LATE)], [rows(early_recv, q) for q in range(6)]))
    prior_out[...] = rows(early_recv, 6).astype(jnp.int32)
    for copy in flying:
        copy.wait_send()
    for exists, copy in pending:
        @pl.when(exists)
        def _(copy=copy):
            copy.wait_send()


def place_kernel(ext, prior_ref, damage_in, migrated, damage_out, sem, damage_sem):
    start = MOST - prior_ref[0, 0]
    copies = [pltpu.make_async_copy(damage_in, damage_out, damage_sem)]
    for j in range(migrated.shape[1] // BIN):
        copies.append(pltpu.make_async_copy(
            ext.at[pl.ds(pl.multiple_of((start + j) * SLOT, SLOT), PARTS)],
            migrated.at[:, pl.ds(j * BIN, BIN)], sem.at[j]))
    for copy in copies:
        copy.start()
    for copy in copies:
        copy.wait()


def per_device(particles, stencil_base, weights, gradients, counts):
    count = particles.shape[1]
    bins = count // BIN
    sizes = tuple(lax.axis_size(a) for a in ("gx", "gy", "gz"))
    vmem = pl.BlockSpec(memory_space=pltpu.VMEM)
    anywhere = pl.BlockSpec(memory_space=pl.ANY)
    f32 = jnp.float32
    two = lambda *shape: [pltpu.VMEM(shape, f32)] * 2
    ext, prior, near_damage = pl.pallas_call(
        functools.partial(step_kernel, sizes),
        name="step",
        out_shape=(
            pltpu.VMEM(((bins + 2 * MOST) * SLOT, LANE), f32),
            pltpu.VMEM((8, LANE), jnp.int32),
            pltpu.VMEM((CX, CY, CZ), f32),
        ),
        in_specs=[vmem] * 4 + [pl.BlockSpec(memory_space=pltpu.SMEM)],
        out_specs=(vmem,) * 3,
        scratch_shapes=[
            pltpu.VMEM((NB, count), jnp.bfloat16),
            pltpu.VMEM((LEFT, count), jnp.bfloat16),
            pltpu.VMEM((JB * LEFT + 8, LANE), f32),
            pltpu.VMEM((ROWS, LW), f32),
            pltpu.VMEM((ROWS, LW), f32),
            pltpu.VMEM((8, LW), f32),
            pltpu.VMEM((JB * FL, LANE), f32),
            pltpu.VMEM((2 * FL, NB), jnp.bfloat16),
            pltpu.VMEM((MOST * 2 * FL, LANE), f32),
            pltpu.VMEM((GROUPS * bins * 8, LANE), f32),
            pltpu.VMEM((bins, LANE), jnp.int32),
            *two(2, ROWS, FACE[0]),
            *two(2, 8, ZB - ZA),
            *two(4, 8, FACE[0]),
            *two(2, ROWS, FACE[1]),
            *two(2, 8, ZB - ZA),
            *two(4, 8, FACE[1]),
            *two(2, ROWS, LW),
            *two(EARLY * 8, LANE),
            *two(LATE * 8, LANE),
            pltpu.SemaphoreType.DMA((22,)),
            pltpu.SemaphoreType.DMA((22,)),
        ],
        compiler_params=pltpu.CompilerParams(
            collective_id=0, has_side_effects=True, vmem_limit_bytes=60 * 1024 * 1024
        ),
    )(particles, stencil_base, weights, gradients.reshape(24, count), counts)
    return pl.pallas_call(
        place_kernel,
        name="place",
        out_shape=(
            jax.ShapeDtypeStruct((PARTS, count + TAIL), f32),
            jax.ShapeDtypeStruct((CX, CY, CZ), f32),
        ),
        in_specs=[anywhere, vmem, anywhere],
        out_specs=(anywhere,) * 2,
        scratch_shapes=[pltpu.SemaphoreType.DMA((bins + MOST,)), pltpu.SemaphoreType.DMA(())],
        compiler_params=pltpu.CompilerParams(vmem_limit_bytes=4 * 1024 * 1024),
    )(ext, prior, near_damage)


def solution(mesh):
    return jax.shard_map(
        per_device,
        mesh=mesh,
        in_specs=(
            P(None, ("gx", "gy", "gz")),
            P(None, ("gx", "gy", "gz")),
            P(None, ("gx", "gy", "gz")),
            P(None, None, ("gx", "gy", "gz")),
            P(("gx", "gy", "gz")),
        ),
        out_specs=(P(None, ("gx", "gy", "gz")), P("gx", "gy", "gz")),
        check_vma=False,
    )
```

```python
import functools
import jax
import jax.numpy as jnp
from jax import lax
from jax.experimental import pallas as pl
from jax.experimental.pallas import tpu as pltpu
from jax.sharding import PartitionSpec as P

CX = 8
CY = 16
CZ = 32
NBIN = 16
BIN = 128
SUBSTEPS = 4
MOST = 8

time_step = 0.1
relax_rate = 0.2
length_sq = 0.6
shear_mod = 1.0
bulk_coef = 1.5
mass_floor = 0.5

MESH = pl.DeviceIdType.MESH


def up_to(value, unit):
    return (value + unit - 1) // unit * unit


H = SUBSTEPS + 1
EX, EY, EZ = CX + 2, CY + 2, CZ + 2
SX, SY, SZ = CX + 2 * H, CY + 2 * H, CZ + 2 * H
LANE = 128
MX = 256
LW = up_to(SY * SZ, LANE)
NB = up_to((CY + 1) * SZ + CZ + 2, MX)
JB = NB // LANE
OFF = (H - 1) * SZ + H - 1
KEEP = H + 1
RD = 24
ROWS = 32
LEFT = EX * 24
PATTERNS = 3
WIDE = {0: KEEP, 1: 2}
FACE = {0: up_to(KEEP * SZ, LANE), 1: up_to(2 * SZ, LANE)}
ZA, ZB = (H - 1) * SZ // LANE * LANE, up_to((H + CY + 1) * SZ, LANE)
FL = EX * 16
TAIL = MOST * BIN
PARTS = 28
SLOT = 32
GROUPS = 8
LATE = 13
EARLY = 7
DIRS = [(dy, dz) for dy in (-1, 0, 1) for dz in (-1, 0, 1) if (dy, dz) != (0, 0)]


def iota(shape, axis):
    return lax.broadcasted_iota(jnp.int32, shape, axis)


def take(value, lane0, width):
    a = lane0 // LANE * LANE
    span = up_to(lane0 - a + width, LANE)
    value = value[:, a : a + span]
    shift = (span - (lane0 - a)) % span
    if shift:
        value = pltpu.roll(value, shift, 1)
    value = value[:, : up_to(width, LANE)]
    return jnp.where(iota(value.shape, 1) < width, value, 0.0)


def put_add(ref, lane0, width, value):
    a = lane0 // LANE * LANE
    span = max(up_to(lane0 - a + width, LANE), value.shape[1])
    extra = span - value.shape[1]
    if extra:
        value = jnp.concatenate([value, jnp.zeros((value.shape[0], extra), jnp.float32)], axis=1)
    if lane0 - a:
        value = pltpu.roll(value, lane0 - a, 1)
    ref[:, a : a + span] += value


def spin(value, shift):
    shift = shift % value.shape[1]
    return pltpu.roll(value, shift, 1) if shift else value


def only(has, value):
    return jnp.where(has, value, jnp.zeros_like(value))


def lane_z(rows):
    lane = lax.broadcasted_iota(jnp.int32, (rows, LW), 1).astype(jnp.float32)
    y = jnp.floor((lane + 0.5) * (1.0 / SZ))
    return lane - SZ * y, y


def onehot(base, first):
    shape = (16, base.shape[1])
    flat = jnp.broadcast_to(base[1:2, :] * SZ + base[2:3, :], shape) - iota(shape, 0)
    flat = flat.astype(jnp.int16)
    one, zero = jnp.bfloat16(1), jnp.bfloat16(0)
    return jnp.concatenate([jnp.where(flat == jnp.int16(first + r), one, zero) for r in range(0, MX, 16)], axis=0)


def make_left(terms, base):
    count = terms[0].shape[1]
    low = iota((8, count), 0) < 4
    turned = [pltpu.roll(t, 4, 0) for t in terms]
    patterns = []
    for a in range(2):
        def join(p, q):
            return jnp.where(low, turned[p] if a else terms[p], terms[q] if a else turned[q])
        parts = [join(0, 1), join(2, 0), join(1, 2)]
        high = [v.astype(jnp.bfloat16).astype(jnp.float32) for v in parts[:2]]
        high_of_last = parts[2].astype(jnp.bfloat16).astype(jnp.float32)
        groups = [high[0], jnp.where(low, high[1], parts[1] - high[1]), parts[2] - high_of_last]
        patterns.append([
            jnp.concatenate([groups[i], groups[j]], axis=0).astype(jnp.bfloat16) for i, j in ((0, 1), (2, 0), (1, 2))
        ])
    bx = jnp.broadcast_to(base[0:1, :], (16, count))
    step = bx - (iota((16, count), 0) >= 8).astype(jnp.int32)
    bx, step = (v.astype(jnp.float32).astype(jnp.bfloat16) for v in (bx, step))
    zero = jnp.bfloat16(0)
    rows = []
    for t in range(LEFT // 16):
        pair, k = divmod(t, 3)
        x = 2 * pair + (1 if k == 2 else 0)
        where = step if k == 1 else bx
        value = jnp.where(
            where == jnp.bfloat16(x), patterns[0][k],
            jnp.where(where == jnp.bfloat16(x - 1), patterns[1][k], zero))
        rows.append(value)
    return jnp.concatenate(rows, axis=0)


def scatter(terms, base_ref, sums, acc):
    count = base_ref.shape[1]
    tiles = NB // MX

    def multiply(*accs):
        for k in range(count // MX):
            lanes = slice(k * MX, (k + 1) * MX)
            base = base_ref[:, lanes]
            left = make_left(terms(lanes), base)
            for n in range(tiles):
                extra = n == tiles - 1 and tiles % 2
                m = k % 2 if extra else n % 2
                pltpu.matmul_push_rhs(onehot(base, n * MX), int(n >= 2), m, transpose=True)
                pltpu.matmul_acc_lhs(accs[n + m if extra else n], left, load_staged_rhs=int(n >= 2))
        for n in range(tiles):
            value = pltpu.matmul_pop(accs[n])
            if n == tiles - 1 and tiles % 2:
                value = value + pltpu.matmul_pop(accs[n + 1])
            for j in range(MX // LANE):
                at = (n * MX // LANE + j) * LEFT
                sums[at : at + LEFT, :] = value[:, j * LANE : (j + 1) * LANE]

    pl.run_scoped(multiply, *[pltpu.ACC(n % 2)((LEFT, MX), jnp.float32) for n in range(up_to(tiles, 2))])
    sums[JB * LEFT :, :] = jnp.zeros((8, LANE), jnp.float32)
    row = iota((8, LANE), 0)
    pieces = []
    for bc in range(4):
        tiles = []
        for j in range(JB):
            base = j * LEFT + bc
            column = [
                sums[pl.ds(base + 4 * c, 8, stride=24), :] + sums[pl.ds(base + 12 + 4 * c, 8, stride=24), :]
                for c in range(3)
            ]
            first = sums[pl.ds(base + 192, 8, stride=4), :]
            second = sums[pl.ds(base + 216, 8, stride=4), :]
            first = first + pltpu.roll(first, 5, 0)
            second = pltpu.roll(second + pltpu.roll(second, 5, 0), 4, 0)
            last = jnp.where(row < 3, first, jnp.where((row >= 4) & (row < 7), second, 0.0))
            tiles.append(jnp.concatenate(column + [last], axis=0))
        pieces.append(jnp.concatenate(tiles, axis=1))
    near = [pieces[2 * b] + pltpu.roll(pieces[2 * b + 1], 1, 1) for b in range(2)]
    total = near[0] + pltpu.roll(near[1], SZ, 1)
    total = jnp.concatenate([total, jnp.zeros((ROWS, LW - NB), jnp.float32)], axis=1)
    acc[...] = pltpu.roll(total, OFF, 1)


def damage_terms(part, weight):
    def terms(lanes):
        share = part[0:1, lanes] * weight[:, lanes]
        return [share, share * part[23:24, lanes], share * part[24:25, lanes]]
    return terms


def velocity_terms(part, weight, slope):
    def terms(lanes):
        mass = part[0:1, lanes]
        scale = -time_step * part[1:2, lanes]
        out = []
        for i in range(3):
            term = (mass * part[2 + i : 3 + i, lanes]) * weight[:, lanes]
            for j in range(3):
                row = 14 + 3 * i + j
                term = term + (scale * part[row : row + 1, lanes]) * slope[8 * j : 8 * j + 8, lanes]
            out.append(term)
        return out
    return terms


def send_spots(kind):
    if kind:
        return ((H - 1) * SZ, (H - 1 + CY) * SZ), (H - 1, H - 1 + CZ)
    return ((H - 1) * SZ, CY * SZ), (H - 1, CZ)


def land_spots(kind):
    if kind:
        return ((H - 1) * SZ, (H - 1 + CY) * SZ), (H - 1, H - 1 + CZ)
    return (0, (SY - KEEP) * SZ), (0, SZ - KEEP)


def pack_y(kind, acc, ysend):
    for d, lane0 in enumerate(send_spots(kind)[0]):
        ysend[d] = take(acc[...], lane0, WIDE[kind] * SZ)


def pack_z(kind, acc, zsend, esend):
    wide = WIDE[kind]
    y_at, z_at = send_spots(kind)
    z, _ = lane_z(8)
    for d, z0 in enumerate(z_at):
        out = jnp.zeros((8, LW), jnp.float32)
        for s in range(4):
            value = spin(acc[8 * s : 8 * s + 8, :], s * wide - z0)
            out = jnp.where((z >= s * wide) & (z < (s + 1) * wide), value, out)
        zsend[d] = out[:, ZA:ZB]
        for e, lane0 in enumerate(y_at):
            esend[2 * e + d] = take(out, lane0, wide * SZ)


def land_y(kind, acc, yrecv, has):
    for d, lane0 in enumerate(land_spots(kind)[0]):
        put_add(acc, lane0, WIDE[kind] * SZ, only(has(2 * d - 1, 0), yrecv[d]))


def land_z(kind, acc, zrecv, erecv, zin, has):
    wide = WIDE[kind]
    y_at, z_at = land_spots(kind)
    z, _ = lane_z(8)
    for d, z0 in enumerate(z_at):
        zin[:, :ZA] = jnp.zeros((8, ZA), jnp.float32)
        zin[:, ZB:] = jnp.zeros((8, LW - ZB), jnp.float32)
        zin[:, ZA:ZB] = only(has(0, 2 * d - 1), zrecv[d])
        for e, lane0 in enumerate(y_at):
            put_add(zin, lane0, wide * SZ, only(has(2 * e - 1, 2 * d - 1), erecv[2 * e + d]))
        whole = zin[...]
        for s in range(4):
            value = jnp.where((z >= s * wide) & (z < (s + 1) * wide), whole, 0.0)
            acc[8 * s : 8 * s + 8, :] += spin(value, z0 - s * wide)


def tail_rows(last, c):
    row = iota(last.shape, 0)
    first = spin0(last, -c)
    second = spin0(last, -c - 3)
    return jnp.where(row == 0, first, jnp.where(row == 1, second, 0.0))


def spin0(value, shift):
    shift = shift % value.shape[0]
    return pltpu.roll(value, shift, 0) if shift else value


def build_full(acc, low, high, has_low, has_high):
    row = iota((8, LW), 0)
    own_last, low_last = acc[24:32, :], low[24:32, :]
    out = []
    for c in range(3):
        at = slice(8 * c, 8 * c + 8)
        first = only(has_low, jnp.where(row >= 4, low[at, :], 0.0))
        middle = acc[at, :] + only(has_low, tail_rows(low_last, c))
        last = tail_rows(own_last, c) + only(has_high, jnp.where(row < 6, high[at, :], 0.0))
        out.append(jnp.concatenate([first, middle, last], axis=0))
    return out


def relax_all(place, nodes, full, damage_out):
    ix, iy, iz = place
    z, y = lane_z(1)
    gz = z - H + (iz * CZ).astype(jnp.float32)
    gy = y - H + (iy * CY).astype(jnp.float32)
    flat_in = (gz >= 0) & (gz < nodes[2]) & (gy >= 0) & (gy < nodes[1]) & (y < SY)
    row = lax.broadcasted_iota(jnp.int32, (RD, 1), 0)
    gx = row - 4 - H + ix * CX
    row_in = (gx >= 0) & (gx < nodes[0]) & (row >= 4) & (row < 4 + SX)
    inside = row_in.astype(jnp.float32) * flat_in.astype(jnp.float32)
    mass = jnp.maximum(full[0], mass_floor)
    factor = inside / mass
    damage = full[1] * factor
    drive = full[2] * factor
    keep = (1.0 - relax_rate * (6.0 * length_sq + 1.0)) * inside - (2.0 * relax_rate) * drive
    push = (2.0 * relax_rate) * drive
    spread = (relax_rate * length_sq) * inside
    for _ in range(SUBSTEPS):
        pair = damage + pltpu.roll(damage, SZ + 1, 1)
        ring = (
            pltpu.roll(damage, 1, 0)
            + pltpu.roll(damage, RD - 1, 0)
            + pltpu.roll(pair, LW - SZ, 1)
            + pltpu.roll(pair, LW - 1, 1)
        )
        damage = spread * ring + keep * damage + push
    own = pltpu.roll(damage, RD - 4 - H, 0)[0:CX]
    for y in range(CY):
        damage_out[:, y, :] = pltpu.roll(own, LW - (H + y) * SZ - H, 1)[:, :CZ]
    return damage, factor


def make_fields(damage, factor, acc, low, high, has_low, has_high, field_left):
    row = iota((8, LW), 0)
    last = acc[24:32, :]
    low_last = only(has_low, low[24:32, :])
    velocity = []
    for c in range(3):
        at = slice(8 * c, 8 * c + 8)
        first = acc[at, :] + tail_rows(low_last, c)
        velocity.append(first * factor[8:16])
        from_high = only(has_high, high[at, :])
        last = last + jnp.where(row == c, spin0(from_high, c), jnp.where(row == 4 + c, spin0(from_high, 3 + c), 0.0))
    pair = lambda v: jnp.where(row < 4, jnp.broadcast_to(v[16:17], row.shape), jnp.broadcast_to(v[17:18], row.shape))
    last = jnp.where((row == 3) | (row == 7), pair(damage), last * pair(factor))
    whole = jnp.concatenate(velocity + [damage[8:16], last], axis=0)
    whole = pltpu.roll(whole, LW - OFF, 1)[:, :NB]
    turned = [whole, pltpu.roll(whole, NB - 1, 1)]
    for bc in range(4):
        moved = turned[bc & 1]
        if bc >> 1:
            moved = pltpu.roll(moved, NB - SZ, 1)
        for j in range(JB):
            lanes = slice(j * LANE, (j + 1) * LANE)
            for f in range(4):
                field_left[pl.ds(j * FL + 4 * f + bc, 8, stride=16), :] = moved[8 * f : 8 * f + 8, lanes]
            field_left[pl.ds(j * FL + 128 + bc, 8, stride=4), :] = moved[32:40, lanes]


def corners(half, base_ref, field_left, got_ref, bx_ref):
    depth = NB // MX
    tiles = TAIL // MX

    def multiply(*accs):
        for k in range(depth):
            value = jnp.concatenate(
                [field_left[j * FL : (j + 1) * FL, :] for j in range(k * MX // LANE, (k + 1) * MX // LANE)], axis=1)
            high = value.astype(jnp.bfloat16)
            low = (value - high.astype(jnp.float32)).astype(jnp.bfloat16)
            lhs = jnp.concatenate([high, low], axis=0)
            for n in range(tiles):
                at = half * TAIL + n * MX
                pltpu.matmul_push_rhs(onehot(base_ref[:, at : at + MX], k * MX), n // 2 % 2, n % 2)
                pltpu.matmul_acc_lhs(accs[n], lhs, load_staged_rhs=n // 2 % 2)
        for n in range(tiles):
            value = pltpu.matmul_pop(accs[n])
            for j in range(MX // LANE):
                for r in range(0, 2 * FL, 8):
                    got_ref[pl.ds(r * MOST + n * MX // LANE + j, 8, stride=MOST), :] = (
                        value[r : r + 8, j * LANE : (j + 1) * LANE])

    pl.run_scoped(multiply, *[pltpu.ACC(n % 2)((2 * FL, MX), jnp.float32) for n in range(tiles)])
    bx = bx_ref[MOST * half : MOST * half + MOST, :]
    at = [bx == x for x in range(CX + 1)]
    out = [[None] * 8 for _ in range(4)]
    for f in range(4):
        for bc in range(4):
            near = [jnp.zeros((MOST, LANE), jnp.float32)] * 2
            for x in range(EX):
                r = 16 * x + 4 * f + bc
                value = got_ref[r * MOST : (r + 1) * MOST, :] + got_ref[(FL + r) * MOST : (FL + r + 1) * MOST, :]
                if x < EX - 1:
                    near[0] = jnp.where(at[x], value, near[0])
                if x > 0:
                    near[1] = jnp.where(at[x - 1], value, near[1])
            out[f][bc], out[f][4 + bc] = near
    return out


def total(values):
    while len(values) > 1:
        values = [a + b for a, b in zip(values[::2], values[1::2])]
    return values[0]


def move(corner, w, g, p):
    moved = [total([w(k) * corner[i][k] for k in range(8)]) for i in range(3)]
    velgrad = [[total([corner[i][k] * g(j, k) for k in range(8)]) for j in range(3)] for i in range(3)]
    damaged = jnp.maximum(p(23), total([w(k) * corner[3][k] for k in range(8)]))
    deform = [[p(5 + 3 * i + j) for j in range(3)] for i in range(3)]
    stretch = [[(1.0 if i == j else 0.0) + time_step * velgrad[i][j] for j in range(3)] for i in range(3)]
    mapped = [
        stretch[i][0] * deform[0][j] + stretch[i][1] * deform[1][j] + stretch[i][2] * deform[2][j]
        for i in range(3) for j in range(3)
    ]
    return moved + mapped + [damaged]


def finish(late, early):
    moved, m, damaged = late[:3], late[3:12], late[12]
    mapped = [m[0:3], m[3:6], m[6:9]]
    jacobian = (
        mapped[0][0] * (mapped[1][1] * mapped[2][2] - mapped[1][2] * mapped[2][1])
        - mapped[0][1] * (mapped[1][0] * mapped[2][2] - mapped[1][2] * mapped[2][0])
        + mapped[0][2] * (mapped[1][0] * mapped[2][1] - mapped[1][1] * mapped[2][0])
    )
    left = {}
    for i in range(3):
        for j in range(i, 3):
            left[i, j] = mapped[i][0] * mapped[j][0] + mapped[i][1] * mapped[j][1] + mapped[i][2] * mapped[j][2]
            left[j, i] = left[i, j]
    degrade = (1.0 - damaged) ** 2
    swell = bulk_coef * (jacobian - 1.0)
    stress = []
    for i in range(3):
        for j in range(3):
            term = shear_mod * (left[i, j] - (1.0 if i == j else 0.0))
            if i == j:
                term = term + swell
            stress.append(degrade * term)
    energy = 0.5 * shear_mod * (left[0, 0] + left[1, 1] + left[2, 2] - 3.0) + 0.5 * bulk_coef * (jacobian - 1.0) ** 2
    history = jnp.maximum(early[2], energy)
    position = [early[3 + i] + time_step * moved[i] for i in range(3)]
    return early[:2] + moved + m + stress + [damaged, history] + position


def step_kernel(
    sizes, part_in, base_in, weight_in, slope_in, counts, ext, prior_out, damage_out,
    part, base_ref, weight, slope, load_sem, out, sums, acc_d, acc_v, zin, field_left, got, turned, bx_ref,
    ysend_d, yrecv_d, zsend_d, zrecv_d, esend_d, erecv_d, ysend_v, yrecv_v, zsend_v, zrecv_v, esend_v, erecv_v,
    xrecv_d, xrecv_v, early_send, early_recv, late_send, late_recv, send_sem, recv_sem,
):
    names = ("gx", "gy", "gz")
    loads = [
        pltpu.make_async_copy(src, dst, load_sem.at[i])
        for i, (src, dst) in enumerate(
            ((base_in, base_ref), (part_in, part), (weight_in, weight), (slope_in, slope)))
    ]
    for load in loads:
        load.start()
    place = [lax.axis_index(a) for a in names]
    has_low = [i > 0 for i in place]
    has_high = [i < n - 1 for i, n in zip(place, sizes)]
    last = sizes[2]
    following, previous = lax.rem(place[2] + 1, last), lax.rem(place[2] + last - 1, last)
    count = part.shape[1]
    bins = count // BIN

    def has(dy, dz):
        found = None
        for k, d in ((1, dy), (2, dz)):
            if d:
                one = has_high[k] if d > 0 else has_low[k]
                found = one if found is None else found & one
        return found

    def device(dy, dz):
        return {names[k]: place[k] + d for k, d in ((1, dy), (2, dz)) if d}

    barrier = pltpu.get_barrier_semaphore()
    waits = 2
    ahead = [(has_low[0], {"gx": place[0] - 1}), (has_high[0], {"gx": place[0] + 1})]
    for exists, other in ahead + [(has(*d), device(*d)) for d in DIRS]:
        @pl.when(exists)
        def _(other=other):
            pl.semaphore_signal(barrier, inc=1, device_id=other, device_id_type=MESH)
        waits = waits + exists.astype(jnp.int32)
    for other in (following, previous):
        pl.semaphore_signal(barrier, inc=1, device_id={"gz": other}, device_id_type=MESH)

    pending = []

    def copy_to(slot, back, src, dst, other):
        return pltpu.make_async_remote_copy(
            src_ref=src, dst_ref=dst, send_sem=send_sem.at[slot], recv_sem=recv_sem.at[back],
            device_id=other, device_id_type=MESH)

    def bufs(kind):
        if kind:
            return (ysend_v, yrecv_v), (zsend_v, zrecv_v), (esend_v, erecv_v)
        return (ysend_d, yrecv_d), (zsend_d, zrecv_d), (esend_d, erecv_d)

    def message(kind, dy, dz):
        y, z = (dy + 1) // 2, (dz + 1) // 2
        if dz == 0:
            (src, dst), at, back = bufs(kind)[0], y, 1 - y
            base = 0
        elif dy == 0:
            (src, dst), at, back = bufs(kind)[1], z, 1 - z
            base = 2
        else:
            (src, dst), at, back = bufs(kind)[2], 2 * y + z, 2 * (1 - y) + 1 - z
            base = 4
        base += 8 * kind
        return copy_to(base + at, base + back, src.at[at], dst.at[back], device(dy, dz))

    def start(kind, chosen):
        for d in chosen:
            copy = message(kind, *d)
            pending.append((has(*d), copy))
            @pl.when(has(*d))
            def _(copy=copy):
                copy.start()

    def arrive(kind, chosen):
        for dy, dz in chosen:
            copy = message(kind, -dy, -dz)
            @pl.when(has(dy, dz))
            def _(copy=copy):
                copy.wait_recv()

    faces_y = [(-1, 0), (1, 0)]
    others = [d for d in DIRS if d[1] != 0]

    def x_messages(kind):
        acc, recv = (acc_v, xrecv_v) if kind else (acc_d, xrecv_d)
        base = 16 + 2 * kind
        return [copy_to(base + d, base + 1 - d, acc, recv.at[1 - d], {"gx": place[0] + 2 * d - 1}) for d in range(2)]

    def x_start(kind):
        for (exists, _), copy in zip(ahead, x_messages(kind)):
            pending.append((exists, copy))
            @pl.when(exists)
            def _(copy=copy):
                copy.start()

    def x_arrive(kind):
        made = x_messages(kind)
        for exists, copy in ((has_low[0], made[1]), (has_high[0], made[0])):
            @pl.when(exists)
            def _(copy=copy):
                copy.wait_recv()

    def ring(slot, src, dst):
        copy = copy_to(slot, slot, src, dst, {"gz": following})
        copy.start()
        return copy

    for load in loads[:3]:
        load.wait()
    scatter(damage_terms(part, weight), base_ref, sums, acc_d)
    pl.semaphore_wait(barrier, waits)
    pack_y(0, acc_d, ysend_d)
    start(0, faces_y)
    pack_z(0, acc_d, zsend_d, esend_d)
    start(0, others)

    loads[3].wait()
    scatter(velocity_terms(part, weight, slope), base_ref, sums, acc_v)
    pack_y(1, acc_v, ysend_v)
    start(1, faces_y)
    pack_z(1, acc_v, zsend_v, esend_v)
    start(1, others)

    lanes = lambda j: slice(j * LANE, (j + 1) * LANE)
    for j in range(bins):
        for group in range(3):
            turned[(group * bins + j) * 8 : (group * bins + j + 1) * 8, :] = part[8 * group : 8 * group + 8, lanes(j)]
        turned[(3 * bins + j) * 8 : (3 * bins + j) * 8 + 4, :] = part[24:28, lanes(j)]
        turned[(4 * bins + j) * 8 : (4 * bins + j + 1) * 8, :] = weight[:, lanes(j)]
        for group in range(3):
            at = ((5 + group) * bins + j) * 8
            turned[at : at + 8, :] = slope[8 * group : 8 * group + 8, lanes(j)]
        bx_ref[j : j + 1, :] = base_ref[0:1, lanes(j)]

    def dense(half):
        def read(group, s):
            return turned[pl.ds((group * bins + half * MOST) * 8 + s, MOST, stride=8), :]
        return (
            lambda k: read(4, k), lambda j, k: read(5 + j, k), lambda r: read(r // 8, r % 8)
        )

    halves = bins // MOST
    flying = []
    _, _, p = dense(halves - 1)
    early = [p(0), p(1), p(24), p(25), p(26), p(27)]
    early.append(jnp.broadcast_to(counts[0], (8, LANE)).astype(jnp.float32))
    for q, value in enumerate(early):
        early_send[8 * q : 8 * q + 8, :] = value
    flying.append(ring(20, early_send, early_recv))
    ext[:, (MOST + bins) * LANE :] = jnp.zeros((PARTS, TAIL), jnp.float32)

    arrive(0, faces_y)
    land_y(0, acc_d, yrecv_d, has)
    arrive(0, others)
    land_z(0, acc_d, zrecv_d, erecv_d, zin, has)
    x_start(0)
    arrive(1, faces_y)
    land_y(1, acc_v, yrecv_v, has)
    arrive(1, others)
    land_z(1, acc_v, zrecv_v, erecv_v, zin, has)
    x_start(1)
    x_arrive(0)
    full = build_full(acc_d, xrecv_d.at[0], xrecv_d.at[1], has_low[0], has_high[0])
    nodes = [n * c for n, c in zip(sizes, (CX, CY, CZ))]
    damage, factor = relax_all(place, nodes, full, damage_out)
    x_arrive(1)
    make_fields(damage, factor, acc_v, xrecv_v.at[0], xrecv_v.at[1], has_low[0], has_high[0], field_left)

    def store(first, values, gone=None):

        for r, value in enumerate(values):
            if gone is not None:
                value = jnp.where(gone, 0.0, value)
            out[pl.ds(first * SLOT + r, MOST, stride=SLOT), :] = value
        for j in range(first, first + MOST):
            for group in range(up_to(PARTS, 8) // 8):
                rows = min(8, PARTS - 8 * group)
                at = j * SLOT + 8 * group
                ext[8 * group : 8 * group + rows, lanes(j)] = out[at : at + rows, :]

    for half in reversed(range(halves)):
        w, g, p = dense(half)
        late = move(corners(half, base_ref, field_left, got, bx_ref), w, g, p)
        gone = None
        if half == halves - 1:
            for q, value in enumerate(late):
                late_send[8 * q : 8 * q + 8, :] = value
            flying.append(ring(21, late_send, late_recv))
            gone = iota((MOST, LANE), 0) + jnp.broadcast_to(counts[0], (MOST, LANE)) >= MOST
        store((half + 1) * MOST, finish(late, [p(0), p(1), p(24), p(25), p(26), p(27)]), gone)

    for copy in flying:
        copy.wait_recv()
    rows = lambda ref, q: ref[8 * q : 8 * q + 8, :]
    store(0, finish([rows(late_recv, q) for q in range(LATE)], [rows(early_recv, q) for q in range(6)]))
    prior_out[...] = rows(early_recv, 6).astype(jnp.int32)
    for copy in flying:
        copy.wait_send()
    for exists, copy in pending:
        @pl.when(exists)
        def _(copy=copy):
            copy.wait_send()


def place_kernel(ext, prior_ref, damage_in, migrated, damage_out, sem):
    width = migrated.shape[1]
    start = pl.multiple_of((MOST - prior_ref[0, 0]) * BIN, BIN)
    copies = [
        pltpu.make_async_copy(damage_in, damage_out, sem.at[0]),
        pltpu.make_async_copy(ext.at[:, pl.ds(start, width)], migrated, sem.at[1]),
    ]
    for copy in copies:
        copy.start()
    for copy in copies:
        copy.wait()


def per_device(particles, stencil_base, weights, gradients, counts):
    count = particles.shape[1]
    bins = count // BIN
    sizes = tuple(lax.axis_size(a) for a in ("gx", "gy", "gz"))
    vmem = pl.BlockSpec(memory_space=pltpu.VMEM)
    anywhere = pl.BlockSpec(memory_space=pl.ANY)
    f32 = jnp.float32
    two = lambda *shape: [pltpu.VMEM(shape, f32)] * 2
    ext, prior, near_damage = pl.pallas_call(
        functools.partial(step_kernel, sizes),
        name="step",
        out_shape=(
            pltpu.VMEM((PARTS, count + 2 * TAIL), f32),
            pltpu.VMEM((8, LANE), jnp.int32),
            pltpu.VMEM((CX, CY, CZ), f32),
        ),
        in_specs=[anywhere] * 4 + [pl.BlockSpec(memory_space=pltpu.SMEM)],
        out_specs=(vmem,) * 3,
        scratch_shapes=[
            pltpu.VMEM((PARTS, count), f32),
            pltpu.VMEM((3, count), jnp.int32),
            pltpu.VMEM((8, count), f32),
            pltpu.VMEM((24, count), f32),
            pltpu.SemaphoreType.DMA((4,)),
            pltpu.VMEM(((bins + MOST) * SLOT, LANE), f32),
            pltpu.VMEM((JB * LEFT + 8, LANE), f32),
            pltpu.VMEM((ROWS, LW), f32),
            pltpu.VMEM((ROWS, LW), f32),
            pltpu.VMEM((8, LW), f32),
            pltpu.VMEM((JB * FL, LANE), f32),
            pltpu.VMEM((MOST * 2 * FL, LANE), f32),
            pltpu.VMEM((GROUPS * bins * 8, LANE), f32),
            pltpu.VMEM((bins, LANE), jnp.int32),
            *two(2, ROWS, FACE[0]),
            *two(2, 8, ZB - ZA),
            *two(4, 8, FACE[0]),
            *two(2, ROWS, FACE[1]),
            *two(2, 8, ZB - ZA),
            *two(4, 8, FACE[1]),
            *two(2, ROWS, LW),
            *two(EARLY * 8, LANE),
            *two(LATE * 8, LANE),
            pltpu.SemaphoreType.DMA((22,)),
            pltpu.SemaphoreType.DMA((22,)),
        ],
        compiler_params=pltpu.CompilerParams(
            collective_id=0, has_side_effects=True, vmem_limit_bytes=60 * 1024 * 1024
        ),
    )(particles, stencil_base, weights, gradients.reshape(24, count), counts)
    return pl.pallas_call(
        place_kernel,
        name="place",
        out_shape=(
            jax.ShapeDtypeStruct((PARTS, count + TAIL), f32),
            jax.ShapeDtypeStruct((CX, CY, CZ), f32),
        ),
        in_specs=[anywhere, vmem, anywhere],
        out_specs=(anywhere,) * 2,
        scratch_shapes=[pltpu.SemaphoreType.DMA((2,))],
        compiler_params=pltpu.CompilerParams(vmem_limit_bytes=4 * 1024 * 1024),
    )(ext, prior, near_damage)


def solution(mesh):
    return jax.shard_map(
        per_device,
        mesh=mesh,
        in_specs=(
            P(None, ("gx", "gy", "gz")),
            P(None, ("gx", "gy", "gz")),
            P(None, ("gx", "gy", "gz")),
            P(None, None, ("gx", "gy", "gz")),
            P(("gx", "gy", "gz")),
        ),
        out_specs=(P(None, ("gx", "gy", "gz")), P("gx", "gy", "gz")),
        check_vma=False,
    )
```

```python
import functools
import jax
import jax.numpy as jnp
from jax import lax
from jax.experimental import pallas as pl
from jax.experimental.pallas import tpu as pltpu
from jax.sharding import PartitionSpec as P

CX = 8
CY = 16
CZ = 32
NBIN = 16
BIN = 128
SUBSTEPS = 4
MOST = 8

time_step = 0.1
relax_rate = 0.2
length_sq = 0.6
shear_mod = 1.0
bulk_coef = 1.5
mass_floor = 0.5

MESH = pl.DeviceIdType.MESH


def up_to(value, unit):
    return (value + unit - 1) // unit * unit


H = SUBSTEPS + 1
EX, EY, EZ = CX + 2, CY + 2, CZ + 2
SX, SY, SZ = CX + 2 * H, CY + 2 * H, CZ + 2 * H
LANE = 128
MX = 256
LW = up_to(SY * SZ, LANE)
NB = up_to((CY + 1) * SZ + CZ + 2, MX)
JB = NB // LANE
OFF = (H - 1) * SZ + H - 1
KEEP = H + 1
RD = 24
ROWS = 32
LEFT = up_to(EX * 12, 16)
WIDE = {0: KEEP, 1: 2}
FACE = {0: up_to(KEEP * SZ, LANE), 1: up_to(2 * SZ, LANE)}
ZA, ZB = (H - 1) * SZ // LANE * LANE, up_to((H + CY + 1) * SZ, LANE)
FL = EX * 16
TAIL = MOST * BIN
PARTS = 28
SLOT = 32
GROUPS = 8
CHUNKS = 1
EARLY_PART = 4
LATE = 13
EARLY = 7
FOLDS = 3
FY = EY // FOLDS
ZF = up_to(FY * SZ, LANE)
DIRS = [(dy, dz) for dy in (-1, 0, 1) for dz in (-1, 0, 1) if (dy, dz) != (0, 0)]


def iota(shape, axis):
    return lax.broadcasted_iota(jnp.int32, shape, axis)


def take(value, lane0, width):
    a = lane0 // LANE * LANE
    span = up_to(lane0 - a + width, LANE)
    value = value[:, a : a + span]
    shift = (span - (lane0 - a)) % span
    if shift:
        value = pltpu.roll(value, shift, 1)
    value = value[:, : up_to(width, LANE)]
    return jnp.where(iota(value.shape, 1) < width, value, 0.0)


def put_add(ref, lane0, width, value):
    a = lane0 // LANE * LANE
    span = max(up_to(lane0 - a + width, LANE), value.shape[1])
    extra = span - value.shape[1]
    if extra:
        value = jnp.concatenate([value, jnp.zeros((value.shape[0], extra), jnp.float32)], axis=1)
    if lane0 - a:
        value = pltpu.roll(value, lane0 - a, 1)
    ref[:, a : a + span] += value


def spin(value, shift):
    shift = shift % value.shape[1]
    return pltpu.roll(value, shift, 1) if shift else value


def only(has, value):
    return jnp.where(has, value, jnp.zeros_like(value))


def lane_z(rows):
    lane = lax.broadcasted_iota(jnp.int32, (rows, LW), 1).astype(jnp.float32)
    y = jnp.floor((lane + 0.5) * (1.0 / SZ))
    return lane - SZ * y, y


def onehot(base, first):
    shape = (16, base.shape[1])
    flat = jnp.broadcast_to(base[1:2, :] * SZ + base[2:3, :], shape) - iota(shape, 0)
    flat = flat.astype(jnp.int16)
    one, zero = jnp.bfloat16(1), jnp.bfloat16(0)
    return jnp.concatenate([jnp.where(flat == jnp.int16(first + r), one, zero) for r in range(0, MX, 16)], axis=0)


def split(value):
    high = value.astype(jnp.bfloat16)
    return high, (value - high.astype(jnp.float32)).astype(jnp.bfloat16)


def bin_steps(base):
    count = base.shape[1]
    bx = jnp.broadcast_to(base[0:1, :], (16, count))
    steps = [bx - (iota((16, count), 0) >= cut).astype(jnp.int32) for cut in (12, 8, 4)]
    return [v.astype(jnp.float32).astype(jnp.bfloat16) for v in steps]


def make_left(terms, steps):
    count = terms[0].shape[1]
    low = iota((8, count), 0) < 4
    turned = [pltpu.roll(t, 4, 0) for t in terms]
    patterns = []
    for a in range(2):
        def join(p, q):
            return jnp.where(low, turned[p] if a else terms[p], terms[q] if a else turned[q])
        parts = [join(0, 1), join(2, 0), join(1, 2)]
        patterns.append([split(jnp.concatenate([parts[i], parts[j]], axis=0)) for i, j in ((0, 1), (2, 0), (1, 2))])
    zero = jnp.bfloat16(0)
    rows = [[], []]
    for t in range(LEFT // 16):
        k = t % 3
        x = 16 * t // 12
        near, far = steps[k] == jnp.bfloat16(x), steps[k] == jnp.bfloat16(x - 1)
        for part in range(2):
            rows[part].append(jnp.where(near, patterns[0][k][part], jnp.where(far, patterns[1][k][part], zero)))
    return [jnp.concatenate(part, axis=0) for part in rows]


def scatter_tiles(terms, base_ref, accs, some, arrived=None):
    tiles = NB // MX
    for k in some:
        if arrived is not None:
            arrived(k)
        lanes = slice(k * MX, (k + 1) * MX)
        base = base_ref[:, lanes]
        left = make_left(terms(lanes), bin_steps(base))
        for n in range(tiles):
            extra = n == tiles - 1 and tiles % 2
            m = k % 2 if extra else n % 2
            acc = accs[n + m if extra else n]
            pltpu.matmul_push_rhs(onehot(base, n * MX), int(n >= 2), m, transpose=True)
            pltpu.matmul_acc_lhs(acc, left[0], load_staged_rhs=int(n >= 2))
            pltpu.matmul_acc_lhs(acc, left[1])


def scatter_pop(accs, sums):
    tiles = NB // MX
    for n in range(tiles):
        value = pltpu.matmul_pop(accs[n])
        if n == tiles - 1 and tiles % 2:
            value = value + pltpu.matmul_pop(accs[n + 1])
        for j in range(MX // LANE):
            at = (n * MX // LANE + j) * LEFT
            sums[at : at + LEFT, :] = value[:, j * LANE : (j + 1) * LANE]


def add_corners(sums, acc):
    pieces = []
    for bc in range(4):
        tiles = []
        for j in range(JB):
            base = j * LEFT + bc
            column = [sums[pl.ds(base + 4 * c, 8, stride=12), :] for c in range(3)]
            tiles.append(jnp.concatenate(column + [sums[pl.ds(base + 96, 8, stride=4), :]], axis=0))
        pieces.append(jnp.concatenate(tiles, axis=1))
    near = [pieces[2 * b] + pltpu.roll(pieces[2 * b + 1], 1, 1) for b in range(2)]
    total = near[0] + pltpu.roll(near[1], SZ, 1)
    total = jnp.concatenate([total, jnp.zeros((ROWS, LW - NB), jnp.float32)], axis=1)
    acc[...] = pltpu.roll(total, OFF, 1)


def damage_terms(part, weight):
    def terms(lanes):
        share = part[0:1, lanes] * weight[:, lanes]
        return [share, share * part[23:24, lanes], share * part[24:25, lanes]]
    return terms


def velocity_terms(part, weight, slope):
    def terms(lanes):
        mass = part[0:1, lanes]
        scale = -time_step * part[1:2, lanes]
        out = []
        for i in range(3):
            term = (mass * part[2 + i : 3 + i, lanes]) * weight[:, lanes]
            for j in range(3):
                row = 14 + 3 * i + j
                term = term + (scale * part[row : row + 1, lanes]) * slope[8 * j : 8 * j + 8, lanes]
            out.append(term)
        return out
    return terms


def send_spots(kind):
    if kind:
        return ((H - 1) * SZ, (H - 1 + CY) * SZ), (H - 1, H - 1 + CZ)
    return ((H - 1) * SZ, CY * SZ), (H - 1, CZ)


def land_spots(kind):
    if kind:
        return ((H - 1) * SZ, (H - 1 + CY) * SZ), (H - 1, H - 1 + CZ)
    return (0, (SY - KEEP) * SZ), (0, SZ - KEEP)


def pack_y(kind, acc, ysend):
    for d, lane0 in enumerate(send_spots(kind)[0]):
        ysend[d] = take(acc[...], lane0, WIDE[kind] * SZ)


def pack_z(kind, acc, zsend, esend):
    wide = WIDE[kind]
    y_at, z_at = send_spots(kind)
    z, _ = lane_z(8)
    for d, z0 in enumerate(z_at):
        out = jnp.zeros((8, LW), jnp.float32)
        for s in range(4):
            value = spin(acc[8 * s : 8 * s + 8, :], s * wide - z0)
            out = jnp.where((z >= s * wide) & (z < (s + 1) * wide), value, out)
        if kind:
            zsend[d] = sum(spin(take(out, (H - 1 + q * FY) * SZ, FY * SZ), 4 * wide * q) for q in range(FOLDS))
        else:
            zsend[d] = out[:, ZA:ZB]
        for e, lane0 in enumerate(y_at):
            esend[2 * e + d] = take(out, lane0, wide * SZ)


def land_y(kind, acc, yrecv, has):
    for d, lane0 in enumerate(land_spots(kind)[0]):
        put_add(acc, lane0, WIDE[kind] * SZ, only(has(2 * d - 1, 0), yrecv[d]))


def land_z(kind, acc, zrecv, erecv, zin, has):
    wide = WIDE[kind]
    y_at, z_at = land_spots(kind)
    z, _ = lane_z(8)
    for d, z0 in enumerate(z_at):
        if kind:
            zin[...] = jnp.zeros((8, LW), jnp.float32)
            folded = only(has(0, 2 * d - 1), zrecv[d])
            short, lane = z[:, :ZF], iota((8, ZF), 1)
            for q in range(FOLDS):
                z1 = 4 * wide * q
                mine = (short >= z1) & (short < z1 + 4 * wide) & (lane < FY * SZ)
                put_add(zin, (H - 1 + q * FY) * SZ, FY * SZ, spin(jnp.where(mine, folded, 0.0), -z1))
        else:
            zin[:, :ZA] = jnp.zeros((8, ZA), jnp.float32)
            zin[:, ZB:] = jnp.zeros((8, LW - ZB), jnp.float32)
            zin[:, ZA:ZB] = only(has(0, 2 * d - 1), zrecv[d])
        for e, lane0 in enumerate(y_at):
            put_add(zin, lane0, wide * SZ, only(has(2 * e - 1, 2 * d - 1), erecv[2 * e + d]))
        whole = zin[...]
        for s in range(4):
            value = jnp.where((z >= s * wide) & (z < (s + 1) * wide), whole, 0.0)
            acc[8 * s : 8 * s + 8, :] += spin(value, z0 - s * wide)


def tail_rows(last, c):
    row = iota(last.shape, 0)
    first = spin0(last, -c)
    second = spin0(last, -c - 2)
    return jnp.where(row == 0, first, jnp.where(row == 1, second, 0.0))


def spin0(value, shift):
    shift = shift % value.shape[0]
    return pltpu.roll(value, shift, 0) if shift else value


def build_full(acc, low, high, has_low, has_high):
    row = iota((8, LW), 0)
    own_last, low_last = acc[24:32, :], low[24:32, :]
    out = []
    for c in range(3):
        at = slice(8 * c, 8 * c + 8)
        first = only(has_low, jnp.where(row >= 4, low[at, :], 0.0))
        middle = acc[at, :] + only(has_low, tail_rows(low_last, c))
        last = tail_rows(own_last, c) + only(has_high, jnp.where(row < 6, high[at, :], 0.0))
        out.append(jnp.concatenate([first, middle, last], axis=0))
    return out


def relax_all(place, nodes, full, line):
    ix, iy, iz = place
    z, y = lane_z(1)
    gz = z - H + (iz * CZ).astype(jnp.float32)
    gy = y - H + (iy * CY).astype(jnp.float32)
    flat_in = (gz >= 0) & (gz < nodes[2]) & (gy >= 0) & (gy < nodes[1]) & (y < SY)
    row = lax.broadcasted_iota(jnp.int32, (RD, 1), 0)
    gx = row - 4 - H + ix * CX
    row_in = (gx >= 0) & (gx < nodes[0]) & (row >= 4) & (row < 4 + SX)
    inside = row_in.astype(jnp.float32) * flat_in.astype(jnp.float32)
    mass = jnp.maximum(full[0], mass_floor)
    factor = inside / mass
    damage = full[1] * factor
    drive = full[2] * factor
    keep = (1.0 - relax_rate * (6.0 * length_sq + 1.0)) * inside - (2.0 * relax_rate) * drive
    push = (2.0 * relax_rate) * drive
    spread = (relax_rate * length_sq) * inside
    tiles = LW // LANE
    line[0:8, :] = jnp.zeros((8, LANE), jnp.float32)
    line[8 + tiles * RD :, :] = jnp.zeros((8, LANE), jnp.float32)
    for _ in range(SUBSTEPS):
        for j in range(tiles):
            line[8 + j * RD : 8 + (j + 1) * RD, :] = damage[:, j * LANE : (j + 1) * LANE]
        pair = damage + pltpu.roll(damage, SZ + 1, 1)
        along = jnp.concatenate(
            [line[pl.ds(7 + j * RD, RD), :] + line[pl.ds(9 + j * RD, RD), :] for j in range(tiles)], axis=1)
        ring = along + pltpu.roll(pair, LW - SZ, 1) + pltpu.roll(pair, LW - 1, 1)
        damage = spread * ring + keep * damage + push
    for j in range(tiles):
        line[8 + j * RD : 8 + (j + 1) * RD, :] = damage[:, j * LANE : (j + 1) * LANE]
    return damage, factor


def show_damage(line, damage_out):
    own = jnp.concatenate([line[pl.ds(8 + j * RD + 4 + H, CX), :] for j in range(LW // LANE)], axis=1)
    for y in range(CY):
        damage_out[:, y, :] = pltpu.roll(own, LW - (H + y) * SZ - H, 1)[:, :CZ]


def make_fields(damage, factor, acc, low, high, has_low, has_high, field_left):
    row = iota((8, LW), 0)
    last = acc[24:32, :]
    low_last = only(has_low, low[24:32, :])
    velocity = []
    for c in range(3):
        at = slice(8 * c, 8 * c + 8)
        first = acc[at, :] + tail_rows(low_last, c)
        velocity.append(first * factor[8:16])
        from_high = only(has_high, high[at, :])
        last = last + jnp.where(row == c, spin0(from_high, c), jnp.where(row == 3 + c, spin0(from_high, 2 + c), 0.0))
    pair = lambda v: jnp.where(row < 4, jnp.broadcast_to(v[16:17], row.shape), jnp.broadcast_to(v[17:18], row.shape))
    last = jnp.where(row < 3, last, pltpu.roll(last, 1, 0))
    last = jnp.where((row == 3) | (row == 7), pair(damage), last * pair(factor))
    whole = jnp.concatenate(velocity + [damage[8:16], last], axis=0)
    whole = pltpu.roll(whole, LW - OFF, 1)[:, :NB]
    turned = [whole, pltpu.roll(whole, NB - 1, 1)]
    for bc in range(4):
        moved = turned[bc & 1]
        if bc >> 1:
            moved = pltpu.roll(moved, NB - SZ, 1)
        for j in range(JB):
            lanes = slice(j * LANE, (j + 1) * LANE)
            for f in range(4):
                field_left[pl.ds(j * FL + 4 * f + bc, 8, stride=16), :] = moved[8 * f : 8 * f + 8, lanes]
            field_left[pl.ds(j * FL + 128 + bc, 8, stride=4), :] = moved[32:40, lanes]


def corners(half, base_ref, field_left, got_ref, bx_ref):
    depth = NB // MX
    tiles = TAIL // MX

    def multiply(*accs):
        for k in range(depth):
            value = jnp.concatenate(
                [field_left[j * FL : (j + 1) * FL, :] for j in range(k * MX // LANE, (k + 1) * MX // LANE)], axis=1)
            high, low = split(value)
            for n in range(tiles):
                at = half * TAIL + n * MX
                pltpu.matmul_push_rhs(onehot(base_ref[:, at : at + MX], k * MX), n // 2 % 2, n % 2)
                pltpu.matmul_acc_lhs(accs[n], high, load_staged_rhs=n // 2 % 2)
                pltpu.matmul_acc_lhs(accs[n], low)
        for n in range(tiles):
            value = pltpu.matmul_pop(accs[n])
            for j in range(MX // LANE):
                for r in range(0, FL, 8):
                    got_ref[pl.ds(r * MOST + n * MX // LANE + j, 8, stride=MOST), :] = (
                        value[r : r + 8, j * LANE : (j + 1) * LANE])

    pl.run_scoped(multiply, *[pltpu.ACC(n % 2)((FL, MX), jnp.float32) for n in range(tiles)])
    bx = bx_ref[MOST * half : MOST * half + MOST, :]
    at = [bx == x for x in range(CX + 1)]
    out = [[None] * 8 for _ in range(4)]
    for f in range(4):
        for bc in range(4):
            near = [jnp.zeros((MOST, LANE), jnp.float32)] * 2
            for x in range(EX):
                r = 16 * x + 4 * f + bc
                value = got_ref[r * MOST : (r + 1) * MOST, :]
                if x < EX - 1:
                    near[0] = jnp.where(at[x], value, near[0])
                if x > 0:
                    near[1] = jnp.where(at[x - 1], value, near[1])
            out[f][bc], out[f][4 + bc] = near
    return out


def total(values):
    while len(values) > 1:
        values = [a + b for a, b in zip(values[::2], values[1::2])]
    return values[0]


def move(corner, w, g, p):
    moved = [total([w(k) * corner[i][k] for k in range(8)]) for i in range(3)]
    velgrad = [[total([corner[i][k] * g(j, k) for k in range(8)]) for j in range(3)] for i in range(3)]
    damaged = jnp.maximum(p(23), total([w(k) * corner[3][k] for k in range(8)]))
    deform = [[p(5 + 3 * i + j) for j in range(3)] for i in range(3)]
    stretch = [[(1.0 if i == j else 0.0) + time_step * velgrad[i][j] for j in range(3)] for i in range(3)]
    mapped = [
        stretch[i][0] * deform[0][j] + stretch[i][1] * deform[1][j] + stretch[i][2] * deform[2][j]
        for i in range(3) for j in range(3)
    ]
    return moved + mapped + [damaged]


def finish(late, early):
    moved, m, damaged = late[:3], late[3:12], late[12]
    mapped = [m[0:3], m[3:6], m[6:9]]
    jacobian = (
        mapped[0][0] * (mapped[1][1] * mapped[2][2] - mapped[1][2] * mapped[2][1])
        - mapped[0][1] * (mapped[1][0] * mapped[2][2] - mapped[1][2] * mapped[2][0])
        + mapped[0][2] * (mapped[1][0] * mapped[2][1] - mapped[1][1] * mapped[2][0])
    )
    left = {}
    for i in range(3):
        for j in range(i, 3):
            left[i, j] = mapped[i][0] * mapped[j][0] + mapped[i][1] * mapped[j][1] + mapped[i][2] * mapped[j][2]
            left[j, i] = left[i, j]
    degrade = (1.0 - damaged) ** 2
    swell = bulk_coef * (jacobian - 1.0)
    stress = []
    for i in range(3):
        for j in range(3):
            term = shear_mod * (left[i, j] - (1.0 if i == j else 0.0))
            if i == j:
                term = term + swell
            stress.append(degrade * term)
    energy = 0.5 * shear_mod * (left[0, 0] + left[1, 1] + left[2, 2] - 3.0) + 0.5 * bulk_coef * (jacobian - 1.0) ** 2
    history = jnp.maximum(early[2], energy)
    position = [early[3 + i] + time_step * moved[i] for i in range(3)]
    return early[:2] + moved + m + stress + [damaged, history] + position


def step_kernel(sizes, *refs):
    slots = up_to(NB // MX, 2)
    kinds = [pltpu.ACC(n % 2)((LEFT, MX), jnp.float32) for _ in range(2) for n in range(slots)]
    pl.run_scoped(lambda *accs: step_body(accs, sizes, *refs), *kinds)


def step_body(
    accs, sizes, part_in, base_in, weight_in, slope_in, counts, ext, prior_out, damage_out,
    part, base_ref, weight, slope, load_sem, out, sums, acc_d, acc_v, zin, line, field_left, got, turned, bx_ref,
    ysend_d, yrecv_d, zsend_d, zrecv_d, esend_d, erecv_d, ysend_v, yrecv_v, zsend_v, zrecv_v, esend_v, erecv_v,
    xrecv_d, xrecv_v, early_send, early_recv, late_send, late_recv, send_sem, recv_sem,
):
    names = ("gx", "gy", "gz")
    count = part.shape[1]
    chunk = count // CHUNKS
    loads = []
    for c in range(CHUNKS):
        lanes = pl.ds(c * chunk, chunk)
        loads.append([
            pltpu.make_async_copy(src.at[:, lanes], dst.at[:, lanes], load_sem.at[4 * c + i])
            for i, (src, dst) in enumerate(
                ((base_in, base_ref), (part_in, part), (weight_in, weight), (slope_in, slope)))
        ])
    for load in loads[0]:
        load.start()
    place = [lax.axis_index(a) for a in names]
    has_low = [i > 0 for i in place]
    has_high = [i < n - 1 for i, n in zip(place, sizes)]
    last = sizes[2]
    following, previous = lax.rem(place[2] + 1, last), lax.rem(place[2] + last - 1, last)
    bins = count // BIN

    def has(dy, dz):
        found = None
        for k, d in ((1, dy), (2, dz)):
            if d:
                one = has_high[k] if d > 0 else has_low[k]
                found = one if found is None else found & one
        return found

    def device(dy, dz):
        return {names[k]: place[k] + d for k, d in ((1, dy), (2, dz)) if d}

    barrier = pltpu.get_barrier_semaphore()
    waits = 2
    ahead = [(has_low[0], {"gx": place[0] - 1}), (has_high[0], {"gx": place[0] + 1})]
    for exists, other in ahead + [(has(*d), device(*d)) for d in DIRS]:
        @pl.when(exists)
        def _(other=other):
            pl.semaphore_signal(barrier, inc=1, device_id=other, device_id_type=MESH)
        waits = waits + exists.astype(jnp.int32)
    for other in (following, previous):
        pl.semaphore_signal(barrier, inc=1, device_id={"gz": other}, device_id_type=MESH)

    pending = []

    def copy_to(slot, back, src, dst, other):
        return pltpu.make_async_remote_copy(
            src_ref=src, dst_ref=dst, send_sem=send_sem.at[slot], recv_sem=recv_sem.at[back],
            device_id=other, device_id_type=MESH)

    def bufs(kind):
        if kind:
            return (ysend_v, yrecv_v), (zsend_v, zrecv_v), (esend_v, erecv_v)
        return (ysend_d, yrecv_d), (zsend_d, zrecv_d), (esend_d, erecv_d)

    def message(kind, dy, dz):
        y, z = (dy + 1) // 2, (dz + 1) // 2
        if dz == 0:
            (src, dst), at, back = bufs(kind)[0], y, 1 - y
            base = 0
        elif dy == 0:
            (src, dst), at, back = bufs(kind)[1], z, 1 - z
            base = 2
        else:
            (src, dst), at, back = bufs(kind)[2], 2 * y + z, 2 * (1 - y) + 1 - z
            base = 4
        base += 8 * kind
        return copy_to(base + at, base + back, src.at[at], dst.at[back], device(dy, dz))

    def start(kind, chosen):
        for d in chosen:
            copy = message(kind, *d)
            pending.append((has(*d), copy))
            @pl.when(has(*d))
            def _(copy=copy):
                copy.start()

    def arrive(kind, chosen):
        for dy, dz in chosen:
            copy = message(kind, -dy, -dz)
            @pl.when(has(dy, dz))
            def _(copy=copy):
                copy.wait_recv()

    faces_y = [(-1, 0), (1, 0)]
    others = [d for d in DIRS if d[1] != 0]

    def x_messages(kind):
        acc, recv = (acc_v, xrecv_v) if kind else (acc_d, xrecv_d)
        base = 16 + 2 * kind
        return [copy_to(base + d, base + 1 - d, acc, recv.at[1 - d], {"gx": place[0] + 2 * d - 1}) for d in range(2)]

    def x_start(kind):
        for (exists, _), copy in zip(ahead, x_messages(kind)):
            pending.append((exists, copy))
            @pl.when(exists)
            def _(copy=copy):
                copy.start()

    def x_arrive(kind):
        made = x_messages(kind)
        for exists, copy in ((has_low[0], made[1]), (has_high[0], made[0])):
            @pl.when(exists)
            def _(copy=copy):
                copy.wait_recv()

    def ring(slot, src, dst):
        copy = copy_to(slot, slot, src, dst, {"gz": following})
        copy.start()
        return copy

    for group in loads[1:]:
        for load in group:
            load.start()

    def arrived(k):
        if k * MX % chunk == 0:
            for load in loads[k * MX // chunk]:
                load.wait()

    slots = up_to(NB // MX, 2)
    spans = count // MX
    early_spans = spans * EARLY_PART // 8

    scatter_tiles(damage_terms(part, weight), base_ref, accs[:slots], range(spans), arrived)
    scatter_pop(accs[:slots], sums.at[0])
    terms = velocity_terms(part, weight, slope)
    scatter_tiles(terms, base_ref, accs[slots:], range(early_spans))
    add_corners(sums.at[0], acc_d)
    pack_z(0, acc_d, zsend_d, esend_d)
    pack_y(0, acc_d, ysend_d)
    pl.semaphore_wait(barrier, waits)
    start(0, others)
    start(0, faces_y)
    scatter_tiles(terms, base_ref, accs[slots:], range(early_spans, spans))
    scatter_pop(accs[slots:], sums.at[1])
    add_corners(sums.at[1], acc_v)
    pack_z(1, acc_v, zsend_v, esend_v)
    start(1, others)
    pack_y(1, acc_v, ysend_v)
    start(1, faces_y)

    lanes = lambda j: slice(j * LANE, (j + 1) * LANE)
    for j in range(bins):
        for group in range(3):
            turned[(group * bins + j) * 8 : (group * bins + j + 1) * 8, :] = part[8 * group : 8 * group + 8, lanes(j)]
        turned[(3 * bins + j) * 8 : (3 * bins + j) * 8 + 4, :] = part[24:28, lanes(j)]
        turned[(4 * bins + j) * 8 : (4 * bins + j + 1) * 8, :] = weight[:, lanes(j)]
        for group in range(3):
            at = ((5 + group) * bins + j) * 8
            turned[at : at + 8, :] = slope[8 * group : 8 * group + 8, lanes(j)]
        bx_ref[j : j + 1, :] = base_ref[0:1, lanes(j)]

    def dense(half):
        def read(group, s):
            return turned[pl.ds((group * bins + half * MOST) * 8 + s, MOST, stride=8), :]
        return (
            lambda k: read(4, k), lambda j, k: read(5 + j, k), lambda r: read(r // 8, r % 8)
        )

    halves = bins // MOST
    flying = []
    _, _, p = dense(halves - 1)
    early = [p(0), p(1), p(24), p(25), p(26), p(27)]
    early.append(jnp.broadcast_to(counts[0], (8, LANE)).astype(jnp.float32))
    for q, value in enumerate(early):
        early_send[8 * q : 8 * q + 8, :] = value
    flying.append(ring(20, early_send, early_recv))
    ext[:, (MOST + bins) * LANE :] = jnp.zeros((PARTS, TAIL), jnp.float32)

    arrive(0, faces_y)
    land_y(0, acc_d, yrecv_d, has)
    arrive(0, others)
    land_z(0, acc_d, zrecv_d, erecv_d, zin, has)
    x_start(0)
    arrive(1, faces_y)
    land_y(1, acc_v, yrecv_v, has)
    arrive(1, others)
    land_z(1, acc_v, zrecv_v, erecv_v, zin, has)
    x_start(1)
    x_arrive(0)
    full = build_full(acc_d, xrecv_d.at[0], xrecv_d.at[1], has_low[0], has_high[0])
    nodes = [n * c for n, c in zip(sizes, (CX, CY, CZ))]
    damage, factor = relax_all(place, nodes, full, line)
    x_arrive(1)
    make_fields(damage, factor, acc_v, xrecv_v.at[0], xrecv_v.at[1], has_low[0], has_high[0], field_left)

    def store(first, values, gone=None):

        for r, value in enumerate(values):
            if gone is not None:
                value = jnp.where(gone, 0.0, value)
            out[pl.ds(first * SLOT + r, MOST, stride=SLOT), :] = value
        for j in range(first, first + MOST):
            for group in range(up_to(PARTS, 8) // 8):
                rows = min(8, PARTS - 8 * group)
                at = j * SLOT + 8 * group
                ext[8 * group : 8 * group + rows, lanes(j)] = out[at : at + rows, :]

    for half in reversed(range(halves)):
        w, g, p = dense(half)
        late = move(corners(half, base_ref, field_left, got, bx_ref), w, g, p)
        gone = None
        if half == halves - 1:
            for q, value in enumerate(late):
                late_send[8 * q : 8 * q + 8, :] = value
            flying.append(ring(21, late_send, late_recv))
            show_damage(line, damage_out)
            gone = iota((MOST, LANE), 0) + jnp.broadcast_to(counts[0], (MOST, LANE)) >= MOST
        store((half + 1) * MOST, finish(late, [p(0), p(1), p(24), p(25), p(26), p(27)]), gone)

    for copy in flying:
        copy.wait_recv()
    rows = lambda ref, q: ref[8 * q : 8 * q + 8, :]
    store(0, finish([rows(late_recv, q) for q in range(LATE)], [rows(early_recv, q) for q in range(6)]))
    prior_out[...] = rows(early_recv, 6).astype(jnp.int32)
    for copy in flying:
        copy.wait_send()
    for exists, copy in pending:
        @pl.when(exists)
        def _(copy=copy):
            copy.wait_send()


def place_kernel(ext, prior_ref, damage_in, migrated, damage_out, sem):
    width = migrated.shape[1]
    start = pl.multiple_of((MOST - prior_ref[0, 0]) * BIN, BIN)
    copies = [
        pltpu.make_async_copy(damage_in, damage_out, sem.at[0]),
        pltpu.make_async_copy(ext.at[:, pl.ds(start, width)], migrated, sem.at[1]),
    ]
    for copy in copies:
        copy.start()
    for copy in copies:
        copy.wait()


def per_device(particles, stencil_base, weights, gradients, counts):
    count = particles.shape[1]
    bins = count // BIN
    sizes = tuple(lax.axis_size(a) for a in ("gx", "gy", "gz"))
    vmem = pl.BlockSpec(memory_space=pltpu.VMEM)
    anywhere = pl.BlockSpec(memory_space=pl.ANY)
    f32 = jnp.float32
    two = lambda *shape: [pltpu.VMEM(shape, f32)] * 2
    ext, prior, near_damage = pl.pallas_call(
        functools.partial(step_kernel, sizes),
        name="step",
        out_shape=(
            pltpu.VMEM((PARTS, count + 2 * TAIL), f32),
            pltpu.VMEM((8, LANE), jnp.int32),
            pltpu.VMEM((CX, CY, CZ), f32),
        ),
        in_specs=[anywhere] * 4 + [pl.BlockSpec(memory_space=pltpu.SMEM)],
        out_specs=(vmem,) * 3,
        scratch_shapes=[
            pltpu.VMEM((PARTS, count), f32),
            pltpu.VMEM((3, count), jnp.int32),
            pltpu.VMEM((8, count), f32),
            pltpu.VMEM((24, count), f32),
            pltpu.SemaphoreType.DMA((4 * CHUNKS,)),
            pltpu.VMEM(((bins + MOST) * SLOT, LANE), f32),
            pltpu.VMEM((2, JB * LEFT, LANE), f32),
            pltpu.VMEM((ROWS, LW), f32),
            pltpu.VMEM((ROWS, LW), f32),
            pltpu.VMEM((8, LW), f32),
            pltpu.VMEM((16 + LW // LANE * RD, LANE), f32),
            pltpu.VMEM((JB * FL, LANE), f32),
            pltpu.VMEM((MOST * FL, LANE), f32),
            pltpu.VMEM((GROUPS * bins * 8, LANE), f32),
            pltpu.VMEM((bins, LANE), jnp.int32),
            *two(2, ROWS, FACE[0]),
            *two(2, 8, ZB - ZA),
            *two(4, 8, FACE[0]),
            *two(2, ROWS, FACE[1]),
            *two(2, 8, ZF),
            *two(4, 8, FACE[1]),
            *two(2, ROWS, LW),
            *two(EARLY * 8, LANE),
            *two(LATE * 8, LANE),
            pltpu.SemaphoreType.DMA((22,)),
            pltpu.SemaphoreType.DMA((22,)),
        ],
        compiler_params=pltpu.CompilerParams(
            collective_id=0, has_side_effects=True, vmem_limit_bytes=60 * 1024 * 1024
        ),
    )(particles, stencil_base, weights, gradients.reshape(24, count), counts)
    return pl.pallas_call(
        place_kernel,
        name="place",
        out_shape=(
            jax.ShapeDtypeStruct((PARTS, count + TAIL), f32),
            jax.ShapeDtypeStruct((CX, CY, CZ), f32),
        ),
        in_specs=[anywhere, vmem, anywhere],
        out_specs=(anywhere,) * 2,
        scratch_shapes=[pltpu.SemaphoreType.DMA((2,))],
        compiler_params=pltpu.CompilerParams(vmem_limit_bytes=4 * 1024 * 1024),
    )(ext, prior, near_damage)


def solution(mesh):
    return jax.shard_map(
        per_device,
        mesh=mesh,
        in_specs=(
            P(None, ("gx", "gy", "gz")),
            P(None, ("gx", "gy", "gz")),
            P(None, ("gx", "gy", "gz")),
            P(None, None, ("gx", "gy", "gz")),
            P(("gx", "gy", "gz")),
        ),
        out_specs=(P(None, ("gx", "gy", "gz")), P("gx", "gy", "gz")),
        check_vma=False,
    )
```

```python
import functools
import jax
import jax.numpy as jnp
from jax import lax
from jax.experimental import pallas as pl
from jax.experimental.pallas import tpu as pltpu
from jax.sharding import PartitionSpec as P

CX = 8
CY = 16
CZ = 32
NBIN = 16
BIN = 128
SUBSTEPS = 4
MOST = 8

time_step = 0.1
relax_rate = 0.2
length_sq = 0.6
shear_mod = 1.0
bulk_coef = 1.5
mass_floor = 0.5

MESH = pl.DeviceIdType.MESH


def up_to(value, unit):
    return (value + unit - 1) // unit * unit


H = SUBSTEPS + 1
EX, EY, EZ = CX + 2, CY + 2, CZ + 2
SX, SY, SZ = CX + 2 * H, CY + 2 * H, CZ + 2 * H
LANE = 128
MX = 256
LW = up_to(SY * SZ, LANE)
NB = up_to((CY + 1) * SZ + CZ + 2, MX)
JB = NB // LANE
OFF = (H - 1) * SZ + H - 1
KEEP = H + 1
RD = 24
ROWS = 32
LEFT = up_to(EX * 12, 16)
WIDE = {0: KEEP, 1: 2}
FACE = {0: up_to(KEEP * SZ, LANE), 1: up_to(2 * SZ, LANE)}
ZA, ZB = (H - 1) * SZ // LANE * LANE, up_to((H + CY + 1) * SZ, LANE)
FL = EX * 16
TAIL = MOST * BIN
PARTS = 28
SLOT = 32
GROUPS = 8
CHUNKS = 1
EARLY_PART = 8
LATE = 13
EARLY = 7
FOLDS = 3
FY = EY // FOLDS
ZF = up_to(FY * SZ, LANE)
DIRS = [(dy, dz) for dy in (-1, 0, 1) for dz in (-1, 0, 1) if (dy, dz) != (0, 0)]


def iota(shape, axis):
    return lax.broadcasted_iota(jnp.int32, shape, axis)


def take(value, lane0, width):
    a = lane0 // LANE * LANE
    span = up_to(lane0 - a + width, LANE)
    value = value[:, a : a + span]
    shift = (span - (lane0 - a)) % span
    if shift:
        value = pltpu.roll(value, shift, 1)
    value = value[:, : up_to(width, LANE)]
    return jnp.where(iota(value.shape, 1) < width, value, 0.0)


def put_add(ref, lane0, width, value):
    a = lane0 // LANE * LANE
    span = max(up_to(lane0 - a + width, LANE), value.shape[1])
    extra = span - value.shape[1]
    if extra:
        value = jnp.concatenate([value, jnp.zeros((value.shape[0], extra), jnp.float32)], axis=1)
    if lane0 - a:
        value = pltpu.roll(value, lane0 - a, 1)
    ref[:, a : a + span] += value


def spin(value, shift):
    shift = shift % value.shape[1]
    return pltpu.roll(value, shift, 1) if shift else value


def only(has, value):
    return jnp.where(has, value, jnp.zeros_like(value))


def lane_z(rows):
    lane = lax.broadcasted_iota(jnp.int32, (rows, LW), 1).astype(jnp.float32)
    y = jnp.floor((lane + 0.5) * (1.0 / SZ))
    return lane - SZ * y, y


def onehot(base, first):
    shape = (16, base.shape[1])
    flat = jnp.broadcast_to(base[1:2, :] * SZ + base[2:3, :], shape) - iota(shape, 0)
    flat = flat.astype(jnp.int16)
    one, zero = jnp.bfloat16(1), jnp.bfloat16(0)
    return jnp.concatenate([jnp.where(flat == jnp.int16(first + r), one, zero) for r in range(0, MX, 16)], axis=0)


def split(value):
    high = value.astype(jnp.bfloat16)
    return high, (value - high.astype(jnp.float32)).astype(jnp.bfloat16)


def bin_steps(base):
    count = base.shape[1]
    bx = jnp.broadcast_to(base[0:1, :], (16, count))
    steps = [bx - (iota((16, count), 0) >= cut).astype(jnp.int32) for cut in (12, 8, 4)]
    return [v.astype(jnp.float32).astype(jnp.bfloat16) for v in steps]


def make_left(terms, steps):
    count = terms[0].shape[1]
    low = iota((8, count), 0) < 4
    turned = [pltpu.roll(t, 4, 0) for t in terms]
    patterns = []
    for a in range(2):
        def join(p, q):
            return jnp.where(low, turned[p] if a else terms[p], terms[q] if a else turned[q])
        parts = [join(0, 1), join(2, 0), join(1, 2)]
        patterns.append([split(jnp.concatenate([parts[i], parts[j]], axis=0)) for i, j in ((0, 1), (2, 0), (1, 2))])
    zero = jnp.bfloat16(0)
    rows = [[], []]
    for t in range(LEFT // 16):
        k = t % 3
        x = 16 * t // 12
        near, far = steps[k] == jnp.bfloat16(x), steps[k] == jnp.bfloat16(x - 1)
        for part in range(2):
            rows[part].append(jnp.where(near, patterns[0][k][part], jnp.where(far, patterns[1][k][part], zero)))
    return [jnp.concatenate(part, axis=0) for part in rows]


def scatter_tiles(terms, base_ref, accs, some, arrived=None):
    tiles = NB // MX
    for k in some:
        if arrived is not None:
            arrived(k)
        lanes = slice(k * MX, (k + 1) * MX)
        base = base_ref[:, lanes]
        left = make_left(terms(lanes), bin_steps(base))
        for n in range(tiles):
            extra = n == tiles - 1 and tiles % 2
            m = k % 2 if extra else n % 2
            acc = accs[n + m if extra else n]
            pltpu.matmul_push_rhs(onehot(base, n * MX), int(n >= 2), m, transpose=True)
            pltpu.matmul_acc_lhs(acc, left[0], load_staged_rhs=int(n >= 2))
            pltpu.matmul_acc_lhs(acc, left[1])


def scatter_pop(accs, sums):
    tiles = NB // MX
    for n in range(tiles):
        value = pltpu.matmul_pop(accs[n])
        if n == tiles - 1 and tiles % 2:
            value = value + pltpu.matmul_pop(accs[n + 1])
        for j in range(MX // LANE):
            at = (n * MX // LANE + j) * LEFT
            sums[at : at + LEFT, :] = value[:, j * LANE : (j + 1) * LANE]


def add_corners(sums, acc):
    pieces = []
    for bc in range(4):
        tiles = []
        for j in range(JB):
            base = j * LEFT + bc
            column = [sums[pl.ds(base + 4 * c, 8, stride=12), :] for c in range(3)]
            tiles.append(jnp.concatenate(column + [sums[pl.ds(base + 96, 8, stride=4), :]], axis=0))
        pieces.append(jnp.concatenate(tiles, axis=1))
    near = [pieces[2 * b] + pltpu.roll(pieces[2 * b + 1], 1, 1) for b in range(2)]
    total = near[0] + pltpu.roll(near[1], SZ, 1)
    total = jnp.concatenate([total, jnp.zeros((ROWS, LW - NB), jnp.float32)], axis=1)
    acc[...] = pltpu.roll(total, OFF, 1)


def damage_terms(part, weight):
    def terms(lanes):
        share = part[0:1, lanes] * weight[:, lanes]
        return [share, share * part[23:24, lanes], share * part[24:25, lanes]]
    return terms


def velocity_terms(part, weight, slope):
    def terms(lanes):
        mass = part[0:1, lanes]
        scale = -time_step * part[1:2, lanes]
        out = []
        for i in range(3):
            term = (mass * part[2 + i : 3 + i, lanes]) * weight[:, lanes]
            for j in range(3):
                row = 14 + 3 * i + j
                term = term + (scale * part[row : row + 1, lanes]) * slope[8 * j : 8 * j + 8, lanes]
            out.append(term)
        return out
    return terms


def send_spots(kind):
    if kind:
        return ((H - 1) * SZ, (H - 1 + CY) * SZ), (H - 1, H - 1 + CZ)
    return ((H - 1) * SZ, CY * SZ), (H - 1, CZ)


def land_spots(kind):
    if kind:
        return ((H - 1) * SZ, (H - 1 + CY) * SZ), (H - 1, H - 1 + CZ)
    return (0, (SY - KEEP) * SZ), (0, SZ - KEEP)


def pack_y(kind, acc, ysend):
    for d, lane0 in enumerate(send_spots(kind)[0]):
        ysend[d] = take(acc[...], lane0, WIDE[kind] * SZ)


def pack_z(kind, acc, zsend, esend):
    wide = WIDE[kind]
    y_at, z_at = send_spots(kind)
    z, _ = lane_z(8)
    for d, z0 in enumerate(z_at):
        out = jnp.zeros((8, LW), jnp.float32)
        for s in range(4):
            value = spin(acc[8 * s : 8 * s + 8, :], s * wide - z0)
            out = jnp.where((z >= s * wide) & (z < (s + 1) * wide), value, out)
        if kind:
            zsend[d] = sum(spin(take(out, (H - 1 + q * FY) * SZ, FY * SZ), 4 * wide * q) for q in range(FOLDS))
        else:
            zsend[d] = out[:, ZA:ZB]
        for e, lane0 in enumerate(y_at):
            esend[2 * e + d] = take(out, lane0, wide * SZ)


def land_y(kind, acc, yrecv, has):
    for d, lane0 in enumerate(land_spots(kind)[0]):
        put_add(acc, lane0, WIDE[kind] * SZ, only(has(2 * d - 1, 0), yrecv[d]))


def land_z(kind, acc, zrecv, erecv, zin, has):
    wide = WIDE[kind]
    y_at, z_at = land_spots(kind)
    z, _ = lane_z(8)
    for d, z0 in enumerate(z_at):
        if kind:
            zin[...] = jnp.zeros((8, LW), jnp.float32)
            folded = only(has(0, 2 * d - 1), zrecv[d])
            short, lane = z[:, :ZF], iota((8, ZF), 1)
            for q in range(FOLDS):
                z1 = 4 * wide * q
                mine = (short >= z1) & (short < z1 + 4 * wide) & (lane < FY * SZ)
                put_add(zin, (H - 1 + q * FY) * SZ, FY * SZ, spin(jnp.where(mine, folded, 0.0), -z1))
        else:
            zin[:, :ZA] = jnp.zeros((8, ZA), jnp.float32)
            zin[:, ZB:] = jnp.zeros((8, LW - ZB), jnp.float32)
            zin[:, ZA:ZB] = only(has(0, 2 * d - 1), zrecv[d])
        for e, lane0 in enumerate(y_at):
            put_add(zin, lane0, wide * SZ, only(has(2 * e - 1, 2 * d - 1), erecv[2 * e + d]))
        whole = zin[...]
        for s in range(4):
            value = jnp.where((z >= s * wide) & (z < (s + 1) * wide), whole, 0.0)
            acc[8 * s : 8 * s + 8, :] += spin(value, z0 - s * wide)


def tail_rows(last, c):
    row = iota(last.shape, 0)
    first = spin0(last, -c)
    second = spin0(last, -c - 2)
    return jnp.where(row == 0, first, jnp.where(row == 1, second, 0.0))


def spin0(value, shift):
    shift = shift % value.shape[0]
    return pltpu.roll(value, shift, 0) if shift else value


def pack_edge(acc, edge):
    row = iota((8, LW), 0)
    out = jnp.zeros((8, LW), jnp.float32)
    for c in range(3):
        value = acc[8 * c : 8 * c + 8, :]
        out = jnp.where(row == c, spin0(value, c), jnp.where(row == 3 + c, spin0(value, 2 + c), out))
    edge[...] = out


def build_full(acc, low, high, has_low, has_high):
    row = iota((8, LW), 0)
    own_last, low_last = acc[24:32, :], low[24:32, :]
    out = []
    for c in range(3):
        at = slice(8 * c, 8 * c + 8)
        first = only(has_low, jnp.where(row >= 4, low[at, :], 0.0))
        middle = acc[at, :] + only(has_low, tail_rows(low_last, c))
        last = tail_rows(own_last, c) + only(has_high, jnp.where(row < 6, high[at, :], 0.0))
        out.append(jnp.concatenate([first, middle, last], axis=0))
    return out


def relax_all(place, nodes, full, line):
    ix, iy, iz = place
    z, y = lane_z(1)
    gz = z - H + (iz * CZ).astype(jnp.float32)
    gy = y - H + (iy * CY).astype(jnp.float32)
    flat_in = (gz >= 0) & (gz < nodes[2]) & (gy >= 0) & (gy < nodes[1]) & (y < SY)
    row = lax.broadcasted_iota(jnp.int32, (RD, 1), 0)
    gx = row - 4 - H + ix * CX
    row_in = (gx >= 0) & (gx < nodes[0]) & (row >= 4) & (row < 4 + SX)
    inside = row_in.astype(jnp.float32) * flat_in.astype(jnp.float32)
    mass = jnp.maximum(full[0], mass_floor)
    factor = inside / mass
    damage = full[1] * factor
    drive = full[2] * factor
    keep = (1.0 - relax_rate * (6.0 * length_sq + 1.0)) * inside - (2.0 * relax_rate) * drive
    push = (2.0 * relax_rate) * drive
    spread = (relax_rate * length_sq) * inside
    tiles = LW // LANE
    line[0:8, :] = jnp.zeros((8, LANE), jnp.float32)
    line[8 + tiles * RD :, :] = jnp.zeros((8, LANE), jnp.float32)
    for _ in range(SUBSTEPS):
        for j in range(tiles):
            line[8 + j * RD : 8 + (j + 1) * RD, :] = damage[:, j * LANE : (j + 1) * LANE]
        pair = damage + pltpu.roll(damage, SZ + 1, 1)
        along = jnp.concatenate(
            [line[pl.ds(7 + j * RD, RD), :] + line[pl.ds(9 + j * RD, RD), :] for j in range(tiles)], axis=1)
        ring = along + pltpu.roll(pair, LW - SZ, 1) + pltpu.roll(pair, LW - 1, 1)
        damage = spread * ring + keep * damage + push
    for j in range(tiles):
        line[8 + j * RD : 8 + (j + 1) * RD, :] = damage[:, j * LANE : (j + 1) * LANE]
    return damage, factor


def show_damage(line, damage_out):
    own = jnp.concatenate([line[pl.ds(8 + j * RD + 4 + H, CX), :] for j in range(LW // LANE)], axis=1)
    for y in range(CY):
        damage_out[:, y, :] = pltpu.roll(own, LW - (H + y) * SZ - H, 1)[:, :CZ]


def make_fields(damage, factor, acc, low, high, has_low, has_high, field_left):
    row = iota((8, LW), 0)
    last = acc[24:32, :]
    low_last = only(has_low, low[...])
    last = last + only(has_high, high[...])
    velocity = []
    for c in range(3):
        at = slice(8 * c, 8 * c + 8)
        first = acc[at, :] + tail_rows(low_last, c)
        velocity.append(first * factor[8:16])
    pair = lambda v: jnp.where(row < 4, jnp.broadcast_to(v[16:17], row.shape), jnp.broadcast_to(v[17:18], row.shape))
    last = jnp.where(row < 3, last, pltpu.roll(last, 1, 0))
    last = jnp.where((row == 3) | (row == 7), pair(damage), last * pair(factor))
    whole = jnp.concatenate(velocity + [damage[8:16], last], axis=0)
    whole = pltpu.roll(whole, LW - OFF, 1)[:, :NB]
    turned = [whole, pltpu.roll(whole, NB - 1, 1)]
    for bc in range(4):
        moved = turned[bc & 1]
        if bc >> 1:
            moved = pltpu.roll(moved, NB - SZ, 1)
        for j in range(JB):
            lanes = slice(j * LANE, (j + 1) * LANE)
            for f in range(4):
                field_left[pl.ds(j * FL + 4 * f + bc, 8, stride=16), :] = moved[8 * f : 8 * f + 8, lanes]
            field_left[pl.ds(j * FL + 128 + bc, 8, stride=4), :] = moved[32:40, lanes]


def corners(half, base_ref, field_left, got_ref, bx_ref):
    depth = NB // MX
    tiles = TAIL // MX

    def multiply(*accs):
        for k in range(depth):
            value = jnp.concatenate(
                [field_left[j * FL : (j + 1) * FL, :] for j in range(k * MX // LANE, (k + 1) * MX // LANE)], axis=1)
            high, low = split(value)
            for n in range(tiles):
                at = half * TAIL + n * MX
                pltpu.matmul_push_rhs(onehot(base_ref[:, at : at + MX], k * MX), n // 2 % 2, n % 2)
                pltpu.matmul_acc_lhs(accs[n], high, load_staged_rhs=n // 2 % 2)
                pltpu.matmul_acc_lhs(accs[n], low)
        for n in range(tiles):
            value = pltpu.matmul_pop(accs[n])
            for j in range(MX // LANE):
                for r in range(0, FL, 8):
                    got_ref[pl.ds(r * MOST + n * MX // LANE + j, 8, stride=MOST), :] = (
                        value[r : r + 8, j * LANE : (j + 1) * LANE])

    pl.run_scoped(multiply, *[pltpu.ACC(n % 2)((FL, MX), jnp.float32) for n in range(tiles)])
    bx = bx_ref[MOST * half : MOST * half + MOST, :]
    at = [bx == x for x in range(CX + 1)]
    out = [[None] * 8 for _ in range(4)]
    for f in range(4):
        for bc in range(4):
            near = [jnp.zeros((MOST, LANE), jnp.float32)] * 2
            for x in range(EX):
                r = 16 * x + 4 * f + bc
                value = got_ref[r * MOST : (r + 1) * MOST, :]
                if x < EX - 1:
                    near[0] = jnp.where(at[x], value, near[0])
                if x > 0:
                    near[1] = jnp.where(at[x - 1], value, near[1])
            out[f][bc], out[f][4 + bc] = near
    return out


def total(values):
    while len(values) > 1:
        values = [a + b for a, b in zip(values[::2], values[1::2])]
    return values[0]


def move(corner, w, g, p):
    moved = [total([w(k) * corner[i][k] for k in range(8)]) for i in range(3)]
    velgrad = [[total([corner[i][k] * g(j, k) for k in range(8)]) for j in range(3)] for i in range(3)]
    damaged = jnp.maximum(p(23), total([w(k) * corner[3][k] for k in range(8)]))
    deform = [[p(5 + 3 * i + j) for j in range(3)] for i in range(3)]
    stretch = [[(1.0 if i == j else 0.0) + time_step * velgrad[i][j] for j in range(3)] for i in range(3)]
    mapped = [
        stretch[i][0] * deform[0][j] + stretch[i][1] * deform[1][j] + stretch[i][2] * deform[2][j]
        for i in range(3) for j in range(3)
    ]
    return moved + mapped + [damaged]


def finish(late, early):
    moved, m, damaged = late[:3], late[3:12], late[12]
    mapped = [m[0:3], m[3:6], m[6:9]]
    jacobian = (
        mapped[0][0] * (mapped[1][1] * mapped[2][2] - mapped[1][2] * mapped[2][1])
        - mapped[0][1] * (mapped[1][0] * mapped[2][2] - mapped[1][2] * mapped[2][0])
        + mapped[0][2] * (mapped[1][0] * mapped[2][1] - mapped[1][1] * mapped[2][0])
    )
    left = {}
    for i in range(3):
        for j in range(i, 3):
            left[i, j] = mapped[i][0] * mapped[j][0] + mapped[i][1] * mapped[j][1] + mapped[i][2] * mapped[j][2]
            left[j, i] = left[i, j]
    degrade = (1.0 - damaged) ** 2
    swell = bulk_coef * (jacobian - 1.0)
    stress = []
    for i in range(3):
        for j in range(3):
            term = shear_mod * (left[i, j] - (1.0 if i == j else 0.0))
            if i == j:
                term = term + swell
            stress.append(degrade * term)
    energy = 0.5 * shear_mod * (left[0, 0] + left[1, 1] + left[2, 2] - 3.0) + 0.5 * bulk_coef * (jacobian - 1.0) ** 2
    history = jnp.maximum(early[2], energy)
    position = [early[3 + i] + time_step * moved[i] for i in range(3)]
    return early[:2] + moved + m + stress + [damaged, history] + position


def step_kernel(sizes, *refs):
    slots = up_to(NB // MX, 2)
    kinds = [pltpu.ACC(n % 2)((LEFT, MX), jnp.float32) for _ in range(2) for n in range(slots)]
    pl.run_scoped(lambda *accs: step_body(accs, sizes, *refs), *kinds)


def step_body(
    accs, sizes, part_in, base_in, weight_in, slope_in, counts, ext, prior_out, damage_out,
    part, base_ref, weight, slope, load_sem, out, sums, acc_d, acc_v, zin, line, field_left, got, turned, bx_ref,
    ysend_d, yrecv_d, zsend_d, zrecv_d, esend_d, erecv_d, ysend_v, yrecv_v, zsend_v, zrecv_v, esend_v, erecv_v,
    xrecv_d, xrecv_v, edge_v, early_send, early_recv, late_send, late_recv, send_sem, recv_sem,
):
    names = ("gx", "gy", "gz")
    count = part.shape[1]
    chunk = count // CHUNKS
    loads = []
    for c in range(CHUNKS):
        lanes = pl.ds(c * chunk, chunk)
        loads.append([
            pltpu.make_async_copy(src.at[:, lanes], dst.at[:, lanes], load_sem.at[4 * c + i])
            for i, (src, dst) in enumerate(
                ((base_in, base_ref), (part_in, part), (weight_in, weight), (slope_in, slope)))
        ])
    for load in loads[0]:
        load.start()
    place = [lax.axis_index(a) for a in names]
    has_low = [i > 0 for i in place]
    has_high = [i < n - 1 for i, n in zip(place, sizes)]
    last = sizes[2]
    following, previous = lax.rem(place[2] + 1, last), lax.rem(place[2] + last - 1, last)
    bins = count // BIN

    def has(dy, dz):
        found = None
        for k, d in ((1, dy), (2, dz)):
            if d:
                one = has_high[k] if d > 0 else has_low[k]
                found = one if found is None else found & one
        return found

    def device(dy, dz):
        return {names[k]: place[k] + d for k, d in ((1, dy), (2, dz)) if d}

    barrier = pltpu.get_barrier_semaphore()
    waits = 2
    ahead = [(has_low[0], {"gx": place[0] - 1}), (has_high[0], {"gx": place[0] + 1})]
    for exists, other in ahead + [(has(*d), device(*d)) for d in DIRS]:
        @pl.when(exists)
        def _(other=other):
            pl.semaphore_signal(barrier, inc=1, device_id=other, device_id_type=MESH)
        waits = waits + exists.astype(jnp.int32)
    for other in (following, previous):
        pl.semaphore_signal(barrier, inc=1, device_id={"gz": other}, device_id_type=MESH)

    pending = []

    def copy_to(slot, back, src, dst, other):
        return pltpu.make_async_remote_copy(
            src_ref=src, dst_ref=dst, send_sem=send_sem.at[slot], recv_sem=recv_sem.at[back],
            device_id=other, device_id_type=MESH)

    def bufs(kind):
        if kind:
            return (ysend_v, yrecv_v), (zsend_v, zrecv_v), (esend_v, erecv_v)
        return (ysend_d, yrecv_d), (zsend_d, zrecv_d), (esend_d, erecv_d)

    def message(kind, dy, dz):
        y, z = (dy + 1) // 2, (dz + 1) // 2
        if dz == 0:
            (src, dst), at, back = bufs(kind)[0], y, 1 - y
            base = 0
        elif dy == 0:
            (src, dst), at, back = bufs(kind)[1], z, 1 - z
            base = 2
        else:
            (src, dst), at, back = bufs(kind)[2], 2 * y + z, 2 * (1 - y) + 1 - z
            base = 4
        base += 8 * kind
        return copy_to(base + at, base + back, src.at[at], dst.at[back], device(dy, dz))

    def start(kind, chosen):
        for d in chosen:
            copy = message(kind, *d)
            pending.append((has(*d), copy))
            @pl.when(has(*d))
            def _(copy=copy):
                copy.start()

    def arrive(kind, chosen):
        for dy, dz in chosen:
            copy = message(kind, -dy, -dz)
            @pl.when(has(dy, dz))
            def _(copy=copy):
                copy.wait_recv()

    faces_y = [(-1, 0), (1, 0)]
    others = [d for d in DIRS if d[1] != 0]

    def x_messages(kind):
        src = (edge_v, acc_v.at[24:32]) if kind else (acc_d, acc_d)
        recv = xrecv_v if kind else xrecv_d
        base = 16 + 2 * kind
        return [
            copy_to(base + d, base + 1 - d, src[d], recv.at[1 - d], {"gx": place[0] + 2 * d - 1}) for d in range(2)]

    def x_start(kind):
        for (exists, _), copy in zip(ahead, x_messages(kind)):
            pending.append((exists, copy))
            @pl.when(exists)
            def _(copy=copy):
                copy.start()

    def x_arrive(kind):
        made = x_messages(kind)
        for exists, copy in ((has_low[0], made[1]), (has_high[0], made[0])):
            @pl.when(exists)
            def _(copy=copy):
                copy.wait_recv()

    def ring(slot, src, dst):
        copy = copy_to(slot, slot, src, dst, {"gz": following})
        copy.start()
        return copy

    for group in loads[1:]:
        for load in group:
            load.start()

    def arrived(k):
        if k * MX % chunk == 0:
            for load in loads[k * MX // chunk]:
                load.wait()

    slots = up_to(NB // MX, 2)
    spans = count // MX
    early_spans = spans * EARLY_PART // 8

    scatter_tiles(damage_terms(part, weight), base_ref, accs[:slots], range(spans), arrived)
    scatter_pop(accs[:slots], sums.at[0])
    terms = velocity_terms(part, weight, slope)
    scatter_tiles(terms, base_ref, accs[slots:], range(early_spans))
    add_corners(sums.at[0], acc_d)
    pack_z(0, acc_d, zsend_d, esend_d)
    pack_y(0, acc_d, ysend_d)
    pl.semaphore_wait(barrier, waits)
    start(0, others)
    start(0, faces_y)
    scatter_tiles(terms, base_ref, accs[slots:], range(early_spans, spans))
    scatter_pop(accs[slots:], sums.at[1])
    add_corners(sums.at[1], acc_v)
    pack_z(1, acc_v, zsend_v, esend_v)
    start(1, others)
    pack_y(1, acc_v, ysend_v)
    start(1, faces_y)

    lanes = lambda j: slice(j * LANE, (j + 1) * LANE)
    for j in range(bins):
        for group in range(3):
            turned[(group * bins + j) * 8 : (group * bins + j + 1) * 8, :] = part[8 * group : 8 * group + 8, lanes(j)]
        turned[(3 * bins + j) * 8 : (3 * bins + j) * 8 + 4, :] = part[24:28, lanes(j)]
        turned[(4 * bins + j) * 8 : (4 * bins + j + 1) * 8, :] = weight[:, lanes(j)]
        for group in range(3):
            at = ((5 + group) * bins + j) * 8
            turned[at : at + 8, :] = slope[8 * group : 8 * group + 8, lanes(j)]
        bx_ref[j : j + 1, :] = base_ref[0:1, lanes(j)]

    def dense(half):
        def read(group, s):
            return turned[pl.ds((group * bins + half * MOST) * 8 + s, MOST, stride=8), :]
        return (
            lambda k: read(4, k), lambda j, k: read(5 + j, k), lambda r: read(r // 8, r % 8)
        )

    halves = bins // MOST
    flying = []
    _, _, p = dense(halves - 1)
    early = [p(0), p(1), p(24), p(25), p(26), p(27)]
    early.append(jnp.broadcast_to(counts[0], (8, LANE)).astype(jnp.float32))
    for q, value in enumerate(early):
        early_send[8 * q : 8 * q + 8, :] = value
    flying.append(ring(20, early_send, early_recv))
    ext[:, (MOST + bins) * LANE :] = jnp.zeros((PARTS, TAIL), jnp.float32)

    arrive(0, faces_y)
    land_y(0, acc_d, yrecv_d, has)
    arrive(0, others)
    land_z(0, acc_d, zrecv_d, erecv_d, zin, has)
    x_start(0)
    arrive(1, faces_y)
    land_y(1, acc_v, yrecv_v, has)
    arrive(1, others)
    land_z(1, acc_v, zrecv_v, erecv_v, zin, has)
    pack_edge(acc_v, edge_v)
    x_start(1)
    x_arrive(0)
    full = build_full(acc_d, xrecv_d.at[0], xrecv_d.at[1], has_low[0], has_high[0])
    nodes = [n * c for n, c in zip(sizes, (CX, CY, CZ))]
    damage, factor = relax_all(place, nodes, full, line)
    x_arrive(1)
    make_fields(damage, factor, acc_v, xrecv_v.at[0], xrecv_v.at[1], has_low[0], has_high[0], field_left)

    def store(first, values, gone=None):

        for r, value in enumerate(values):
            if gone is not None:
                value = jnp.where(gone, 0.0, value)
            out[pl.ds(first * SLOT + r, MOST, stride=SLOT), :] = value
        for j in range(first, first + MOST):
            for group in range(up_to(PARTS, 8) // 8):
                rows = min(8, PARTS - 8 * group)
                at = j * SLOT + 8 * group
                ext[8 * group : 8 * group + rows, lanes(j)] = out[at : at + rows, :]

    for half in reversed(range(halves)):
        w, g, p = dense(half)
        late = move(corners(half, base_ref, field_left, got, bx_ref), w, g, p)
        gone = None
        if half == halves - 1:
            for q, value in enumerate(late):
                late_send[8 * q : 8 * q + 8, :] = value
            flying.append(ring(21, late_send, late_recv))
            show_damage(line, damage_out)
            gone = iota((MOST, LANE), 0) + jnp.broadcast_to(counts[0], (MOST, LANE)) >= MOST
        store((half + 1) * MOST, finish(late, [p(0), p(1), p(24), p(25), p(26), p(27)]), gone)

    for copy in flying:
        copy.wait_recv()
    rows = lambda ref, q: ref[8 * q : 8 * q + 8, :]
    store(0, finish([rows(late_recv, q) for q in range(LATE)], [rows(early_recv, q) for q in range(6)]))
    prior_out[...] = rows(early_recv, 6).astype(jnp.int32)
    for copy in flying:
        copy.wait_send()
    for exists, copy in pending:
        @pl.when(exists)
        def _(copy=copy):
            copy.wait_send()


def place_kernel(ext, prior_ref, damage_in, migrated, damage_out, sem):
    width = migrated.shape[1]
    start = pl.multiple_of((MOST - prior_ref[0, 0]) * BIN, BIN)
    copies = [
        pltpu.make_async_copy(damage_in, damage_out, sem.at[0]),
        pltpu.make_async_copy(ext.at[:, pl.ds(start, width)], migrated, sem.at[1]),
    ]
    for copy in copies:
        copy.start()
    for copy in copies:
        copy.wait()


def per_device(particles, stencil_base, weights, gradients, counts):
    count = particles.shape[1]
    bins = count // BIN
    sizes = tuple(lax.axis_size(a) for a in ("gx", "gy", "gz"))
    vmem = pl.BlockSpec(memory_space=pltpu.VMEM)
    anywhere = pl.BlockSpec(memory_space=pl.ANY)
    f32 = jnp.float32
    two = lambda *shape: [pltpu.VMEM(shape, f32)] * 2
    ext, prior, near_damage = pl.pallas_call(
        functools.partial(step_kernel, sizes),
        name="step",
        out_shape=(
            pltpu.VMEM((PARTS, count + 2 * TAIL), f32),
            pltpu.VMEM((8, LANE), jnp.int32),
            pltpu.VMEM((CX, CY, CZ), f32),
        ),
        in_specs=[anywhere] * 4 + [pl.BlockSpec(memory_space=pltpu.SMEM)],
        out_specs=(vmem,) * 3,
        scratch_shapes=[
            pltpu.VMEM((PARTS, count), f32),
            pltpu.VMEM((3, count), jnp.int32),
            pltpu.VMEM((8, count), f32),
            pltpu.VMEM((24, count), f32),
            pltpu.SemaphoreType.DMA((4 * CHUNKS,)),
            pltpu.VMEM(((bins + MOST) * SLOT, LANE), f32),
            pltpu.VMEM((2, JB * LEFT, LANE), f32),
            pltpu.VMEM((ROWS, LW), f32),
            pltpu.VMEM((ROWS, LW), f32),
            pltpu.VMEM((8, LW), f32),
            pltpu.VMEM((16 + LW // LANE * RD, LANE), f32),
            pltpu.VMEM((JB * FL, LANE), f32),
            pltpu.VMEM((MOST * FL, LANE), f32),
            pltpu.VMEM((GROUPS * bins * 8, LANE), f32),
            pltpu.VMEM((bins, LANE), jnp.int32),
            *two(2, ROWS, FACE[0]),
            *two(2, 8, ZB - ZA),
            *two(4, 8, FACE[0]),
            *two(2, ROWS, FACE[1]),
            *two(2, 8, ZF),
            *two(4, 8, FACE[1]),
            pltpu.VMEM((2, ROWS, LW), f32),
            pltpu.VMEM((2, 8, LW), f32),
            pltpu.VMEM((8, LW), f32),
            *two(EARLY * 8, LANE),
            *two(LATE * 8, LANE),
            pltpu.SemaphoreType.DMA((22,)),
            pltpu.SemaphoreType.DMA((22,)),
        ],
        compiler_params=pltpu.CompilerParams(
            collective_id=0, has_side_effects=True, vmem_limit_bytes=60 * 1024 * 1024
        ),
    )(particles, stencil_base, weights, gradients.reshape(24, count), counts)
    return pl.pallas_call(
        place_kernel,
        name="place",
        out_shape=(
            jax.ShapeDtypeStruct((PARTS, count + TAIL), f32),
            jax.ShapeDtypeStruct((CX, CY, CZ), f32),
        ),
        in_specs=[anywhere, vmem, anywhere],
        out_specs=(anywhere,) * 2,
        scratch_shapes=[pltpu.SemaphoreType.DMA((2,))],
        compiler_params=pltpu.CompilerParams(vmem_limit_bytes=4 * 1024 * 1024),
    )(ext, prior, near_damage)


def solution(mesh):
    return jax.shard_map(
        per_device,
        mesh=mesh,
        in_specs=(
            P(None, ("gx", "gy", "gz")),
            P(None, ("gx", "gy", "gz")),
            P(None, ("gx", "gy", "gz")),
            P(None, None, ("gx", "gy", "gz")),
            P(("gx", "gy", "gz")),
        ),
        out_specs=(P(None, ("gx", "gy", "gz")), P("gx", "gy", "gz")),
        check_vma=False,
    )
```

```python
import functools
import jax
import jax.numpy as jnp
from jax import lax
from jax.experimental import pallas as pl
from jax.experimental.pallas import tpu as pltpu
from jax.sharding import PartitionSpec as P

CX = 8
CY = 16
CZ = 32
NBIN = 16
BIN = 128
SUBSTEPS = 4
MOST = 8

time_step = 0.1
relax_rate = 0.2
length_sq = 0.6
shear_mod = 1.0
bulk_coef = 1.5
mass_floor = 0.5

MESH = pl.DeviceIdType.MESH


def up_to(value, unit):
    return (value + unit - 1) // unit * unit


H = SUBSTEPS + 1
EX, EY, EZ = CX + 2, CY + 2, CZ + 2
SX, SY, SZ = CX + 2 * H, CY + 2 * H, CZ + 2 * H
LANE = 128
MX = 256
LW = up_to(SY * SZ, LANE)
NB = up_to((CY + 1) * SZ + CZ + 2, MX)
JB = NB // LANE
OFF = (H - 1) * SZ + H - 1
KEEP = H + 1
RD = 24
ROWS = 32
LEFT = up_to(EX * 12, 16)
WIDE = {0: KEEP, 1: 2}
FACE = {0: up_to(KEEP * SZ, LANE), 1: up_to(2 * SZ, LANE)}
ZA, ZB = (H - 1) * SZ // LANE * LANE, up_to((H + CY + 1) * SZ, LANE)
FD = 64
TAIL = MOST * BIN
PARTS = 28
SLOT = 32
GROUPS = 8
CHUNKS = 1
EARLY_PART = 8
LATE = 13
EARLY = 7
FOLDS = 3
FY = EY // FOLDS
ZF = up_to(FY * SZ, LANE)
DIRS = [(dy, dz) for dy in (-1, 0, 1) for dz in (-1, 0, 1) if (dy, dz) != (0, 0)]


def iota(shape, axis):
    return lax.broadcasted_iota(jnp.int32, shape, axis)


def take(value, lane0, width):
    a = lane0 // LANE * LANE
    span = up_to(lane0 - a + width, LANE)
    value = value[:, a : a + span]
    shift = (span - (lane0 - a)) % span
    if shift:
        value = pltpu.roll(value, shift, 1)
    value = value[:, : up_to(width, LANE)]
    return jnp.where(iota(value.shape, 1) < width, value, 0.0)


def put_add(ref, lane0, width, value):
    a = lane0 // LANE * LANE
    span = max(up_to(lane0 - a + width, LANE), value.shape[1])
    extra = span - value.shape[1]
    if extra:
        value = jnp.concatenate([value, jnp.zeros((value.shape[0], extra), jnp.float32)], axis=1)
    if lane0 - a:
        value = pltpu.roll(value, lane0 - a, 1)
    ref[:, a : a + span] += value


def spin(value, shift):
    shift = shift % value.shape[1]
    return pltpu.roll(value, shift, 1) if shift else value


def only(has, value):
    return jnp.where(has, value, jnp.zeros_like(value))


def lane_z(rows):
    lane = lax.broadcasted_iota(jnp.int32, (rows, LW), 1).astype(jnp.float32)
    y = jnp.floor((lane + 0.5) * (1.0 / SZ))
    return lane - SZ * y, y


def onehot(base, first):
    shape = (16, base.shape[1])
    flat = jnp.broadcast_to(base[1:2, :] * SZ + base[2:3, :], shape) - iota(shape, 0)
    flat = flat.astype(jnp.int16)
    one, zero = jnp.bfloat16(1), jnp.bfloat16(0)
    return jnp.concatenate([jnp.where(flat == jnp.int16(first + r), one, zero) for r in range(0, MX, 16)], axis=0)


def split(value):
    high = value.astype(jnp.bfloat16)
    return high, (value - high.astype(jnp.float32)).astype(jnp.bfloat16)


def bin_steps(base):
    count = base.shape[1]
    bx = jnp.broadcast_to(base[0:1, :], (16, count))
    steps = [bx - (iota((16, count), 0) >= cut).astype(jnp.int32) for cut in (12, 8, 4)]
    return [v.astype(jnp.float32).astype(jnp.bfloat16) for v in steps]


def make_left(terms, steps):
    count = terms[0].shape[1]
    low = iota((8, count), 0) < 4
    turned = [pltpu.roll(t, 4, 0) for t in terms]
    patterns = []
    for a in range(2):
        def join(p, q):
            return jnp.where(low, turned[p] if a else terms[p], terms[q] if a else turned[q])
        parts = [join(0, 1), join(2, 0), join(1, 2)]
        patterns.append([split(jnp.concatenate([parts[i], parts[j]], axis=0)) for i, j in ((0, 1), (2, 0), (1, 2))])
    zero = jnp.bfloat16(0)
    rows = [[], []]
    for t in range(LEFT // 16):
        k = t % 3
        x = 16 * t // 12
        near, far = steps[k] == jnp.bfloat16(x), steps[k] == jnp.bfloat16(x - 1)
        for part in range(2):
            rows[part].append(jnp.where(near, patterns[0][k][part], jnp.where(far, patterns[1][k][part], zero)))
    return [jnp.concatenate(part, axis=0) for part in rows]


def scatter_tiles(terms, base_ref, accs, some, arrived=None):
    tiles = NB // MX
    for k in some:
        if arrived is not None:
            arrived(k)
        lanes = slice(k * MX, (k + 1) * MX)
        base = base_ref[:, lanes]
        left = make_left(terms(lanes), bin_steps(base))
        for n in range(tiles):
            extra = n == tiles - 1 and tiles % 2
            m = k % 2 if extra else n % 2
            acc = accs[n + m if extra else n]
            pltpu.matmul_push_rhs(onehot(base, n * MX), int(n >= 2), m, transpose=True)
            pltpu.matmul_acc_lhs(acc, left[0], load_staged_rhs=int(n >= 2))
            pltpu.matmul_acc_lhs(acc, left[1])


def scatter_pop(accs, sums):
    tiles = NB // MX
    for n in range(tiles):
        value = pltpu.matmul_pop(accs[n])
        if n == tiles - 1 and tiles % 2:
            value = value + pltpu.matmul_pop(accs[n + 1])
        for j in range(MX // LANE):
            at = (n * MX // LANE + j) * LEFT
            sums[at : at + LEFT, :] = value[:, j * LANE : (j + 1) * LANE]


def add_corners(sums, acc):
    pieces = []
    for bc in range(4):
        tiles = []
        for j in range(JB):
            base = j * LEFT + bc
            column = [sums[pl.ds(base + 4 * c, 8, stride=12), :] for c in range(3)]
            tiles.append(jnp.concatenate(column + [sums[pl.ds(base + 96, 8, stride=4), :]], axis=0))
        pieces.append(jnp.concatenate(tiles, axis=1))
    near = [pieces[2 * b] + pltpu.roll(pieces[2 * b + 1], 1, 1) for b in range(2)]
    total = near[0] + pltpu.roll(near[1], SZ, 1)
    total = jnp.concatenate([total, jnp.zeros((ROWS, LW - NB), jnp.float32)], axis=1)
    acc[...] = pltpu.roll(total, OFF, 1)


def damage_terms(part, weight):
    def terms(lanes):
        share = part[0:1, lanes] * weight[:, lanes]
        return [share, share * part[23:24, lanes], share * part[24:25, lanes]]
    return terms


def velocity_terms(part, weight, slope):
    def terms(lanes):
        mass = part[0:1, lanes]
        scale = -time_step * part[1:2, lanes]
        out = []
        for i in range(3):
            term = (mass * part[2 + i : 3 + i, lanes]) * weight[:, lanes]
            for j in range(3):
                row = 14 + 3 * i + j
                term = term + (scale * part[row : row + 1, lanes]) * slope[8 * j : 8 * j + 8, lanes]
            out.append(term)
        return out
    return terms


def send_spots(kind):
    if kind:
        return ((H - 1) * SZ, (H - 1 + CY) * SZ), (H - 1, H - 1 + CZ)
    return ((H - 1) * SZ, CY * SZ), (H - 1, CZ)


def land_spots(kind):
    if kind:
        return ((H - 1) * SZ, (H - 1 + CY) * SZ), (H - 1, H - 1 + CZ)
    return (0, (SY - KEEP) * SZ), (0, SZ - KEEP)


def pack_y(kind, acc, ysend):
    for d, lane0 in enumerate(send_spots(kind)[0]):
        ysend[d] = take(acc[...], lane0, WIDE[kind] * SZ)


def pack_z(kind, acc, zsend, esend):
    wide = WIDE[kind]
    y_at, z_at = send_spots(kind)
    z, _ = lane_z(8)
    for d, z0 in enumerate(z_at):
        out = jnp.zeros((8, LW), jnp.float32)
        for s in range(4):
            value = spin(acc[8 * s : 8 * s + 8, :], s * wide - z0)
            out = jnp.where((z >= s * wide) & (z < (s + 1) * wide), value, out)
        if kind:
            zsend[d] = sum(spin(take(out, (H - 1 + q * FY) * SZ, FY * SZ), 4 * wide * q) for q in range(FOLDS))
        else:
            zsend[d] = out[:, ZA:ZB]
        for e, lane0 in enumerate(y_at):
            esend[2 * e + d] = take(out, lane0, wide * SZ)


def land_y(kind, acc, yrecv, has):
    for d, lane0 in enumerate(land_spots(kind)[0]):
        put_add(acc, lane0, WIDE[kind] * SZ, only(has(2 * d - 1, 0), yrecv[d]))


def land_z(kind, acc, zrecv, erecv, zin, has):
    wide = WIDE[kind]
    y_at, z_at = land_spots(kind)
    z, _ = lane_z(8)
    for d, z0 in enumerate(z_at):
        if kind:
            zin[...] = jnp.zeros((8, LW), jnp.float32)
            folded = only(has(0, 2 * d - 1), zrecv[d])
            short, lane = z[:, :ZF], iota((8, ZF), 1)
            for q in range(FOLDS):
                z1 = 4 * wide * q
                mine = (short >= z1) & (short < z1 + 4 * wide) & (lane < FY * SZ)
                put_add(zin, (H - 1 + q * FY) * SZ, FY * SZ, spin(jnp.where(mine, folded, 0.0), -z1))
        else:
            zin[:, :ZA] = jnp.zeros((8, ZA), jnp.float32)
            zin[:, ZB:] = jnp.zeros((8, LW - ZB), jnp.float32)
            zin[:, ZA:ZB] = only(has(0, 2 * d - 1), zrecv[d])
        for e, lane0 in enumerate(y_at):
            put_add(zin, lane0, wide * SZ, only(has(2 * e - 1, 2 * d - 1), erecv[2 * e + d]))
        whole = zin[...]
        for s in range(4):
            value = jnp.where((z >= s * wide) & (z < (s + 1) * wide), whole, 0.0)
            acc[8 * s : 8 * s + 8, :] += spin(value, z0 - s * wide)


def tail_rows(last, c):
    row = iota(last.shape, 0)
    first = spin0(last, -c)
    second = spin0(last, -c - 2)
    return jnp.where(row == 0, first, jnp.where(row == 1, second, 0.0))


def spin0(value, shift):
    shift = shift % value.shape[0]
    return pltpu.roll(value, shift, 0) if shift else value


def pack_edge(acc, edge):
    row = iota((8, LW), 0)
    out = jnp.zeros((8, LW), jnp.float32)
    for c in range(3):
        value = acc[8 * c : 8 * c + 8, :]
        out = jnp.where(row == c, spin0(value, c), jnp.where(row == 3 + c, spin0(value, 2 + c), out))
    edge[...] = out


def build_full(acc, low, high, has_low, has_high):
    row = iota((8, LW), 0)
    own_last, low_last = acc[24:32, :], low[24:32, :]
    out = []
    for c in range(3):
        at = slice(8 * c, 8 * c + 8)
        first = only(has_low, jnp.where(row >= 4, low[at, :], 0.0))
        middle = acc[at, :] + only(has_low, tail_rows(low_last, c))
        last = tail_rows(own_last, c) + only(has_high, jnp.where(row < 6, high[at, :], 0.0))
        out.append(jnp.concatenate([first, middle, last], axis=0))
    return out


def relax_start(place, nodes, full):
    ix, iy, iz = place
    z, y = lane_z(1)
    gz = z - H + (iz * CZ).astype(jnp.float32)
    gy = y - H + (iy * CY).astype(jnp.float32)
    flat_in = (gz >= 0) & (gz < nodes[2]) & (gy >= 0) & (gy < nodes[1]) & (y < SY)
    row = lax.broadcasted_iota(jnp.int32, (RD, 1), 0)
    gx = row - 4 - H + ix * CX
    row_in = (gx >= 0) & (gx < nodes[0]) & (row >= 4) & (row < 4 + SX)
    inside = row_in.astype(jnp.float32) * flat_in.astype(jnp.float32)
    mass = jnp.maximum(full[0], mass_floor)
    factor = inside / mass
    damage = full[1] * factor
    drive = full[2] * factor
    keep = (1.0 - relax_rate * (6.0 * length_sq + 1.0)) * inside - (2.0 * relax_rate) * drive
    push = (2.0 * relax_rate) * drive
    spread = (relax_rate * length_sq) * inside
    return factor, damage, keep, push, spread


def relax_all(coefficients, line):
    _, damage, keep, push, spread = coefficients
    tiles = LW // LANE
    line[0:8, :] = jnp.zeros((8, LANE), jnp.float32)
    line[8 + tiles * RD :, :] = jnp.zeros((8, LANE), jnp.float32)
    for _ in range(SUBSTEPS):
        for j in range(tiles):
            line[8 + j * RD : 8 + (j + 1) * RD, :] = damage[:, j * LANE : (j + 1) * LANE]
        pair = damage + pltpu.roll(damage, SZ + 1, 1)
        along = jnp.concatenate(
            [line[pl.ds(7 + j * RD, RD), :] + line[pl.ds(9 + j * RD, RD), :] for j in range(tiles)], axis=1)
        ring = along + pltpu.roll(pair, LW - SZ, 1) + pltpu.roll(pair, LW - 1, 1)
        damage = spread * ring + keep * damage + push
    for j in range(tiles):
        line[8 + j * RD : 8 + (j + 1) * RD, :] = damage[:, j * LANE : (j + 1) * LANE]
    return damage


def show_damage(line, damage_out):
    own = jnp.concatenate([line[pl.ds(8 + j * RD + 4 + H, CX), :] for j in range(LW // LANE)], axis=1)
    for y in range(CY):
        damage_out[:, y, :] = pltpu.roll(own, LW - (H + y) * SZ - H, 1)[:, :CZ]


def velocity_field(factor, acc, low, high, has_low, has_high, field):
    row = iota((8, LW), 0)
    low_last = only(has_low, low[...])
    last = acc[24:32, :] + only(has_high, high[...])
    velocity = [(acc[8 * c : 8 * c + 8, :] + tail_rows(low_last, c)) * factor[8:16] for c in range(3)]
    spread = lambda r: jnp.broadcast_to(factor[r : r + 1], row.shape)
    last = last * jnp.where(row < 3, spread(16), jnp.where(row < 6, spread(17), 0.0))
    whole = pltpu.roll(jnp.concatenate(velocity + [last], axis=0), LW - OFF, 1)[:, :NB]
    turned = [whole, pltpu.roll(whole, NB - 1, 1)]
    for bc in range(4):
        moved = turned[bc & 1]
        if bc >> 1:
            moved = pltpu.roll(moved, NB - SZ, 1)
        for j in range(JB):
            at, lanes = j * LEFT + bc, slice(j * LANE, (j + 1) * LANE)
            for c in range(3):
                field[pl.ds(at + 4 * c, 8, stride=12), :] = moved[8 * c : 8 * c + 8, lanes]
            field[pl.ds(at + 96, 8, stride=4), :] = moved[24:32, lanes]


def damage_field(damage, field):
    whole = pltpu.roll(damage[8:24], LW - OFF, 1)[:, :NB]
    turned = [whole, pltpu.roll(whole, NB - 1, 1)]
    for bc in range(4):
        moved = turned[bc & 1]
        if bc >> 1:
            moved = pltpu.roll(moved, NB - SZ, 1)
        for j in range(JB):
            for part in range(2):
                field[pl.ds(j * FD + 32 * part + bc, 8, stride=4), :] = (
                    moved[8 * part : 8 * part + 8, j * LANE : (j + 1) * LANE])


def near_nodes(half, rows, base_ref, field, got_ref):
    depth = NB // MX
    tiles = TAIL // MX

    def multiply(*accs):
        for k in range(depth):
            high, low = split(jnp.concatenate(
                [field[j * rows : (j + 1) * rows, :] for j in range(k * MX // LANE, (k + 1) * MX // LANE)], axis=1))
            for n in range(tiles):
                at = half * TAIL + n * MX
                pltpu.matmul_push_rhs(onehot(base_ref[:, at : at + MX], k * MX), n // 2 % 2, n % 2)
                pltpu.matmul_acc_lhs(accs[n], high, load_staged_rhs=n // 2 % 2)
                pltpu.matmul_acc_lhs(accs[n], low)
        for n in range(tiles):
            value = pltpu.matmul_pop(accs[n])
            for j in range(MX // LANE):
                for r in range(0, rows, 8):
                    got_ref[pl.ds(r * MOST + n * MX // LANE + j, 8, stride=MOST), :] = (
                        value[r : r + 8, j * LANE : (j + 1) * LANE])

    pl.run_scoped(multiply, *[pltpu.ACC(n % 2)((rows, MX), jnp.float32) for n in range(tiles)])


def corners(half, got_ref, fields, bx_ref):
    bx = bx_ref[MOST * half : MOST * half + MOST, :]
    at = [bx == x for x in range(CX + 1)]
    out = [[None] * 8 for _ in range(fields)]
    for f in range(fields):
        for bc in range(4):
            near = [jnp.zeros((MOST, LANE), jnp.float32)] * 2
            for x in range(EX):
                r = 4 * (fields * x + f) + bc
                value = got_ref[r * MOST : (r + 1) * MOST, :]
                if x < EX - 1:
                    near[0] = jnp.where(at[x], value, near[0])
                if x > 0:
                    near[1] = jnp.where(at[x - 1], value, near[1])
            out[f][bc], out[f][4 + bc] = near
    return out


def total(values):
    while len(values) > 1:
        values = [a + b for a, b in zip(values[::2], values[1::2])]
    return values[0]


def move(corner, w, g, p):
    moved = [total([w(k) * corner[i][k] for k in range(8)]) for i in range(3)]
    velgrad = [[total([corner[i][k] * g(j, k) for k in range(8)]) for j in range(3)] for i in range(3)]
    deform = [[p(5 + 3 * i + j) for j in range(3)] for i in range(3)]
    stretch = [[(1.0 if i == j else 0.0) + time_step * velgrad[i][j] for j in range(3)] for i in range(3)]
    mapped = [
        stretch[i][0] * deform[0][j] + stretch[i][1] * deform[1][j] + stretch[i][2] * deform[2][j]
        for i in range(3) for j in range(3)
    ]
    return moved + mapped


def damage_of(corner, w, p):
    return [jnp.maximum(p(23), total([w(k) * corner[0][k] for k in range(8)]))]


def finish(late, early):
    moved, m, damaged = late[:3], late[3:12], late[12]
    mapped = [m[0:3], m[3:6], m[6:9]]
    jacobian = (
        mapped[0][0] * (mapped[1][1] * mapped[2][2] - mapped[1][2] * mapped[2][1])
        - mapped[0][1] * (mapped[1][0] * mapped[2][2] - mapped[1][2] * mapped[2][0])
        + mapped[0][2] * (mapped[1][0] * mapped[2][1] - mapped[1][1] * mapped[2][0])
    )
    left = {}
    for i in range(3):
        for j in range(i, 3):
            left[i, j] = mapped[i][0] * mapped[j][0] + mapped[i][1] * mapped[j][1] + mapped[i][2] * mapped[j][2]
            left[j, i] = left[i, j]
    degrade = (1.0 - damaged) ** 2
    swell = bulk_coef * (jacobian - 1.0)
    stress = []
    for i in range(3):
        for j in range(3):
            term = shear_mod * (left[i, j] - (1.0 if i == j else 0.0))
            if i == j:
                term = term + swell
            stress.append(degrade * term)
    energy = 0.5 * shear_mod * (left[0, 0] + left[1, 1] + left[2, 2] - 3.0) + 0.5 * bulk_coef * (jacobian - 1.0) ** 2
    history = jnp.maximum(early[2], energy)
    position = [early[3 + i] + time_step * moved[i] for i in range(3)]
    return early[:2] + moved + m + stress + [damaged, history] + position


def step_kernel(sizes, *refs):
    slots = up_to(NB // MX, 2)
    kinds = [pltpu.ACC(n % 2)((LEFT, MX), jnp.float32) for _ in range(2) for n in range(slots)]
    pl.run_scoped(lambda *accs: step_body(accs, sizes, *refs), *kinds)


def step_body(
    accs, sizes, part_in, base_in, weight_in, slope_in, counts, ext, prior_out, damage_out,
    part, base_ref, weight, slope, load_sem, out, sums, acc_d, acc_v, zin, line, field_v, field_d, got_v, got_d, turned, bx_ref,
    ysend_d, yrecv_d, zsend_d, zrecv_d, esend_d, erecv_d, ysend_v, yrecv_v, zsend_v, zrecv_v, esend_v, erecv_v,
    xrecv_d, xrecv_v, edge_v, early_send, early_recv, late_send, late_recv, send_sem, recv_sem,
):
    names = ("gx", "gy", "gz")
    count = part.shape[1]
    chunk = count // CHUNKS
    loads = []
    for c in range(CHUNKS):
        lanes = pl.ds(c * chunk, chunk)
        loads.append([
            pltpu.make_async_copy(src.at[:, lanes], dst.at[:, lanes], load_sem.at[4 * c + i])
            for i, (src, dst) in enumerate(
                ((base_in, base_ref), (part_in, part), (weight_in, weight), (slope_in, slope)))
        ])
    for load in loads[0]:
        load.start()
    place = [lax.axis_index(a) for a in names]
    has_low = [i > 0 for i in place]
    has_high = [i < n - 1 for i, n in zip(place, sizes)]
    last = sizes[2]
    following, previous = lax.rem(place[2] + 1, last), lax.rem(place[2] + last - 1, last)
    bins = count // BIN

    def has(dy, dz):
        found = None
        for k, d in ((1, dy), (2, dz)):
            if d:
                one = has_high[k] if d > 0 else has_low[k]
                found = one if found is None else found & one
        return found

    def device(dy, dz):
        return {names[k]: place[k] + d for k, d in ((1, dy), (2, dz)) if d}

    barrier = pltpu.get_barrier_semaphore()
    waits = 2
    ahead = [(has_low[0], {"gx": place[0] - 1}), (has_high[0], {"gx": place[0] + 1})]
    for exists, other in ahead + [(has(*d), device(*d)) for d in DIRS]:
        @pl.when(exists)
        def _(other=other):
            pl.semaphore_signal(barrier, inc=1, device_id=other, device_id_type=MESH)
        waits = waits + exists.astype(jnp.int32)
    for other in (following, previous):
        pl.semaphore_signal(barrier, inc=1, device_id={"gz": other}, device_id_type=MESH)

    pending = []

    def copy_to(slot, back, src, dst, other):
        return pltpu.make_async_remote_copy(
            src_ref=src, dst_ref=dst, send_sem=send_sem.at[slot], recv_sem=recv_sem.at[back],
            device_id=other, device_id_type=MESH)

    def bufs(kind):
        if kind:
            return (ysend_v, yrecv_v), (zsend_v, zrecv_v), (esend_v, erecv_v)
        return (ysend_d, yrecv_d), (zsend_d, zrecv_d), (esend_d, erecv_d)

    def message(kind, dy, dz):
        y, z = (dy + 1) // 2, (dz + 1) // 2
        if dz == 0:
            (src, dst), at, back = bufs(kind)[0], y, 1 - y
            base = 0
        elif dy == 0:
            (src, dst), at, back = bufs(kind)[1], z, 1 - z
            base = 2
        else:
            (src, dst), at, back = bufs(kind)[2], 2 * y + z, 2 * (1 - y) + 1 - z
            base = 4
        base += 8 * kind
        return copy_to(base + at, base + back, src.at[at], dst.at[back], device(dy, dz))

    def start(kind, chosen):
        for d in chosen:
            copy = message(kind, *d)
            pending.append((has(*d), copy))
            @pl.when(has(*d))
            def _(copy=copy):
                copy.start()

    def arrive(kind, chosen):
        for dy, dz in chosen:
            copy = message(kind, -dy, -dz)
            @pl.when(has(dy, dz))
            def _(copy=copy):
                copy.wait_recv()

    faces_y = [(-1, 0), (1, 0)]
    others = [d for d in DIRS if d[1] != 0]

    def x_messages(kind):
        src = (edge_v, acc_v.at[24:32]) if kind else (acc_d, acc_d)
        recv = xrecv_v if kind else xrecv_d
        base = 16 + 2 * kind
        return [
            copy_to(base + d, base + 1 - d, src[d], recv.at[1 - d], {"gx": place[0] + 2 * d - 1}) for d in range(2)]

    def x_start(kind):
        for (exists, _), copy in zip(ahead, x_messages(kind)):
            pending.append((exists, copy))
            @pl.when(exists)
            def _(copy=copy):
                copy.start()

    def x_arrive(kind):
        made = x_messages(kind)
        for exists, copy in ((has_low[0], made[1]), (has_high[0], made[0])):
            @pl.when(exists)
            def _(copy=copy):
                copy.wait_recv()

    def ring(slot, src, dst):
        copy = copy_to(slot, slot, src, dst, {"gz": following})
        copy.start()
        return copy

    for group in loads[1:]:
        for load in group:
            load.start()

    def arrived(k):
        if k * MX % chunk == 0:
            for load in loads[k * MX // chunk]:
                load.wait()

    slots = up_to(NB // MX, 2)
    spans = count // MX
    early_spans = spans * EARLY_PART // 8

    scatter_tiles(damage_terms(part, weight), base_ref, accs[:slots], range(spans), arrived)
    scatter_pop(accs[:slots], sums.at[0])
    terms = velocity_terms(part, weight, slope)
    scatter_tiles(terms, base_ref, accs[slots:], range(early_spans))
    add_corners(sums.at[0], acc_d)
    pack_z(0, acc_d, zsend_d, esend_d)
    pack_y(0, acc_d, ysend_d)
    pl.semaphore_wait(barrier, waits)
    start(0, others)
    start(0, faces_y)
    scatter_tiles(terms, base_ref, accs[slots:], range(early_spans, spans))
    scatter_pop(accs[slots:], sums.at[1])
    add_corners(sums.at[1], acc_v)
    pack_z(1, acc_v, zsend_v, esend_v)
    start(1, others)
    pack_y(1, acc_v, ysend_v)
    start(1, faces_y)

    lanes = lambda j: slice(j * LANE, (j + 1) * LANE)
    for j in range(bins):
        for group in range(3):
            turned[(group * bins + j) * 8 : (group * bins + j + 1) * 8, :] = part[8 * group : 8 * group + 8, lanes(j)]
        turned[(3 * bins + j) * 8 : (3 * bins + j) * 8 + 4, :] = part[24:28, lanes(j)]
        turned[(4 * bins + j) * 8 : (4 * bins + j + 1) * 8, :] = weight[:, lanes(j)]
        for group in range(3):
            at = ((5 + group) * bins + j) * 8
            turned[at : at + 8, :] = slope[8 * group : 8 * group + 8, lanes(j)]
        bx_ref[j : j + 1, :] = base_ref[0:1, lanes(j)]

    def dense(half):
        def read(group, s):
            return turned[pl.ds((group * bins + half * MOST) * 8 + s, MOST, stride=8), :]
        return (
            lambda k: read(4, k), lambda j, k: read(5 + j, k), lambda r: read(r // 8, r % 8)
        )

    halves = bins // MOST
    flying = []
    _, _, p = dense(halves - 1)
    early = [p(0), p(1), p(24), p(25), p(26), p(27)]
    early.append(jnp.broadcast_to(counts[0], (8, LANE)).astype(jnp.float32))
    for q, value in enumerate(early):
        early_send[8 * q : 8 * q + 8, :] = value
    flying.append(ring(20, early_send, early_recv))
    ext[:, (MOST + bins) * LANE :] = jnp.zeros((PARTS, TAIL), jnp.float32)

    arrive(0, faces_y)
    land_y(0, acc_d, yrecv_d, has)
    arrive(0, others)
    land_z(0, acc_d, zrecv_d, erecv_d, zin, has)
    x_start(0)
    arrive(1, faces_y)
    land_y(1, acc_v, yrecv_v, has)
    arrive(1, others)
    land_z(1, acc_v, zrecv_v, erecv_v, zin, has)
    pack_edge(acc_v, edge_v)
    x_start(1)
    x_arrive(0)
    x_arrive(1)
    full = build_full(acc_d, xrecv_d.at[0], xrecv_d.at[1], has_low[0], has_high[0])
    nodes = [n * c for n, c in zip(sizes, (CX, CY, CZ))]
    coefficients = relax_start(place, nodes, full)
    tail_half = bins // MOST - 1
    velocity_field(
        coefficients[0], acc_v, xrecv_v.at[0], xrecv_v.at[1], has_low[0], has_high[0], field_v)
    near_nodes(tail_half, LEFT, base_ref, field_v, got_v)
    w, g, p = dense(tail_half)
    tail_late = move(corners(tail_half, got_v, 3, bx_ref), w, g, p)
    damage = relax_all(coefficients, line)
    for q, value in enumerate(tail_late):
        late_send[8 * q : 8 * q + 8, :] = value
    flying.append(ring(21, late_send.at[: 8 * LATE - 8], late_recv.at[: 8 * LATE - 8]))
    damage_field(damage, field_d)

    def store(first, values, gone=None):

        for r, value in enumerate(values):
            if gone is not None:
                value = jnp.where(gone, 0.0, value)
            out[pl.ds(first * SLOT + r, MOST, stride=SLOT), :] = value
        for j in range(first, first + MOST):
            for group in range(up_to(PARTS, 8) // 8):
                rows = min(8, PARTS - 8 * group)
                at = j * SLOT + 8 * group
                ext[8 * group : 8 * group + rows, lanes(j)] = out[at : at + rows, :]

    for half in reversed(range(halves)):
        w, g, p = dense(half)
        if half != tail_half:
            near_nodes(half, LEFT, base_ref, field_v, got_v)
            late = move(corners(half, got_v, 3, bx_ref), w, g, p)
        else:
            late = tail_late
        near_nodes(half, FD, base_ref, field_d, got_d)
        late = late + damage_of(corners(half, got_d, 1, bx_ref), w, p)
        gone = None
        if half == halves - 1:
            late_send[8 * LATE - 8 :, :] = late[-1]
            flying.append(ring(22, late_send.at[8 * LATE - 8 :], late_recv.at[8 * LATE - 8 :]))
            show_damage(line, damage_out)
            gone = iota((MOST, LANE), 0) + jnp.broadcast_to(counts[0], (MOST, LANE)) >= MOST
        store((half + 1) * MOST, finish(late, [p(0), p(1), p(24), p(25), p(26), p(27)]), gone)

    for copy in flying:
        copy.wait_recv()
    rows = lambda ref, q: ref[8 * q : 8 * q + 8, :]
    store(0, finish([rows(late_recv, q) for q in range(LATE)], [rows(early_recv, q) for q in range(6)]))
    prior_out[...] = rows(early_recv, 6).astype(jnp.int32)
    for copy in flying:
        copy.wait_send()
    for exists, copy in pending:
        @pl.when(exists)
        def _(copy=copy):
            copy.wait_send()


def place_kernel(ext, prior_ref, damage_in, migrated, damage_out, sem):
    width = migrated.shape[1]
    start = pl.multiple_of((MOST - prior_ref[0, 0]) * BIN, BIN)
    copies = [
        pltpu.make_async_copy(damage_in, damage_out, sem.at[0]),
        pltpu.make_async_copy(ext.at[:, pl.ds(start, width)], migrated, sem.at[1]),
    ]
    for copy in copies:
        copy.start()
    for copy in copies:
        copy.wait()


def per_device(particles, stencil_base, weights, gradients, counts):
    count = particles.shape[1]
    bins = count // BIN
    sizes = tuple(lax.axis_size(a) for a in ("gx", "gy", "gz"))
    vmem = pl.BlockSpec(memory_space=pltpu.VMEM)
    anywhere = pl.BlockSpec(memory_space=pl.ANY)
    f32 = jnp.float32
    two = lambda *shape: [pltpu.VMEM(shape, f32)] * 2
    ext, prior, near_damage = pl.pallas_call(
        functools.partial(step_kernel, sizes),
        name="step",
        out_shape=(
            pltpu.VMEM((PARTS, count + 2 * TAIL), f32),
            pltpu.VMEM((8, LANE), jnp.int32),
            pltpu.VMEM((CX, CY, CZ), f32),
        ),
        in_specs=[anywhere] * 4 + [pl.BlockSpec(memory_space=pltpu.SMEM)],
        out_specs=(vmem,) * 3,
        scratch_shapes=[
            pltpu.VMEM((PARTS, count), f32),
            pltpu.VMEM((3, count), jnp.int32),
            pltpu.VMEM((8, count), f32),
            pltpu.VMEM((24, count), f32),
            pltpu.SemaphoreType.DMA((4 * CHUNKS,)),
            pltpu.VMEM(((bins + MOST) * SLOT, LANE), f32),
            pltpu.VMEM((2, JB * LEFT, LANE), f32),
            pltpu.VMEM((ROWS, LW), f32),
            pltpu.VMEM((ROWS, LW), f32),
            pltpu.VMEM((8, LW), f32),
            pltpu.VMEM((16 + LW // LANE * RD, LANE), f32),
            pltpu.VMEM((JB * LEFT, LANE), f32),
            pltpu.VMEM((JB * FD, LANE), f32),
            pltpu.VMEM((MOST * LEFT, LANE), f32),
            pltpu.VMEM((MOST * FD, LANE), f32),
            pltpu.VMEM((GROUPS * bins * 8, LANE), f32),
            pltpu.VMEM((bins, LANE), jnp.int32),
            *two(2, ROWS, FACE[0]),
            *two(2, 8, ZB - ZA),
            *two(4, 8, FACE[0]),
            *two(2, ROWS, FACE[1]),
            *two(2, 8, ZF),
            *two(4, 8, FACE[1]),
            pltpu.VMEM((2, ROWS, LW), f32),
            pltpu.VMEM((2, 8, LW), f32),
            pltpu.VMEM((8, LW), f32),
            *two(EARLY * 8, LANE),
            *two(LATE * 8, LANE),
            pltpu.SemaphoreType.DMA((23,)),
            pltpu.SemaphoreType.DMA((23,)),
        ],
        compiler_params=pltpu.CompilerParams(
            collective_id=0, has_side_effects=True, vmem_limit_bytes=60 * 1024 * 1024
        ),
    )(particles, stencil_base, weights, gradients.reshape(24, count), counts)
    return pl.pallas_call(
        place_kernel,
        name="place",
        out_shape=(
            jax.ShapeDtypeStruct((PARTS, count + TAIL), f32),
            jax.ShapeDtypeStruct((CX, CY, CZ), f32),
        ),
        in_specs=[anywhere, vmem, anywhere],
        out_specs=(anywhere,) * 2,
        scratch_shapes=[pltpu.SemaphoreType.DMA((2,))],
        compiler_params=pltpu.CompilerParams(vmem_limit_bytes=4 * 1024 * 1024),
    )(ext, prior, near_damage)


def solution(mesh):
    return jax.shard_map(
        per_device,
        mesh=mesh,
        in_specs=(
            P(None, ("gx", "gy", "gz")),
            P(None, ("gx", "gy", "gz")),
            P(None, ("gx", "gy", "gz")),
            P(None, None, ("gx", "gy", "gz")),
            P(("gx", "gy", "gz")),
        ),
        out_specs=(P(None, ("gx", "gy", "gz")), P("gx", "gy", "gz")),
        check_vma=False,
    )
```

```python
import functools
import jax
import jax.numpy as jnp
from jax import lax
from jax.experimental import pallas as pl
from jax.experimental.pallas import tpu as pltpu
from jax.sharding import PartitionSpec as P

CX = 8
CY = 16
CZ = 32
NBIN = 16
BIN = 128
SUBSTEPS = 4
MOST = 8

time_step = 0.1
relax_rate = 0.2
length_sq = 0.6
shear_mod = 1.0
bulk_coef = 1.5
mass_floor = 0.5

MESH = pl.DeviceIdType.MESH


def up_to(value, unit):
    return (value + unit - 1) // unit * unit


H = SUBSTEPS + 1
EX, EY, EZ = CX + 2, CY + 2, CZ + 2
SX, SY, SZ = CX + 2 * H, CY + 2 * H, CZ + 2 * H
LANE = 128
MX = 256
LW = up_to(SY * SZ, LANE)
NB = up_to((CY + 1) * SZ + CZ + 2, MX)
JB = NB // LANE
OFF = (H - 1) * SZ + H - 1
KEEP = H + 1
RD = 24
ROWS = 32
LEFT = up_to(EX * 12, 16)
WIDE = {0: KEEP, 1: 2}
FACE = {0: up_to(KEEP * SZ, LANE), 1: up_to(2 * SZ, LANE)}
ZA, ZB = (H - 1) * SZ // LANE * LANE, up_to((H + CY + 1) * SZ, LANE)
FD = 64
TAIL = MOST * BIN
PARTS = 28
SLOT = 32
GROUPS = 8
CHUNKS = 1
EARLY_PART = 8
LATE = 13
EARLY = 7
FOLDS = 3
FY = EY // FOLDS
ZF = up_to(FY * SZ, LANE)
DIRS = [(dy, dz) for dy in (-1, 0, 1) for dz in (-1, 0, 1) if (dy, dz) != (0, 0)]


def iota(shape, axis):
    return lax.broadcasted_iota(jnp.int32, shape, axis)


def take(value, lane0, width):
    a = lane0 // LANE * LANE
    span = up_to(lane0 - a + width, LANE)
    value = value[:, a : a + span]
    shift = (span - (lane0 - a)) % span
    if shift:
        value = pltpu.roll(value, shift, 1)
    value = value[:, : up_to(width, LANE)]
    return jnp.where(iota(value.shape, 1) < width, value, 0.0)


def put_add(ref, lane0, width, value):
    a = lane0 // LANE * LANE
    span = max(up_to(lane0 - a + width, LANE), value.shape[1])
    extra = span - value.shape[1]
    if extra:
        value = jnp.concatenate([value, jnp.zeros((value.shape[0], extra), jnp.float32)], axis=1)
    if lane0 - a:
        value = pltpu.roll(value, lane0 - a, 1)
    ref[:, a : a + span] += value


def spin(value, shift):
    shift = shift % value.shape[1]
    return pltpu.roll(value, shift, 1) if shift else value


def only(has, value):
    return jnp.where(has, value, jnp.zeros_like(value))


def lane_z(rows):
    lane = lax.broadcasted_iota(jnp.int32, (rows, LW), 1).astype(jnp.float32)
    y = jnp.floor((lane + 0.5) * (1.0 / SZ))
    return lane - SZ * y, y


def onehot(base, first):
    shape = (16, base.shape[1])
    flat = jnp.broadcast_to(base[1:2, :] * SZ + base[2:3, :], shape) - iota(shape, 0)
    flat = flat.astype(jnp.int16)
    one, zero = jnp.bfloat16(1), jnp.bfloat16(0)
    return jnp.concatenate([jnp.where(flat == jnp.int16(first + r), one, zero) for r in range(0, MX, 16)], axis=0)


def split(value):
    high = value.astype(jnp.bfloat16)
    return high, (value - high.astype(jnp.float32)).astype(jnp.bfloat16)


def bin_steps(base):
    count = base.shape[1]
    bx = jnp.broadcast_to(base[0:1, :], (16, count))
    steps = [bx - (iota((16, count), 0) >= cut).astype(jnp.int32) for cut in (12, 8, 4)]
    return [v.astype(jnp.float32).astype(jnp.bfloat16) for v in steps]


def make_left(terms, steps):
    count = terms[0].shape[1]
    low = iota((8, count), 0) < 4
    turned = [pltpu.roll(t, 4, 0) for t in terms]
    patterns = []
    for a in range(2):
        def join(p, q):
            return jnp.where(low, turned[p] if a else terms[p], terms[q] if a else turned[q])
        parts = [join(0, 1), join(2, 0), join(1, 2)]
        patterns.append([split(jnp.concatenate([parts[i], parts[j]], axis=0)) for i, j in ((0, 1), (2, 0), (1, 2))])
    zero = jnp.bfloat16(0)
    rows = [[], []]
    for t in range(LEFT // 16):
        k = t % 3
        x = 16 * t // 12
        near, far = steps[k] == jnp.bfloat16(x), steps[k] == jnp.bfloat16(x - 1)
        for part in range(2):
            rows[part].append(jnp.where(near, patterns[0][k][part], jnp.where(far, patterns[1][k][part], zero)))
    return [jnp.concatenate(part, axis=0) for part in rows]


def scatter_tiles(terms, base_ref, accs, some, arrived=None):
    tiles = NB // MX
    for k in some:
        if arrived is not None:
            arrived(k)
        lanes = slice(k * MX, (k + 1) * MX)
        base = base_ref[:, lanes]
        left = make_left(terms(lanes), bin_steps(base))
        for n in range(tiles):
            extra = n == tiles - 1 and tiles % 2
            m = k % 2 if extra else n % 2
            acc = accs[n + m if extra else n]
            pltpu.matmul_push_rhs(onehot(base, n * MX), int(n >= 2), m, transpose=True)
            pltpu.matmul_acc_lhs(acc, left[0], load_staged_rhs=int(n >= 2))
            pltpu.matmul_acc_lhs(acc, left[1])


def scatter_pop(accs, sums):
    tiles = NB // MX
    for n in range(tiles):
        value = pltpu.matmul_pop(accs[n])
        if n == tiles - 1 and tiles % 2:
            value = value + pltpu.matmul_pop(accs[n + 1])
        for j in range(MX // LANE):
            at = (n * MX // LANE + j) * LEFT
            sums[at : at + LEFT, :] = value[:, j * LANE : (j + 1) * LANE]


def add_corners(sums, acc):
    pieces = []
    for bc in range(4):
        tiles = []
        for j in range(JB):
            base = j * LEFT + bc
            column = [sums[pl.ds(base + 4 * c, 8, stride=12), :] for c in range(3)]
            tiles.append(jnp.concatenate(column + [sums[pl.ds(base + 96, 8, stride=4), :]], axis=0))
        pieces.append(jnp.concatenate(tiles, axis=1))
    near = [pieces[2 * b] + pltpu.roll(pieces[2 * b + 1], 1, 1) for b in range(2)]
    total = near[0] + pltpu.roll(near[1], SZ, 1)
    total = jnp.concatenate([total, jnp.zeros((ROWS, LW - NB), jnp.float32)], axis=1)
    acc[...] = pltpu.roll(total, OFF, 1)


def damage_terms(part, weight):
    def terms(lanes):
        share = part[0:1, lanes] * weight[:, lanes]
        return [share, share * part[23:24, lanes], share * part[24:25, lanes]]
    return terms


def velocity_terms(part, weight, slope):
    def terms(lanes):
        mass = part[0:1, lanes]
        scale = -time_step * part[1:2, lanes]
        out = []
        for i in range(3):
            term = (mass * part[2 + i : 3 + i, lanes]) * weight[:, lanes]
            for j in range(3):
                row = 14 + 3 * i + j
                term = term + (scale * part[row : row + 1, lanes]) * slope[8 * j : 8 * j + 8, lanes]
            out.append(term)
        return out
    return terms


def send_spots(kind):
    if kind:
        return ((H - 1) * SZ, (H - 1 + CY) * SZ), (H - 1, H - 1 + CZ)
    return ((H - 1) * SZ, CY * SZ), (H - 1, CZ)


def land_spots(kind):
    if kind:
        return ((H - 1) * SZ, (H - 1 + CY) * SZ), (H - 1, H - 1 + CZ)
    return (0, (SY - KEEP) * SZ), (0, SZ - KEEP)


def pack_y(kind, acc, ysend):
    for d, lane0 in enumerate(send_spots(kind)[0]):
        ysend[d] = take(acc[...], lane0, WIDE[kind] * SZ)


def pack_z(kind, acc, zsend, esend):
    wide = WIDE[kind]
    y_at, z_at = send_spots(kind)
    z, _ = lane_z(8)
    for d, z0 in enumerate(z_at):
        out = jnp.zeros((8, LW), jnp.float32)
        for s in range(4):
            value = spin(acc[8 * s : 8 * s + 8, :], s * wide - z0)
            out = jnp.where((z >= s * wide) & (z < (s + 1) * wide), value, out)
        if kind:
            zsend[d] = sum(spin(take(out, (H - 1 + q * FY) * SZ, FY * SZ), 4 * wide * q) for q in range(FOLDS))
        else:
            zsend[d] = out[:, ZA:ZB]
        for e, lane0 in enumerate(y_at):
            esend[2 * e + d] = take(out, lane0, wide * SZ)


def land_y(kind, acc, yrecv, has):
    for d, lane0 in enumerate(land_spots(kind)[0]):
        put_add(acc, lane0, WIDE[kind] * SZ, only(has(2 * d - 1, 0), yrecv[d]))


def land_z(kind, acc, zrecv, erecv, zin, has):
    wide = WIDE[kind]
    y_at, z_at = land_spots(kind)
    z, _ = lane_z(8)
    for d, z0 in enumerate(z_at):
        if kind:
            zin[...] = jnp.zeros((8, LW), jnp.float32)
            folded = only(has(0, 2 * d - 1), zrecv[d])
            short, lane = z[:, :ZF], iota((8, ZF), 1)
            for q in range(FOLDS):
                z1 = 4 * wide * q
                mine = (short >= z1) & (short < z1 + 4 * wide) & (lane < FY * SZ)
                put_add(zin, (H - 1 + q * FY) * SZ, FY * SZ, spin(jnp.where(mine, folded, 0.0), -z1))
        else:
            zin[:, :ZA] = jnp.zeros((8, ZA), jnp.float32)
            zin[:, ZB:] = jnp.zeros((8, LW - ZB), jnp.float32)
            zin[:, ZA:ZB] = only(has(0, 2 * d - 1), zrecv[d])
        for e, lane0 in enumerate(y_at):
            put_add(zin, lane0, wide * SZ, only(has(2 * e - 1, 2 * d - 1), erecv[2 * e + d]))
        whole = zin[...]
        for s in range(4):
            value = jnp.where((z >= s * wide) & (z < (s + 1) * wide), whole, 0.0)
            acc[8 * s : 8 * s + 8, :] += spin(value, z0 - s * wide)


def tail_rows(last, c):
    row = iota(last.shape, 0)
    first = spin0(last, -c)
    second = spin0(last, -c - 2)
    return jnp.where(row == 0, first, jnp.where(row == 1, second, 0.0))


def spin0(value, shift):
    shift = shift % value.shape[0]
    return pltpu.roll(value, shift, 0) if shift else value


def pack_edge(acc, edge):
    row = iota((8, LW), 0)
    out = jnp.zeros((8, LW), jnp.float32)
    for c in range(3):
        value = acc[8 * c : 8 * c + 8, :]
        out = jnp.where(row == c, spin0(value, c), jnp.where(row == 3 + c, spin0(value, 2 + c), out))
    edge[...] = out


def build_full(acc, low, high, has_low, has_high):
    row = iota((8, LW), 0)
    own_last, low_last = acc[24:32, :], low[24:32, :]
    out = []
    for c in range(3):
        at = slice(8 * c, 8 * c + 8)
        first = only(has_low, jnp.where(row >= 4, low[at, :], 0.0))
        middle = acc[at, :] + only(has_low, tail_rows(low_last, c))
        last = tail_rows(own_last, c) + only(has_high, jnp.where(row < 6, high[at, :], 0.0))
        out.append(jnp.concatenate([first, middle, last], axis=0))
    return out


def relax_start(place, nodes, full):
    ix, iy, iz = place
    z, y = lane_z(1)
    gz = z - H + (iz * CZ).astype(jnp.float32)
    gy = y - H + (iy * CY).astype(jnp.float32)
    flat_in = (gz >= 0) & (gz < nodes[2]) & (gy >= 0) & (gy < nodes[1]) & (y < SY)
    row = lax.broadcasted_iota(jnp.int32, (RD, 1), 0)
    gx = row - 4 - H + ix * CX
    row_in = (gx >= 0) & (gx < nodes[0]) & (row >= 4) & (row < 4 + SX)
    inside = row_in.astype(jnp.float32) * flat_in.astype(jnp.float32)
    mass = jnp.maximum(full[0], mass_floor)
    factor = inside / mass
    damage = full[1] * factor
    drive = full[2] * factor
    keep = (1.0 - relax_rate * (6.0 * length_sq + 1.0)) * inside - (2.0 * relax_rate) * drive
    push = (2.0 * relax_rate) * drive
    spread = (relax_rate * length_sq) * inside
    return factor, damage, keep, push, spread


def relax_all(coefficients, line):
    _, damage, keep, push, spread = coefficients
    tiles = LW // LANE
    line[0:8, :] = jnp.zeros((8, LANE), jnp.float32)
    line[8 + tiles * RD :, :] = jnp.zeros((8, LANE), jnp.float32)
    for _ in range(SUBSTEPS):
        for j in range(tiles):
            line[8 + j * RD : 8 + (j + 1) * RD, :] = damage[:, j * LANE : (j + 1) * LANE]
        pair = damage + pltpu.roll(damage, SZ + 1, 1)
        along = jnp.concatenate(
            [line[pl.ds(7 + j * RD, RD), :] + line[pl.ds(9 + j * RD, RD), :] for j in range(tiles)], axis=1)
        ring = along + pltpu.roll(pair, LW - SZ, 1) + pltpu.roll(pair, LW - 1, 1)
        damage = spread * ring + keep * damage + push
    for j in range(tiles):
        line[8 + j * RD : 8 + (j + 1) * RD, :] = damage[:, j * LANE : (j + 1) * LANE]
    return damage


def show_damage(line, damage_out):
    own = jnp.concatenate([line[pl.ds(8 + j * RD + 4 + H, CX), :] for j in range(LW // LANE)], axis=1)
    for y in range(CY):
        damage_out[:, y, :] = pltpu.roll(own, LW - (H + y) * SZ - H, 1)[:, :CZ]


def velocity_field(factor, acc, low, high, has_low, has_high, field):
    row = iota((8, LW), 0)
    low_last = only(has_low, low[...])
    last = acc[24:32, :] + only(has_high, high[...])
    velocity = [(acc[8 * c : 8 * c + 8, :] + tail_rows(low_last, c)) * factor[8:16] for c in range(3)]
    spread = lambda r: jnp.broadcast_to(factor[r : r + 1], row.shape)
    last = last * jnp.where(row < 3, spread(16), jnp.where(row < 6, spread(17), 0.0))
    whole = pltpu.roll(jnp.concatenate(velocity + [last], axis=0), LW - OFF, 1)[:, :NB]
    turned = [whole, pltpu.roll(whole, NB - 1, 1)]
    for bc in range(4):
        moved = turned[bc & 1]
        if bc >> 1:
            moved = pltpu.roll(moved, NB - SZ, 1)
        for j in range(JB):
            at, lanes = j * LEFT + bc, slice(j * LANE, (j + 1) * LANE)
            for c in range(3):
                field[pl.ds(at + 4 * c, 8, stride=12), :] = moved[8 * c : 8 * c + 8, lanes]
            field[pl.ds(at + 96, 8, stride=4), :] = moved[24:32, lanes]


def damage_field(damage, field):
    whole = pltpu.roll(damage[8:24], LW - OFF, 1)[:, :NB]
    turned = [whole, pltpu.roll(whole, NB - 1, 1)]
    for bc in range(4):
        moved = turned[bc & 1]
        if bc >> 1:
            moved = pltpu.roll(moved, NB - SZ, 1)
        for j in range(JB):
            for part in range(2):
                field[pl.ds(j * FD + 32 * part + bc, 8, stride=4), :] = (
                    moved[8 * part : 8 * part + 8, j * LANE : (j + 1) * LANE])


def near_nodes(half, rows, base_ref, field, got_ref):
    depth = NB // MX
    tiles = TAIL // MX

    def multiply(*accs):
        for k in range(depth):
            high, low = split(jnp.concatenate(
                [field[j * rows : (j + 1) * rows, :] for j in range(k * MX // LANE, (k + 1) * MX // LANE)], axis=1))
            for n in range(tiles):
                at = half * TAIL + n * MX
                pltpu.matmul_push_rhs(onehot(base_ref[:, at : at + MX], k * MX), n // 2 % 2, n % 2)
                pltpu.matmul_acc_lhs(accs[n], high, load_staged_rhs=n // 2 % 2)
                pltpu.matmul_acc_lhs(accs[n], low)
        for n in range(tiles):
            value = pltpu.matmul_pop(accs[n])
            for j in range(MX // LANE):
                for r in range(0, rows, 8):
                    got_ref[pl.ds(r * MOST + n * MX // LANE + j, 8, stride=MOST), :] = (
                        value[r : r + 8, j * LANE : (j + 1) * LANE])

    pl.run_scoped(multiply, *[pltpu.ACC(n % 2)((rows, MX), jnp.float32) for n in range(tiles)])


def corners(half, got_ref, fields, bx_ref):
    bx = bx_ref[MOST * half : MOST * half + MOST, :]
    at = [bx == x for x in range(CX + 1)]
    out = [[None] * 8 for _ in range(fields)]
    for f in range(fields):
        for bc in range(4):
            near = [jnp.zeros((MOST, LANE), jnp.float32)] * 2
            for x in range(EX):
                r = 4 * (fields * x + f) + bc
                value = got_ref[r * MOST : (r + 1) * MOST, :]
                if x < EX - 1:
                    near[0] = jnp.where(at[x], value, near[0])
                if x > 0:
                    near[1] = jnp.where(at[x - 1], value, near[1])
            out[f][bc], out[f][4 + bc] = near
    return out


def total(values):
    while len(values) > 1:
        values = [a + b for a, b in zip(values[::2], values[1::2])]
    return values[0]


def move(corner, w, g, p):
    moved = [total([w(k) * corner[i][k] for k in range(8)]) for i in range(3)]
    velgrad = [[total([corner[i][k] * g(j, k) for k in range(8)]) for j in range(3)] for i in range(3)]
    deform = [[p(5 + 3 * i + j) for j in range(3)] for i in range(3)]
    stretch = [[(1.0 if i == j else 0.0) + time_step * velgrad[i][j] for j in range(3)] for i in range(3)]
    mapped = [
        stretch[i][0] * deform[0][j] + stretch[i][1] * deform[1][j] + stretch[i][2] * deform[2][j]
        for i in range(3) for j in range(3)
    ]
    return moved + mapped


def damage_of(corner, w, p):
    return [jnp.maximum(p(23), total([w(k) * corner[0][k] for k in range(8)]))]


def finish(late, early):
    moved, m, damaged = late[:3], late[3:12], late[12]
    mapped = [m[0:3], m[3:6], m[6:9]]
    jacobian = (
        mapped[0][0] * (mapped[1][1] * mapped[2][2] - mapped[1][2] * mapped[2][1])
        - mapped[0][1] * (mapped[1][0] * mapped[2][2] - mapped[1][2] * mapped[2][0])
        + mapped[0][2] * (mapped[1][0] * mapped[2][1] - mapped[1][1] * mapped[2][0])
    )
    left = {}
    for i in range(3):
        for j in range(i, 3):
            left[i, j] = mapped[i][0] * mapped[j][0] + mapped[i][1] * mapped[j][1] + mapped[i][2] * mapped[j][2]
            left[j, i] = left[i, j]
    degrade = (1.0 - damaged) ** 2
    swell = bulk_coef * (jacobian - 1.0)
    stress = []
    for i in range(3):
        for j in range(3):
            term = shear_mod * (left[i, j] - (1.0 if i == j else 0.0))
            if i == j:
                term = term + swell
            stress.append(degrade * term)
    energy = 0.5 * shear_mod * (left[0, 0] + left[1, 1] + left[2, 2] - 3.0) + 0.5 * bulk_coef * (jacobian - 1.0) ** 2
    history = jnp.maximum(early[2], energy)
    position = [early[3 + i] + time_step * moved[i] for i in range(3)]
    return early[:2] + moved + m + stress + [damaged, history] + position


def step_kernel(sizes, *refs):
    slots = up_to(NB // MX, 2)
    kinds = [pltpu.ACC(n % 2)((LEFT, MX), jnp.float32) for _ in range(2) for n in range(slots)]
    pl.run_scoped(lambda *accs: step_body(accs, sizes, *refs), *kinds)


def step_body(
    accs, sizes, part_in, base_in, weight_in, slope_in, counts, ext, prior_out, damage_out,
    part, base_ref, weight, slope, load_sem, out, sums, acc_d, acc_v, zin, line, field_v, field_d, got_v, got_d, turned, bx_ref,
    ysend_d, yrecv_d, zsend_d, zrecv_d, esend_d, erecv_d, ysend_v, yrecv_v, zsend_v, zrecv_v, esend_v, erecv_v,
    xrecv_d, xrecv_v, edge_v, early_send, early_recv, late_send, late_recv, send_sem, recv_sem,
):
    names = ("gx", "gy", "gz")
    count = part.shape[1]
    chunk = count // CHUNKS
    loads = []
    for c in range(CHUNKS):
        lanes = pl.ds(c * chunk, chunk)
        loads.append([
            pltpu.make_async_copy(src.at[:, lanes], dst.at[:, lanes], load_sem.at[4 * c + i])
            for i, (src, dst) in enumerate(
                ((base_in, base_ref), (part_in, part), (weight_in, weight), (slope_in, slope)))
        ])
    for load in loads[0]:
        load.start()
    place = [lax.axis_index(a) for a in names]
    has_low = [i > 0 for i in place]
    has_high = [i < n - 1 for i, n in zip(place, sizes)]
    last = sizes[2]
    following, previous = lax.rem(place[2] + 1, last), lax.rem(place[2] + last - 1, last)
    bins = count // BIN

    def has(dy, dz):
        found = None
        for k, d in ((1, dy), (2, dz)):
            if d:
                one = has_high[k] if d > 0 else has_low[k]
                found = one if found is None else found & one
        return found

    def device(dy, dz):
        return {names[k]: place[k] + d for k, d in ((1, dy), (2, dz)) if d}

    barrier = pltpu.get_barrier_semaphore()
    waits = 2
    ahead = [(has_low[0], {"gx": place[0] - 1}), (has_high[0], {"gx": place[0] + 1})]
    for exists, other in ahead + [(has(*d), device(*d)) for d in DIRS]:
        @pl.when(exists)
        def _(other=other):
            pl.semaphore_signal(barrier, inc=1, device_id=other, device_id_type=MESH)
        waits = waits + exists.astype(jnp.int32)
    for other in (following, previous):
        pl.semaphore_signal(barrier, inc=1, device_id={"gz": other}, device_id_type=MESH)

    pending = []

    def copy_to(slot, back, src, dst, other):
        return pltpu.make_async_remote_copy(
            src_ref=src, dst_ref=dst, send_sem=send_sem.at[slot], recv_sem=recv_sem.at[back],
            device_id=other, device_id_type=MESH)

    def bufs(kind):
        if kind:
            return (ysend_v, yrecv_v), (zsend_v, zrecv_v), (esend_v, erecv_v)
        return (ysend_d, yrecv_d), (zsend_d, zrecv_d), (esend_d, erecv_d)

    def message(kind, dy, dz):
        y, z = (dy + 1) // 2, (dz + 1) // 2
        if dz == 0:
            (src, dst), at, back = bufs(kind)[0], y, 1 - y
            base = 0
        elif dy == 0:
            (src, dst), at, back = bufs(kind)[1], z, 1 - z
            base = 2
        else:
            (src, dst), at, back = bufs(kind)[2], 2 * y + z, 2 * (1 - y) + 1 - z
            base = 4
        base += 8 * kind
        return copy_to(base + at, base + back, src.at[at], dst.at[back], device(dy, dz))

    def start(kind, chosen):
        for d in chosen:
            copy = message(kind, *d)
            pending.append((has(*d), copy))
            @pl.when(has(*d))
            def _(copy=copy):
                copy.start()

    def arrive(kind, chosen):
        for dy, dz in chosen:
            copy = message(kind, -dy, -dz)
            @pl.when(has(dy, dz))
            def _(copy=copy):
                copy.wait_recv()

    faces_y = [(-1, 0), (1, 0)]
    others = [d for d in DIRS if d[1] != 0]

    def x_messages(kind):
        src = (edge_v, acc_v.at[24:32]) if kind else (acc_d, acc_d)
        recv = xrecv_v if kind else xrecv_d
        base = 16 + 2 * kind
        return [
            copy_to(base + d, base + 1 - d, src[d], recv.at[1 - d], {"gx": place[0] + 2 * d - 1}) for d in range(2)]

    def x_start(kind):
        for (exists, _), copy in zip(ahead, x_messages(kind)):
            pending.append((exists, copy))
            @pl.when(exists)
            def _(copy=copy):
                copy.start()

    def x_arrive(kind):
        made = x_messages(kind)
        for exists, copy in ((has_low[0], made[1]), (has_high[0], made[0])):
            @pl.when(exists)
            def _(copy=copy):
                copy.wait_recv()

    def ring(slot, src, dst):
        copy = copy_to(slot, slot, src, dst, {"gz": following})
        copy.start()
        return copy

    for group in loads[1:]:
        for load in group:
            load.start()

    def arrived(k):
        if k * MX % chunk == 0:
            for load in loads[k * MX // chunk]:
                load.wait()

    slots = up_to(NB // MX, 2)
    spans = count // MX
    early_spans = spans * EARLY_PART // 8

    scatter_tiles(damage_terms(part, weight), base_ref, accs[:slots], range(spans), arrived)
    scatter_pop(accs[:slots], sums.at[0])
    terms = velocity_terms(part, weight, slope)
    scatter_tiles(terms, base_ref, accs[slots:], range(early_spans))
    add_corners(sums.at[0], acc_d)
    pack_z(0, acc_d, zsend_d, esend_d)
    pack_y(0, acc_d, ysend_d)
    pl.semaphore_wait(barrier, waits)
    start(0, others)
    start(0, faces_y)
    scatter_tiles(terms, base_ref, accs[slots:], range(early_spans, spans))
    scatter_pop(accs[slots:], sums.at[1])
    add_corners(sums.at[1], acc_v)
    pack_z(1, acc_v, zsend_v, esend_v)
    start(1, others)
    pack_y(1, acc_v, ysend_v)
    start(1, faces_y)

    lanes = lambda j: slice(j * LANE, (j + 1) * LANE)
    for j in range(bins):
        for group in range(3):
            turned[(group * bins + j) * 8 : (group * bins + j + 1) * 8, :] = part[8 * group : 8 * group + 8, lanes(j)]
        turned[(3 * bins + j) * 8 : (3 * bins + j) * 8 + 4, :] = part[24:28, lanes(j)]
        turned[(4 * bins + j) * 8 : (4 * bins + j + 1) * 8, :] = weight[:, lanes(j)]
        for group in range(3):
            at = ((5 + group) * bins + j) * 8
            turned[at : at + 8, :] = slope[8 * group : 8 * group + 8, lanes(j)]
        bx_ref[j : j + 1, :] = base_ref[0:1, lanes(j)]

    def dense(half):
        def read(group, s):
            return turned[pl.ds((group * bins + half * MOST) * 8 + s, MOST, stride=8), :]
        return (
            lambda k: read(4, k), lambda j, k: read(5 + j, k), lambda r: read(r // 8, r % 8)
        )

    halves = bins // MOST
    flying = []
    _, _, p = dense(halves - 1)
    early = [p(0), p(1), p(24), p(25), p(26), p(27)]
    early.append(jnp.broadcast_to(counts[0], (8, LANE)).astype(jnp.float32))
    for q, value in enumerate(early):
        early_send[8 * q : 8 * q + 8, :] = value
    ext[:, (MOST + bins) * LANE :] = jnp.zeros((PARTS, TAIL), jnp.float32)

    arrive(0, faces_y)
    land_y(0, acc_d, yrecv_d, has)
    arrive(0, others)
    land_z(0, acc_d, zrecv_d, erecv_d, zin, has)
    x_start(0)
    flying.append(ring(20, early_send, early_recv))
    arrive(1, faces_y)
    land_y(1, acc_v, yrecv_v, has)
    arrive(1, others)
    land_z(1, acc_v, zrecv_v, erecv_v, zin, has)
    pack_edge(acc_v, edge_v)
    x_start(1)
    x_arrive(0)
    x_arrive(1)
    full = build_full(acc_d, xrecv_d.at[0], xrecv_d.at[1], has_low[0], has_high[0])
    nodes = [n * c for n, c in zip(sizes, (CX, CY, CZ))]
    coefficients = relax_start(place, nodes, full)
    tail_half = bins // MOST - 1
    velocity_field(
        coefficients[0], acc_v, xrecv_v.at[0], xrecv_v.at[1], has_low[0], has_high[0], field_v)
    near_nodes(tail_half, LEFT, base_ref, field_v, got_v)
    w, g, p = dense(tail_half)
    tail_late = move(corners(tail_half, got_v, 3, bx_ref), w, g, p)
    damage = relax_all(coefficients, line)
    for q, value in enumerate(tail_late):
        late_send[8 * q : 8 * q + 8, :] = value
    flying.append(ring(21, late_send.at[: 8 * LATE - 8], late_recv.at[: 8 * LATE - 8]))
    damage_field(damage, field_d)

    def store(first, values, gone=None):

        for r, value in enumerate(values):
            if gone is not None:
                value = jnp.where(gone, 0.0, value)
            out[pl.ds(first * SLOT + r, MOST, stride=SLOT), :] = value
        for j in range(first, first + MOST):
            for group in range(up_to(PARTS, 8) // 8):
                rows = min(8, PARTS - 8 * group)
                at = j * SLOT + 8 * group
                ext[8 * group : 8 * group + rows, lanes(j)] = out[at : at + rows, :]

    for half in reversed(range(halves)):
        w, g, p = dense(half)
        if half != tail_half:
            near_nodes(half, LEFT, base_ref, field_v, got_v)
            late = move(corners(half, got_v, 3, bx_ref), w, g, p)
        else:
            late = tail_late
        near_nodes(half, FD, base_ref, field_d, got_d)
        late = late + damage_of(corners(half, got_d, 1, bx_ref), w, p)
        gone = None
        if half == halves - 1:
            late_send[8 * LATE - 8 :, :] = late[-1]
            flying.append(ring(22, late_send.at[8 * LATE - 8 :], late_recv.at[8 * LATE - 8 :]))
            show_damage(line, damage_out)
            gone = iota((MOST, LANE), 0) + jnp.broadcast_to(counts[0], (MOST, LANE)) >= MOST
        store((half + 1) * MOST, finish(late, [p(0), p(1), p(24), p(25), p(26), p(27)]), gone)

    for copy in flying:
        copy.wait_recv()
    rows = lambda ref, q: ref[8 * q : 8 * q + 8, :]
    store(0, finish([rows(late_recv, q) for q in range(LATE)], [rows(early_recv, q) for q in range(6)]))
    prior_out[...] = rows(early_recv, 6).astype(jnp.int32)
    for copy in flying:
        copy.wait_send()
    for exists, copy in pending:
        @pl.when(exists)
        def _(copy=copy):
            copy.wait_send()


def place_kernel(ext, prior_ref, damage_in, migrated, damage_out, sem):
    width = migrated.shape[1]
    start = pl.multiple_of((MOST - prior_ref[0, 0]) * BIN, BIN)
    copies = [
        pltpu.make_async_copy(damage_in, damage_out, sem.at[0]),
        pltpu.make_async_copy(ext.at[:, pl.ds(start, width)], migrated, sem.at[1]),
    ]
    for copy in copies:
        copy.start()
    for copy in copies:
        copy.wait()


def per_device(particles, stencil_base, weights, gradients, counts):
    count = particles.shape[1]
    bins = count // BIN
    sizes = tuple(lax.axis_size(a) for a in ("gx", "gy", "gz"))
    vmem = pl.BlockSpec(memory_space=pltpu.VMEM)
    anywhere = pl.BlockSpec(memory_space=pl.ANY)
    f32 = jnp.float32
    two = lambda *shape: [pltpu.VMEM(shape, f32)] * 2
    ext, prior, near_damage = pl.pallas_call(
        functools.partial(step_kernel, sizes),
        name="step",
        out_shape=(
            pltpu.VMEM((PARTS, count + 2 * TAIL), f32),
            pltpu.VMEM((8, LANE), jnp.int32),
            pltpu.VMEM((CX, CY, CZ), f32),
        ),
        in_specs=[anywhere] * 4 + [pl.BlockSpec(memory_space=pltpu.SMEM)],
        out_specs=(vmem,) * 3,
        scratch_shapes=[
            pltpu.VMEM((PARTS, count), f32),
            pltpu.VMEM((3, count), jnp.int32),
            pltpu.VMEM((8, count), f32),
            pltpu.VMEM((24, count), f32),
            pltpu.SemaphoreType.DMA((4 * CHUNKS,)),
            pltpu.VMEM(((bins + MOST) * SLOT, LANE), f32),
            pltpu.VMEM((2, JB * LEFT, LANE), f32),
            pltpu.VMEM((ROWS, LW), f32),
            pltpu.VMEM((ROWS, LW), f32),
            pltpu.VMEM((8, LW), f32),
            pltpu.VMEM((16 + LW // LANE * RD, LANE), f32),
            pltpu.VMEM((JB * LEFT, LANE), f32),
            pltpu.VMEM((JB * FD, LANE), f32),
            pltpu.VMEM((MOST * LEFT, LANE), f32),
            pltpu.VMEM((MOST * FD, LANE), f32),
            pltpu.VMEM((GROUPS * bins * 8, LANE), f32),
            pltpu.VMEM((bins, LANE), jnp.int32),
            *two(2, ROWS, FACE[0]),
            *two(2, 8, ZB - ZA),
            *two(4, 8, FACE[0]),
            *two(2, ROWS, FACE[1]),
            *two(2, 8, ZF),
            *two(4, 8, FACE[1]),
            pltpu.VMEM((2, ROWS, LW), f32),
            pltpu.VMEM((2, 8, LW), f32),
            pltpu.VMEM((8, LW), f32),
            *two(EARLY * 8, LANE),
            *two(LATE * 8, LANE),
            pltpu.SemaphoreType.DMA((23,)),
            pltpu.SemaphoreType.DMA((23,)),
        ],
        compiler_params=pltpu.CompilerParams(
            collective_id=0, has_side_effects=True, vmem_limit_bytes=60 * 1024 * 1024
        ),
    )(particles, stencil_base, weights, gradients.reshape(24, count), counts)
    return pl.pallas_call(
        place_kernel,
        name="place",
        out_shape=(
            jax.ShapeDtypeStruct((PARTS, count + TAIL), f32),
            jax.ShapeDtypeStruct((CX, CY, CZ), f32),
        ),
        in_specs=[anywhere, vmem, anywhere],
        out_specs=(anywhere,) * 2,
        scratch_shapes=[pltpu.SemaphoreType.DMA((2,))],
        compiler_params=pltpu.CompilerParams(vmem_limit_bytes=4 * 1024 * 1024),
    )(ext, prior, near_damage)


def solution(mesh):
    return jax.shard_map(
        per_device,
        mesh=mesh,
        in_specs=(
            P(None, ("gx", "gy", "gz")),
            P(None, ("gx", "gy", "gz")),
            P(None, ("gx", "gy", "gz")),
            P(None, None, ("gx", "gy", "gz")),
            P(("gx", "gy", "gz")),
        ),
        out_specs=(P(None, ("gx", "gy", "gz")), P("gx", "gy", "gz")),
        check_vma=False,
    )
```
